256 devices in a mesh: pipe: 8 (over z_lo, y), dp: 32 (over x, z_hi, core).
Axes of the slice: x: 4, y: 4, z: 8 (z_hi: 4, z_lo: 2; z = z_hi * 2 + z_lo), core: 2. Of those that a mesh axis runs over, the one named last changes fastest.
Arguments:
- inputs: bfloat16 [2, 4096, 2048], P(None, 'dp'), may hold values from -6 to 6
- cotangent: bfloat16 [2, 4096, 2048], P(None, 'dp'), may hold values from -0.125 to 0.125
- joined: int32 [2, 16], replicated, may hold values 0 or 1
- w_qkv: bfloat16 [8, 2048, 1536], P('pipe', 'dp'), may hold values from -0.125 to 0.125
- w_out: bfloat16 [8, 1024, 2048], P('pipe', 'dp'), may hold values from -0.1875 to 0.1875
Outputs:
- grad_qkv: float32 [8, 2048, 1536], P('pipe', 'dp')
- grad_out: float32 [8, 1024, 2048], P('pipe', 'dp')
The draws below stay inside these ranges and needn't reach their ends.
Inputs may be any that keep to these rules, and one draw needn't show every extreme that they name: joined[m, j] is 1 where bin j of micro-batch m holds one molecule covering both of its blocks, 0 where each block holds its own molecule.
All inputs are finite; a program needn't handle non-finite values.
Results may differ from the reference program's by a relative error of at most 0.028.
Values may be sent and summed in bfloat16 or wider, within the bound.
No kernel may reach another device: no remote copies, remote signals or barrier semaphores. Data moves between devices by JAX's collectives and lax.ppermute only.
A program may use at most 192 MiB of HBM per device.

```python
import math
import jax
import jax.numpy as jnp
from jax import lax

D = 2048
HEADS = 16
HEAD = 64
KVH = 4
BLOCK = 128
MICRO = 2
LAYERS = 8
SEQ = 4096
BINS = 16
HQ = 1024
WCOLS = 1536


def with_ends(values, stream_key, smallest, top_value):
    longest = values.shape.index(max(values.shape))
    spots = []
    for shift in (0, 1):
        where = [jax.random.randint(jax.random.fold_in(stream_key, axis), (), 0, length) for axis, length in enumerate(values.shape)]
        where[longest] = (where[longest] + shift) % values.shape[longest]
        spots.append(tuple(where))
    return values.at[spots[0]].set(smallest).at[spots[1]].set(top_value)


def block_levels(key, shape, shards, low, largest):
    factor_of, own = 1.0, jax.random.fold_in(key, 6)
    for dim, parts in shards:
        steps = jnp.exp(jax.random.uniform(jax.random.fold_in(own, dim), (parts,), jnp.float32, low / len(shards), largest / len(shards)))
        factor_of = factor_of * jnp.repeat(steps, shape[dim] // parts).reshape([-1 if axis == dim else 1 for axis in range(len(shape))])
    return factor_of


def bell_draw(own_key, shape, width, bound, split=(), kind=jnp.bfloat16):
    drawn = width * jax.random.normal(own_key, shape, jnp.float32)
    if split:
        drawn = drawn * block_levels(own_key, shape, split, -0.22, 0.18)
    return jnp.clip(drawn, -bound, bound).astype(kind)


def setup_inputs(seed: int = 0) -> dict:
    splits = jax.random.split(jax.random.key(seed), 6)
    inputs = bell_draw(splits[0], (MICRO, SEQ, D), 1.0, 6.0, ((1, 32),))
    cotangent = bell_draw(splits[1], (MICRO, SEQ, D), 0.02, 0.125, ((1, 32),))
    joined = with_ends((jax.random.randint(splits[2], (MICRO, BINS), 0, 2) < 1).astype(jnp.int32), jax.random.fold_in(splits[2], 1), 0, 1)
    w_qkv = bell_draw(splits[3], (LAYERS, D, WCOLS), D ** -0.5, 0.125, ((0, 8), (1, 32)))
    w_out = bell_draw(splits[4], (LAYERS, HQ, D), HQ ** -0.5, 0.1875, ((0, 8), (1, 32)))
    return dict(inputs=inputs, cotangent=cotangent, joined=joined, w_qkv=w_qkv, w_out=w_out)


norm_eps = 1e-05

def normalize(hidden):
    widened = hidden.astype(jnp.float32)
    inv_rms = lax.rsqrt(lax.optimization_barrier(jnp.mean(widened * widened, axis=-1, keepdims=True)) + norm_eps)
    return (widened * inv_rms).astype(jnp.bfloat16)

def project(hidden, w_qkv):
    normed = normalize(hidden)
    projected = jnp.dot(normed, w_qkv, preferred_element_type=jnp.float32)
    inner_width = HEADS * HEAD
    kv_width = KVH * HEAD
    queries = projected[:, :inner_width].astype(jnp.bfloat16)
    own_kv = jnp.stack([projected[:, inner_width:inner_width + kv_width], projected[:, inner_width + kv_width:]]).astype(jnp.bfloat16)
    return (normed, queries, own_kv)

def attend(queries, key_rows, value_rows, visible):
    row_count = queries.shape[0]
    key_count = key_rows.shape[0]
    grouped = queries.astype(jnp.float32).reshape(row_count, KVH, HEADS // KVH, HEAD)
    key_heads = key_rows.astype(jnp.float32).reshape(key_count, KVH, HEAD)
    value_heads = value_rows.astype(jnp.float32).reshape(key_count, KVH, HEAD)
    scores = jnp.einsum('tkgd,ukd->kgtu', grouped, key_heads) * (1.0 / math.sqrt(HEAD))
    raised = jnp.exp(scores) * visible
    prob_rows = (raised / lax.optimization_barrier(jnp.sum(raised, axis=-1, keepdims=True))).astype(jnp.bfloat16)
    prob_rows = lax.optimization_barrier(prob_rows)
    context = jnp.einsum('kgtu,ukd->tkgd', prob_rows.astype(jnp.float32), value_heads)
    return context.reshape(row_count, HEADS * HEAD).astype(jnp.bfloat16)

def attend_pair(queries, own_kv, pair_kv, joined_flag):
    row_count = own_kv.shape[1]
    pair_mask = jnp.where(joined_flag > 0, 1.0, 0.0).astype(jnp.float32) * jnp.ones((row_count,), jnp.float32)
    visible = jnp.concatenate([jnp.ones((row_count,), jnp.float32), pair_mask])
    key_rows = jnp.concatenate([own_kv[0], pair_kv[0]])
    value_rows = jnp.concatenate([own_kv[1], pair_kv[1]])
    return attend(queries, key_rows, value_rows, visible)

def finish(hidden, context, w_out):
    return (hidden.astype(jnp.float32) + jnp.dot(context, w_out, preferred_element_type=jnp.float32)).astype(jnp.bfloat16)

def attention_grads(upstream, queries, own_kv, pair_kv, joined_flag, w_out):
    d_context = jnp.dot(upstream, w_out.T, preferred_element_type=jnp.float32).astype(jnp.bfloat16)

    def forward_part(query_rows, own_rows, pair_rows):
        return attend_pair(query_rows, own_rows, pair_rows, joined_flag)
    unused, pull = jax.vjp(forward_part, queries, own_kv, pair_kv)
    return pull(d_context)

def input_grads(upstream, hidden, d_query, d_own, back_kv, w_qkv):
    combined = (d_own.astype(jnp.float32) + back_kv.astype(jnp.float32)).astype(jnp.bfloat16)
    d_proj = jnp.concatenate([d_query, combined[0], combined[1]], axis=-1)
    d_normed = jnp.dot(d_proj, w_qkv.T, preferred_element_type=jnp.float32)
    widened = hidden.astype(jnp.float32)
    inv_rms = lax.rsqrt(lax.optimization_barrier(jnp.mean(widened * widened, axis=-1, keepdims=True)) + norm_eps)
    cubed = inv_rms * inv_rms * inv_rms
    d_widened = inv_rms * d_normed - widened * cubed * lax.optimization_barrier(jnp.mean(d_normed * widened, axis=-1, keepdims=True))
    previous = (upstream.astype(jnp.float32) + d_widened).astype(jnp.bfloat16)
    return (d_proj, previous)

def swap_pairs(blocks):
    shape = blocks.shape
    paired = blocks.reshape((shape[0] // 2, 2) + shape[1:])
    return jnp.flip(paired, axis=1).reshape(shape)

def block_sum(left_rows, right_rows):

    def add_block(total, operands):
        term = jnp.dot(operands[0].T, operands[1], preferred_element_type=jnp.float32)
        rounded = lax.optimization_barrier(term.astype(jnp.bfloat16))
        return (total + rounded.astype(jnp.float32), None)
    start = jnp.zeros((left_rows.shape[2], right_rows.shape[2]), jnp.float32)
    total, unused = lax.scan(add_block, start, (left_rows, right_rows))
    return total

def reference(inputs, cotangent, joined, w_qkv, w_out):
    layer_count = w_qkv.shape[0]
    micro_count = inputs.shape[0]
    block_count = inputs.shape[1] // BLOCK
    model_width = inputs.shape[2]
    records = []
    for batch_index in range(micro_count):
        hidden = inputs[batch_index].reshape(block_count, BLOCK, model_width)
        bin_flags = jnp.repeat(joined[batch_index], 2)
        layer_records = []
        for layer_index in range(layer_count):
            normed, queries, own_kv = jax.vmap(project, (0, None))(hidden, w_qkv[layer_index])
            pair_kv = swap_pairs(own_kv)
            context = jax.vmap(attend_pair)(queries, own_kv, pair_kv, bin_flags)
            layer_records.append((hidden, normed, queries, own_kv, pair_kv, context))
            hidden = jax.vmap(finish, (0, 0, None))(hidden, context, w_out[layer_index])
        records.append(layer_records)
    normed_terms = [[] for layer_index in range(layer_count)]
    proj_terms = [[] for layer_index in range(layer_count)]
    context_terms = [[] for layer_index in range(layer_count)]
    upstream_terms = [[] for layer_index in range(layer_count)]
    for batch_index in range(micro_count):
        upstream = cotangent[batch_index].reshape(block_count, BLOCK, model_width)
        bin_flags = jnp.repeat(joined[batch_index], 2)
        for layer_index in reversed(range(layer_count)):
            hidden, normed, queries, own_kv, pair_kv, context = records[batch_index][layer_index]
            d_query, d_own, d_pair = jax.vmap(attention_grads, (0, 0, 0, 0, 0, None))(upstream, queries, own_kv, pair_kv, bin_flags, w_out[layer_index])
            back_kv = swap_pairs(d_pair)
            d_proj, previous = jax.vmap(input_grads, (0, 0, 0, 0, 0, None))(upstream, hidden, d_query, d_own, back_kv, w_qkv[layer_index])
            normed_terms[layer_index].append(normed)
            proj_terms[layer_index].append(d_proj)
            context_terms[layer_index].append(context)
            upstream_terms[layer_index].append(upstream)
            upstream = previous
    grads_qkv = []
    grads_out = []
    for layer_index in range(layer_count):
        normed_all = jnp.concatenate(normed_terms[layer_index], axis=1)
        proj_all = jnp.concatenate(proj_terms[layer_index], axis=1)
        context_all = jnp.concatenate(context_terms[layer_index], axis=1)
        upstream_all = jnp.concatenate(upstream_terms[layer_index], axis=1)
        grads_qkv.append(block_sum(normed_all, proj_all))
        grads_out.append(block_sum(context_all, upstream_all))
    return (jnp.stack(grads_qkv), jnp.stack(grads_out))
```

```python
import functools
import math

import jax
import jax.numpy as jnp
import numpy as np
from jax import lax
from jax.experimental import pallas as pl
from jax.experimental.pallas import tpu as pltpu
from jax.sharding import PartitionSpec as P

HEADS = 16
HEAD = 64
KVH = 4
GROUP = HEADS // KVH
ROWS = 256
HALF = 128
D = 2048
HQ = HEADS * HEAD
KV = KVH * HEAD
WCOLS = HQ + 2 * KV
CHUNK = 256
EPS = 1e-5
SCALE = 1.0 / math.sqrt(HEAD)
TO_EXP2 = SCALE * math.log2(math.e)
NT = (((1,), (1,)), ((), ()))
VMEM_LIMIT = 48 * 1024 * 1024
ANY = pl.BlockSpec(memory_space=pl.ANY)
SMEM = pl.BlockSpec(memory_space=pltpu.SMEM)


def dot_nt(left, right):
    return lax.dot_general(left, right, NT, preferred_element_type=jnp.float32)


def dot_nn(left, right):
    return jnp.dot(left, right, preferred_element_type=jnp.float32)


def cols(start, size):
    return pl.ds(pl.multiple_of(start, size), size)


def bias_matrix(joined):
    row = lax.broadcasted_iota(jnp.int32, (ROWS, ROWS), 0)
    col = lax.broadcasted_iota(jnp.int32, (ROWS, ROWS), 1)
    same = (row >= HALF) == (col >= HALF)
    return jnp.where(jnp.logical_or(same, joined > 0), 0.0, -1e30).astype(jnp.float32)


def probs_t(keys, query, bias):
    logits = dot_nt(keys, query) * TO_EXP2 + bias
    total = jnp.sum(jnp.exp2(logits), axis=0, keepdims=True)
    return jnp.exp2(logits - jnp.log2(total))


def forward_kernel(
    final, info, h_in, wq_in, wo_in, a0, a1, a2, a3,
    h_out, normed_out, proj_out, ctx_out, keep_out,
    h_v, normed_v, wq_v, wo_v, proj_v, ctx_v, out_v, bias_v, key_s, vt_s, in_sem, q_sem, o_sem, w_sem,
):
    del a0, a1, a2, a3

    @pl.when(info[0] == 1)
    def _():
        h_copy = pltpu.make_async_copy(h_in, h_v, in_sem)
        h_copy.start()

        def q_copy(i):
            c = cols(i * CHUNK, CHUNK)
            return pltpu.make_async_copy(wq_in.at[:, c], wq_v.at[:, c], q_sem.at[i])

        def o_copy(i):
            c = cols(i * CHUNK, CHUNK)
            return pltpu.make_async_copy(wo_in.at[:, c], wo_v.at[:, c], o_sem.at[i])

        for i in (4, 5, 0, 1, 2, 3):
            q_copy(i).start()
        if not final:
            for i in range(8):
                o_copy(i).start()
        bias_v[...] = bias_matrix(info[1])
        h_copy.wait()
        keep = pltpu.make_async_copy(h_v, keep_out, w_sem.at[0])
        keep.start()
        wide = h_v[...].astype(jnp.float32)
        scale = lax.rsqrt(jnp.mean(wide * wide, axis=-1, keepdims=True) + EPS)
        normed_v[...] = (wide * scale).astype(jnp.bfloat16)
        normed_copy = pltpu.make_async_copy(normed_v, normed_out, w_sem.at[1])
        normed_copy.start()
        q_copy(4).wait()
        q_copy(5).wait()
        keys = dot_nn(normed_v[...], wq_v[:, HQ : HQ + KV]).astype(jnp.bfloat16)
        proj_v[:, HQ : HQ + KV] = keys
        values = dot_nn(normed_v[...], wq_v[:, HQ + KV :])
        proj_v[:, HQ + KV :] = values.astype(jnp.bfloat16)
        values_t = values.T.astype(jnp.bfloat16)
        for g in range(KVH):
            key_s[g] = keys[:, g * HEAD : (g + 1) * HEAD]
            vt_s[g] = values_t[g * HEAD : (g + 1) * HEAD, :]

        def group(g, carry):
            c = cols(g * CHUNK, CHUNK)
            q_copy(g).wait()
            queries = dot_nn(normed_v[...], wq_v[:, c]).astype(jnp.bfloat16)
            proj_v[:, c] = queries
            pieces = []
            for i in range(GROUP):
                part = queries[:, i * HEAD : (i + 1) * HEAD]
                weights = probs_t(key_s[g], part, bias_v[...]).astype(jnp.bfloat16)
                pieces.append(dot_nn(vt_s[g], weights))
            ctx_v[:, c] = jnp.concatenate(pieces, axis=0).T.astype(jnp.bfloat16)
            return carry

        lax.fori_loop(0, KVH, group, 0)
        proj_copy = pltpu.make_async_copy(proj_v, proj_out, w_sem.at[2])
        proj_copy.start()
        ctx_copy = pltpu.make_async_copy(ctx_v, ctx_out, w_sem.at[3])
        ctx_copy.start()

        def finish(i, carry):
            c = cols(i * CHUNK, CHUNK)
            o_copy(i).wait()
            out = h_v[:, c].astype(jnp.float32) + dot_nn(ctx_v[...], wo_v[:, c])
            out_v[:, c] = out.astype(jnp.bfloat16)
            return carry

        if not final:
            lax.fori_loop(0, 8, finish, 0)
            out_copy = pltpu.make_async_copy(out_v, h_out, w_sem.at[4])
            out_copy.start()
            out_copy.wait()
        keep.wait()
        normed_copy.wait()
        proj_copy.wait()
        ctx_copy.wait()


def bf16(*shape):
    return jax.ShapeDtypeStruct(shape, jnp.bfloat16)


def v16(*shape):
    return pltpu.VMEM(shape, jnp.bfloat16)


def v32(*shape):
    return pltpu.VMEM(shape, jnp.float32)


def forward_layer(final, info, hidden, w_qkv, w_out, normed, proj, ctx, kept):
    return pl.pallas_call(
        functools.partial(forward_kernel, final),
        out_shape=(bf16(ROWS, D), bf16(ROWS, D), bf16(ROWS, WCOLS), bf16(ROWS, HQ), bf16(ROWS, D)),
        in_specs=[SMEM] + [ANY] * 7,
        out_specs=(ANY,) * 5,
        input_output_aliases={4: 1, 5: 2, 6: 3, 7: 4},
        scratch_shapes=[
            v16(ROWS, D), v16(ROWS, D), v16(D, WCOLS), v16(HQ, D), v16(ROWS, WCOLS), v16(ROWS, HQ), v16(ROWS, D),
            v32(ROWS, ROWS), v16(KVH, ROWS, HEAD), v16(KVH, HEAD, ROWS),
            pltpu.SemaphoreType.DMA, pltpu.SemaphoreType.DMA((6,)), pltpu.SemaphoreType.DMA((8,)),
            pltpu.SemaphoreType.DMA((5,)),
        ],
        compiler_params=pltpu.CompilerParams(vmem_limit_bytes=VMEM_LIMIT),
        cost_estimate=pl.CostEstimate(flops=3_000_000_000, bytes_accessed=14_000_000, transcendentals=2_000_000),
        name="forward_last" if final else "forward_layer",
    )(info, hidden, w_qkv, w_out, normed, proj, ctx, kept)


def backward_kernel(
    last, info, u_in, h_in, proj_in, wq_in, wo_in, a0, a1,
    up_out, dproj_out, keep_out,
    u_v, h_v, proj_v, wq_v, wo_v, dproj_v, dn_v, bias_v, key_s, kt_s, value_s, dk_s, dv_s,
    in_sem, q_sem, o_sem, w_sem,
):
    del a0, a1

    @pl.when(info[0] == 1)
    def _():
        u_copy = pltpu.make_async_copy(u_in, u_v, in_sem.at[0])
        u_copy.start()
        proj_copy = pltpu.make_async_copy(proj_in, proj_v, in_sem.at[1])
        h_copy = pltpu.make_async_copy(h_in, h_v, in_sem.at[2])

        def o_copy(i):
            r = cols(i * CHUNK, CHUNK)
            return pltpu.make_async_copy(wo_in.at[r, :], wo_v.at[r, :], o_sem.at[i])

        def q_copy(i):
            r = cols(i * CHUNK, CHUNK)
            return pltpu.make_async_copy(wq_in.at[r, :], wq_v.at[r, :], q_sem.at[i])

        o_copy(0).start()
        proj_copy.start()
        for i in range(1, 4):
            o_copy(i).start()
        if not last:
            h_copy.start()
            for i in range(8):
                q_copy(i).start()
        bias_v[...] = bias_matrix(info[1])
        proj_copy.wait()
        keys_t = proj_v[:, HQ : HQ + KV].astype(jnp.float32).T.astype(jnp.bfloat16)
        for g in range(KVH):
            key_s[g] = proj_v[:, HQ + g * HEAD : HQ + (g + 1) * HEAD]
            value_s[g] = proj_v[:, HQ + KV + g * HEAD : HQ + KV + (g + 1) * HEAD]
            kt_s[g] = keys_t[g * HEAD : (g + 1) * HEAD, :]
        u_copy.wait()
        keep = pltpu.make_async_copy(u_v, keep_out, w_sem.at[0])
        keep.start()

        def group(g, carry):
            c = cols(g * CHUNK, CHUNK)
            o_copy(g).wait()
            d_ctx = dot_nt(u_v[...], wo_v[c, :]).astype(jnp.bfloat16)
            queries = proj_v[:, c]
            pieces = []
            d_key = jnp.zeros((ROWS, HEAD), jnp.float32)
            d_value = jnp.zeros((ROWS, HEAD), jnp.float32)
            for i in range(GROUP):
                part = queries[:, i * HEAD : (i + 1) * HEAD]
                d_part = d_ctx[:, i * HEAD : (i + 1) * HEAD]
                weights = probs_t(key_s[g], part, bias_v[...])
                d_weights = dot_nt(value_s[g], d_part)
                inner = jnp.sum(d_weights * weights, axis=0, keepdims=True)
                d_scores = (weights * (d_weights - inner) * SCALE).astype(jnp.bfloat16)
                pieces.append(dot_nn(kt_s[g], d_scores))
                d_key += dot_nn(d_scores, part)
                d_value += dot_nn(weights.astype(jnp.bfloat16), d_part)
            dproj_v[:, c] = jnp.concatenate(pieces, axis=0).T.astype(jnp.bfloat16)
            dk_s[g] = d_key.astype(jnp.bfloat16)
            dv_s[g] = d_value.astype(jnp.bfloat16)
            return carry

        lax.fori_loop(0, KVH, group, 0)
        dproj_v[:, HQ : HQ + KV] = jnp.concatenate([dk_s[g] for g in range(KVH)], axis=1)
        dproj_v[:, HQ + KV :] = jnp.concatenate([dv_s[g] for g in range(KVH)], axis=1)
        dproj_copy = pltpu.make_async_copy(dproj_v, dproj_out, w_sem.at[1])
        dproj_copy.start()
        if not last:
            h_copy.wait()

            def widen(i, partial):
                c = cols(i * CHUNK, CHUNK)
                q_copy(i).wait()
                d_normed = dot_nt(dproj_v[...], wq_v[c, :])
                dn_v[:, c] = d_normed
                product = d_normed * h_v[:, c].astype(jnp.float32)
                return partial + product[:, :HALF] + product[:, HALF:]

            partial = lax.fori_loop(0, 8, widen, jnp.zeros((ROWS, HALF), jnp.float32))
            mean = jnp.sum(partial, axis=-1, keepdims=True) * (1.0 / D)
            wide = h_v[...].astype(jnp.float32)
            scale = lax.rsqrt(jnp.mean(wide * wide, axis=-1, keepdims=True) + EPS)
            pull = scale * scale * scale * mean

            def previous(i, carry):
                c = cols(i * CHUNK, CHUNK)
                out = u_v[:, c].astype(jnp.float32) + (scale * dn_v[:, c] - h_v[:, c].astype(jnp.float32) * pull)
                h_v[:, c] = out.astype(jnp.bfloat16)
                return carry

            lax.fori_loop(0, 8, previous, 0)
            up_copy = pltpu.make_async_copy(h_v, up_out, w_sem.at[2])
            up_copy.start()
            up_copy.wait()
        keep.wait()
        dproj_copy.wait()


def backward_layer(last, info, upstream, kept, proj, w_qkv, w_out, dproj, ups):
    return pl.pallas_call(
        functools.partial(backward_kernel, last),
        out_shape=(bf16(ROWS, D), bf16(ROWS, WCOLS), bf16(ROWS, D)),
        in_specs=[SMEM] + [ANY] * 7,
        out_specs=(ANY,) * 3,
        input_output_aliases={6: 1, 7: 2},
        scratch_shapes=[
            v16(ROWS, D), v16(ROWS, D), v16(ROWS, WCOLS), v16(D, WCOLS), v16(HQ, D), v16(ROWS, WCOLS), v32(ROWS, D),
            v32(ROWS, ROWS), v16(KVH, ROWS, HEAD), v16(KVH, HEAD, ROWS), v16(KVH, ROWS, HEAD),
            v16(KVH, ROWS, HEAD), v16(KVH, ROWS, HEAD),
            pltpu.SemaphoreType.DMA((3,)), pltpu.SemaphoreType.DMA((8,)), pltpu.SemaphoreType.DMA((4,)),
            pltpu.SemaphoreType.DMA((3,)),
        ],
        compiler_params=pltpu.CompilerParams(vmem_limit_bytes=VMEM_LIMIT),
        cost_estimate=pl.CostEstimate(flops=4_000_000_000, bytes_accessed=15_000_000, transcendentals=2_000_000),
        name="backward_last" if last else "backward_layer",
    )(info, upstream, kept, proj, w_qkv, w_out, dproj, ups)


LAYERS = 8
FINE = (("zlo", 2), ("y", 4), ("x", 4), ("zhi", 4), ("core", 2))
NAMES = tuple(name for name, size in FINE)
SIZES = tuple(size for name, size in FINE)
RING = ("x", "zhi", "zlo")
STAGE = ("y", "core")


def regroup(back):
    pairs = []
    for zlo, y, x, zhi, core in np.ndindex(*SIZES):
        source = np.ravel_multi_index((zlo, y, x, zhi, core), SIZES)
        target = np.ravel_multi_index((core, zlo * 2 + y // 2, x, zhi, y % 2), SIZES)
        pairs.append((int(target), int(source)) if back else (int(source), int(target)))
    return pairs


def on_device(inputs, cotangent, joined, w_qkv, w_out):
    micro = lax.axis_index("zlo")
    stage = 2 * lax.axis_index("y") + lax.axis_index("core")
    bin_index = 4 * lax.axis_index("x") + lax.axis_index("zhi")
    flag = joined[micro, bin_index]
    near, far = w_qkv[0], w_out[0]
    near = lax.ppermute(near, NAMES, regroup(False))
    far = lax.ppermute(far, NAMES, regroup(False))
    full_qkv = lax.all_gather(near, RING, axis=0, tiled=True)
    full_out = lax.all_gather(far, RING, axis=0, tiled=True)
    block = lax.dynamic_index_in_dim(inputs, micro, 0, keepdims=False)
    hidden = jnp.concatenate([block, lax.ppermute(block, "core", [(1, 0)])])
    block = lax.dynamic_index_in_dim(cotangent, micro, 0, keepdims=False)
    upstream = jnp.concatenate([lax.ppermute(block, "core", [(0, 1)]), block])

    def info(layer):
        return jnp.stack([(stage == layer).astype(jnp.int32), flag])

    normed = jnp.zeros((ROWS, D), jnp.bfloat16)
    kept = jnp.zeros((ROWS, D), jnp.bfloat16)
    proj = jnp.zeros((ROWS, WCOLS), jnp.bfloat16)
    ctx = jnp.zeros((ROWS, HQ), jnp.bfloat16)
    for layer in range(LAYERS):
        final = layer == LAYERS - 1
        result, normed, proj, ctx, kept = forward_layer(
            final, info(layer), hidden, full_qkv, full_out, normed, proj, ctx, kept
        )
        if not final:
            hidden = lax.ppermute(result, STAGE, [(layer, layer + 1)])
    dproj = jnp.zeros((ROWS, WCOLS), jnp.bfloat16)
    ups = jnp.zeros((ROWS, D), jnp.bfloat16)
    for layer in reversed(range(LAYERS)):
        result, dproj, ups = backward_layer(
            layer == 0, info(layer), upstream, kept, proj, full_qkv, full_out, dproj, ups
        )
        if layer:
            upstream = lax.ppermute(result, STAGE, [(layer, layer - 1)])
    contract = (((0,), (0,)), ((), ()))
    part_out = lax.dot_general(ctx, ups, contract, preferred_element_type=jnp.float32).astype(jnp.bfloat16)
    part_qkv = lax.dot_general(normed, dproj, contract, preferred_element_type=jnp.float32).astype(jnp.bfloat16)
    grad_out = lax.psum_scatter(part_out, RING, scatter_dimension=0, tiled=True)
    grad_qkv = lax.psum_scatter(part_qkv, RING, scatter_dimension=0, tiled=True)
    grad_out = lax.ppermute(grad_out, NAMES, regroup(True)).astype(jnp.float32)
    grad_qkv = lax.ppermute(grad_qkv, NAMES, regroup(True)).astype(jnp.float32)
    return (grad_qkv[None], grad_out[None])


def solution(mesh):
    fine = jax.sharding.Mesh(mesh.devices.reshape(SIZES), NAMES)
    token = P(None, ("x", "zhi", "core"), None)
    weight = P(("zlo", "y"), ("x", "zhi", "core"), None)
    return jax.shard_map(
        on_device,
        mesh=fine,
        in_specs=(token, token, P(), weight, weight),
        out_specs=(weight, weight),
        check_vma=False,
    )
```

```python
import functools
import math

import jax
import jax.numpy as jnp
import numpy as np
from jax import lax
from jax.experimental import pallas as pl
from jax.experimental.pallas import tpu as pltpu
from jax.sharding import PartitionSpec as P

HEADS = 16
HEAD = 64
KVH = 4
GROUP = HEADS // KVH
ROWS = 256
HALF = 128
D = 2048
HQ = HEADS * HEAD
KV = KVH * HEAD
WCOLS = HQ + 2 * KV
CHUNK = 256
EPS = 1e-5
SCALE = 1.0 / math.sqrt(HEAD)
TO_EXP2 = SCALE * math.log2(math.e)
NT = (((1,), (1,)), ((), ()))
VMEM_LIMIT = 48 * 1024 * 1024
ANY = pl.BlockSpec(memory_space=pl.ANY)
SMEM = pl.BlockSpec(memory_space=pltpu.SMEM)


def dot_nt(left, right):
    return lax.dot_general(left, right, NT, preferred_element_type=jnp.float32)


def dot_nn(left, right):
    return jnp.dot(left, right, preferred_element_type=jnp.float32)


def cols(start, size):
    return pl.ds(pl.multiple_of(start, size), size)


def bias_matrix(joined):
    row = lax.broadcasted_iota(jnp.int32, (ROWS, ROWS), 0)
    col = lax.broadcasted_iota(jnp.int32, (ROWS, ROWS), 1)
    same = (row >= HALF) == (col >= HALF)
    return jnp.where(jnp.logical_or(same, joined > 0), 0.0, -1e30).astype(jnp.float32)


def probs_t(keys, query, bias):
    logits = dot_nt(keys, query) * TO_EXP2 + bias
    total = jnp.sum(jnp.exp2(logits), axis=0, keepdims=True)
    return jnp.exp2(logits - jnp.log2(total))


def forward_kernel(
    final, info, h_in, wq_in, wo_in, a0, a1, a2, a3,
    h_out, normed_out, proj_out, ctx_out, keep_out,
    h_v, normed_v, wq_v, wo_v, proj_v, ctx_v, out_v, bias_v, key_s, vt_s, in_sem, q_sem, o_sem, w_sem,
):
    del a0, a1, a2, a3

    @pl.when(info[0] == 1)
    def _():
        h_copy = pltpu.make_async_copy(h_in, h_v, in_sem)
        h_copy.start()

        def q_copy(i):
            c = cols(i * CHUNK, CHUNK)
            return pltpu.make_async_copy(wq_in.at[:, c], wq_v.at[:, c], q_sem.at[i])

        def o_copy(i):
            c = cols(i * CHUNK, CHUNK)
            return pltpu.make_async_copy(wo_in.at[:, c], wo_v.at[:, c], o_sem.at[i])

        for i in (4, 5, 0, 1, 2, 3):
            q_copy(i).start()
        if not final:
            for i in range(8):
                o_copy(i).start()
        bias_v[...] = bias_matrix(info[1])
        h_copy.wait()
        keep = pltpu.make_async_copy(h_v, keep_out, w_sem.at[0])
        keep.start()
        wide = h_v[...].astype(jnp.float32)
        scale = lax.rsqrt(jnp.mean(wide * wide, axis=-1, keepdims=True) + EPS)
        normed_v[...] = (wide * scale).astype(jnp.bfloat16)
        normed_copy = pltpu.make_async_copy(normed_v, normed_out, w_sem.at[1])
        normed_copy.start()
        q_copy(4).wait()
        q_copy(5).wait()
        keys = dot_nn(normed_v[...], wq_v[:, HQ : HQ + KV]).astype(jnp.bfloat16)
        proj_v[:, HQ : HQ + KV] = keys
        values = dot_nn(normed_v[...], wq_v[:, HQ + KV :])
        proj_v[:, HQ + KV :] = values.astype(jnp.bfloat16)
        values_t = values.T.astype(jnp.bfloat16)
        for g in range(KVH):
            key_s[g] = keys[:, g * HEAD : (g + 1) * HEAD]
            vt_s[g] = values_t[g * HEAD : (g + 1) * HEAD, :]

        def group(g, carry):
            c = cols(g * CHUNK, CHUNK)
            q_copy(g).wait()
            queries = dot_nn(normed_v[...], wq_v[:, c]).astype(jnp.bfloat16)
            proj_v[:, c] = queries
            pieces = []
            for i in range(GROUP):
                part = queries[:, i * HEAD : (i + 1) * HEAD]
                weights = probs_t(key_s[g], part, bias_v[...]).astype(jnp.bfloat16)
                pieces.append(dot_nn(vt_s[g], weights))
            ctx_v[:, c] = jnp.concatenate(pieces, axis=0).T.astype(jnp.bfloat16)
            return carry

        lax.fori_loop(0, KVH, group, 0)
        proj_copy = pltpu.make_async_copy(proj_v, proj_out, w_sem.at[2])
        proj_copy.start()
        ctx_copy = pltpu.make_async_copy(ctx_v, ctx_out, w_sem.at[3])
        ctx_copy.start()

        def finish(i, carry):
            c = cols(i * CHUNK, CHUNK)
            o_copy(i).wait()
            out = h_v[:, c].astype(jnp.float32) + dot_nn(ctx_v[...], wo_v[:, c])
            out_v[:, c] = out.astype(jnp.bfloat16)
            return carry

        if not final:
            lax.fori_loop(0, 8, finish, 0)
            out_copy = pltpu.make_async_copy(out_v, h_out, w_sem.at[4])
            out_copy.start()
            out_copy.wait()
        keep.wait()
        normed_copy.wait()
        proj_copy.wait()
        ctx_copy.wait()


def bf16(*shape):
    return jax.ShapeDtypeStruct(shape, jnp.bfloat16)


def v16(*shape):
    return pltpu.VMEM(shape, jnp.bfloat16)


def v32(*shape):
    return pltpu.VMEM(shape, jnp.float32)


def forward_layer(final, info, hidden, w_qkv, w_out, normed, proj, ctx, kept):
    return pl.pallas_call(
        functools.partial(forward_kernel, final),
        out_shape=(bf16(ROWS, D), bf16(ROWS, D), bf16(ROWS, WCOLS), bf16(ROWS, HQ), bf16(ROWS, D)),
        in_specs=[SMEM] + [ANY] * 7,
        out_specs=(ANY,) * 5,
        input_output_aliases={4: 1, 5: 2, 6: 3, 7: 4},
        scratch_shapes=[
            v16(ROWS, D), v16(ROWS, D), v16(D, WCOLS), v16(HQ, D), v16(ROWS, WCOLS), v16(ROWS, HQ), v16(ROWS, D),
            v32(ROWS, ROWS), v16(KVH, ROWS, HEAD), v16(KVH, HEAD, ROWS),
            pltpu.SemaphoreType.DMA, pltpu.SemaphoreType.DMA((6,)), pltpu.SemaphoreType.DMA((8,)),
            pltpu.SemaphoreType.DMA((5,)),
        ],
        compiler_params=pltpu.CompilerParams(vmem_limit_bytes=VMEM_LIMIT),
        cost_estimate=pl.CostEstimate(flops=3_000_000_000, bytes_accessed=14_000_000, transcendentals=2_000_000),
        name="forward_last" if final else "forward_layer",
    )(info, hidden, w_qkv, w_out, normed, proj, ctx, kept)


def backward_kernel(
    last, info, u_in, h_in, proj_in, wq_in, wo_in, a0, a1,
    up_out, dproj_out, keep_out,
    u_v, h_v, proj_v, wq_v, wo_v, dproj_v, dn_v, bias_v, key_s, kt_s, value_s, dk_s, dv_s,
    in_sem, q_sem, o_sem, w_sem,
):
    del a0, a1

    @pl.when(info[0] == 1)
    def _():
        u_copy = pltpu.make_async_copy(u_in, u_v, in_sem.at[0])
        u_copy.start()
        proj_copy = pltpu.make_async_copy(proj_in, proj_v, in_sem.at[1])
        h_copy = pltpu.make_async_copy(h_in, h_v, in_sem.at[2])

        def o_copy(i):
            r = cols(i * CHUNK, CHUNK)
            return pltpu.make_async_copy(wo_in.at[r, :], wo_v.at[r, :], o_sem.at[i])

        def q_copy(i):
            r = cols(i * CHUNK, CHUNK)
            return pltpu.make_async_copy(wq_in.at[r, :], wq_v.at[r, :], q_sem.at[i])

        o_copy(0).start()
        proj_copy.start()
        for i in range(1, 4):
            o_copy(i).start()
        if not last:
            h_copy.start()
            for i in range(8):
                q_copy(i).start()
        bias_v[...] = bias_matrix(info[1])
        proj_copy.wait()
        keys_t = proj_v[:, HQ : HQ + KV].astype(jnp.float32).T.astype(jnp.bfloat16)
        for g in range(KVH):
            key_s[g] = proj_v[:, HQ + g * HEAD : HQ + (g + 1) * HEAD]
            value_s[g] = proj_v[:, HQ + KV + g * HEAD : HQ + KV + (g + 1) * HEAD]
            kt_s[g] = keys_t[g * HEAD : (g + 1) * HEAD, :]
        u_copy.wait()
        keep = pltpu.make_async_copy(u_v, keep_out, w_sem.at[0])
        keep.start()

        def group(g, carry):
            c = cols(g * CHUNK, CHUNK)
            o_copy(g).wait()
            d_ctx = dot_nt(u_v[...], wo_v[c, :]).astype(jnp.bfloat16)
            queries = proj_v[:, c]
            pieces = []
            d_key = jnp.zeros((ROWS, HEAD), jnp.float32)
            d_value = jnp.zeros((ROWS, HEAD), jnp.float32)
            for i in range(GROUP):
                part = queries[:, i * HEAD : (i + 1) * HEAD]
                d_part = d_ctx[:, i * HEAD : (i + 1) * HEAD]
                weights = probs_t(key_s[g], part, bias_v[...])
                d_weights = dot_nt(value_s[g], d_part)
                inner = jnp.sum(d_weights * weights, axis=0, keepdims=True)
                d_scores = (weights * (d_weights - inner) * SCALE).astype(jnp.bfloat16)
                pieces.append(dot_nn(kt_s[g], d_scores))
                d_key += dot_nn(d_scores, part)
                d_value += dot_nn(weights.astype(jnp.bfloat16), d_part)
            dproj_v[:, c] = jnp.concatenate(pieces, axis=0).T.astype(jnp.bfloat16)
            dk_s[g] = d_key.astype(jnp.bfloat16)
            dv_s[g] = d_value.astype(jnp.bfloat16)
            return carry

        lax.fori_loop(0, KVH, group, 0)
        dproj_v[:, HQ : HQ + KV] = jnp.concatenate([dk_s[g] for g in range(KVH)], axis=1)
        dproj_v[:, HQ + KV :] = jnp.concatenate([dv_s[g] for g in range(KVH)], axis=1)
        dproj_copy = pltpu.make_async_copy(dproj_v, dproj_out, w_sem.at[1])
        dproj_copy.start()
        if not last:
            h_copy.wait()

            def widen(i, partial):
                c = cols(i * CHUNK, CHUNK)
                q_copy(i).wait()
                d_normed = dot_nt(dproj_v[...], wq_v[c, :])
                dn_v[:, c] = d_normed
                product = d_normed * h_v[:, c].astype(jnp.float32)
                return partial + product[:, :HALF] + product[:, HALF:]

            partial = lax.fori_loop(0, 8, widen, jnp.zeros((ROWS, HALF), jnp.float32))
            mean = jnp.sum(partial, axis=-1, keepdims=True) * (1.0 / D)
            wide = h_v[...].astype(jnp.float32)
            scale = lax.rsqrt(jnp.mean(wide * wide, axis=-1, keepdims=True) + EPS)
            pull = scale * scale * scale * mean

            def previous(i, carry):
                c = cols(i * CHUNK, CHUNK)
                out = u_v[:, c].astype(jnp.float32) + (scale * dn_v[:, c] - h_v[:, c].astype(jnp.float32) * pull)
                h_v[:, c] = out.astype(jnp.bfloat16)
                return carry

            lax.fori_loop(0, 8, previous, 0)
            up_copy = pltpu.make_async_copy(h_v, up_out, w_sem.at[2])
            up_copy.start()
            up_copy.wait()
        keep.wait()
        dproj_copy.wait()


def backward_layer(last, info, upstream, kept, proj, w_qkv, w_out, dproj, ups):
    return pl.pallas_call(
        functools.partial(backward_kernel, last),
        out_shape=(bf16(ROWS, D), bf16(ROWS, WCOLS), bf16(ROWS, D)),
        in_specs=[SMEM] + [ANY] * 7,
        out_specs=(ANY,) * 3,
        input_output_aliases={6: 1, 7: 2},
        scratch_shapes=[
            v16(ROWS, D), v16(ROWS, D), v16(ROWS, WCOLS), v16(D, WCOLS), v16(HQ, D), v16(ROWS, WCOLS), v32(ROWS, D),
            v32(ROWS, ROWS), v16(KVH, ROWS, HEAD), v16(KVH, HEAD, ROWS), v16(KVH, ROWS, HEAD),
            v16(KVH, ROWS, HEAD), v16(KVH, ROWS, HEAD),
            pltpu.SemaphoreType.DMA((3,)), pltpu.SemaphoreType.DMA((8,)), pltpu.SemaphoreType.DMA((4,)),
            pltpu.SemaphoreType.DMA((3,)),
        ],
        compiler_params=pltpu.CompilerParams(vmem_limit_bytes=VMEM_LIMIT),
        cost_estimate=pl.CostEstimate(flops=4_000_000_000, bytes_accessed=15_000_000, transcendentals=2_000_000),
        name="backward_last" if last else "backward_layer",
    )(info, upstream, kept, proj, w_qkv, w_out, dproj, ups)


LAYERS = 8
FINE = (("zlo", 2), ("y", 4), ("x", 4), ("zhi", 4), ("core", 2))
NAMES = tuple(name for name, size in FINE)
SIZES = tuple(size for name, size in FINE)
STAGE = ("y", "core")


def regroup(back):
    pairs = []
    for zlo, y, x, zhi, core in np.ndindex(*SIZES):
        source = np.ravel_multi_index((zlo, y, x, zhi, core), SIZES)
        target = np.ravel_multi_index((core, zlo * 2 + y // 2, x, zhi, y % 2), SIZES)
        pairs.append((int(target), int(source)) if back else (int(source), int(target)))
    return pairs


def z_index(z):
    return (z % 2) * 4 + z // 2


def send_x(value, step):
    return lax.ppermute(value, "x", [(i, (i + step) % 4) for i in range(4)])


def send_z(value, step):
    return lax.ppermute(value, ("zlo", "zhi"), [(z_index(i), z_index((i + step) % 8)) for i in range(8)])


def gather_ring(own, count, send):
    below, above = [own], [own]
    for step in range(count // 2 - 1):
        below.append(send(below[-1], 1))
        above.append(send(above[-1], -1))
    half = own.shape[0] // 2
    far = [send(below[-1][:half], 1), send(above[-1][half:], -1)]
    return above + far + below[:0:-1]


def scatter_ring(take, count, send, axis):
    far = count // 2

    def halves(value):
        return jnp.split(value, 2, axis=axis)

    def add(own, came):
        return (own.astype(jnp.float32) + came.astype(jnp.float32)).astype(jnp.bfloat16)

    low, high = halves(take(far))
    up, down = send(low, 1), send(high, -1)
    for step in range(far - 1, 0, -1):
        if step == far - 1:
            low, high = halves(take(step))
            next_up = jnp.concatenate([add(low, up), high], axis=axis)
            low, high = halves(take(-step))
            next_down = jnp.concatenate([low, add(high, down)], axis=axis)
        else:
            next_up, next_down = add(take(step), up), add(take(-step), down)
        up, down = send(next_up, 1), send(next_down, -1)
    total = take(0).astype(jnp.float32) + up.astype(jnp.float32) + down.astype(jnp.float32)
    return total.astype(jnp.bfloat16)


def assemble_kernel(place, *refs):
    qkv_parts, out_parts, (full_qkv, full_out, sems) = refs[:5], refs[5:14], refs[14:]
    x, z = place[0], place[1]
    copies = []
    for ref, dx, first, pieces in zip(qkv_parts, (0, 1, 2, 2, 3), (0, 0, 0, 4, 0), (8, 8, 4, 4, 8)):
        for i in range(pieces):
            row = (lax.rem(x + dx, 4) * 8 + lax.rem(z + first + i, 8)) * 64
            target = full_qkv.at[pl.ds(pl.multiple_of(row, 64), 64), :]
            copies.append(pltpu.make_async_copy(ref.at[pl.ds(i * 64, 64), :], target, sems.at[len(copies)]))
    for ref, dz, first, pieces in zip(
        out_parts, (0, 1, 2, 3, 4, 4, 5, 6, 7), (0, 0, 0, 0, 0, 2, 0, 0, 0), (4, 4, 4, 4, 2, 2, 4, 4, 4)
    ):
        for i in range(pieces):
            row = (lax.rem(x + first + i, 4) * 8 + lax.rem(z + dz, 8)) * 32
            target = full_out.at[pl.ds(pl.multiple_of(row, 32), 32), :]
            copies.append(pltpu.make_async_copy(ref.at[pl.ds(i * 32, 32), :], target, sems.at[len(copies)]))
    for copy in copies:
        copy.start()
    for copy in copies:
        copy.wait()


def gather_weights(near, far, x, z):
    column = jnp.concatenate(gather_ring(near, 8, send_z))
    row = jnp.concatenate(gather_ring(far, 4, send_x))
    qkv_parts = gather_ring(column, 4, send_x)
    out_parts = gather_ring(row, 8, send_z)
    return pl.pallas_call(
        assemble_kernel,
        out_shape=(bf16(D, WCOLS), bf16(HQ, D)),
        in_specs=[SMEM] + [ANY] * 14,
        out_specs=(ANY, ANY),
        scratch_shapes=[pltpu.SemaphoreType.DMA((64,))],
        cost_estimate=pl.CostEstimate(flops=0, bytes_accessed=21_000_000, transcendentals=0),
        name="assemble",
    )(jnp.stack([x, z]), *qkv_parts, *out_parts)


def scatter_qkv(part, x, z):
    part = part.reshape(4, 512, WCOLS)
    mine = scatter_ring(lambda d: lax.dynamic_index_in_dim(part, (x + d) % 4, 0, keepdims=False), 4, send_x, 0)
    mine = mine.reshape(8, 64, WCOLS)
    return scatter_ring(lambda d: lax.dynamic_index_in_dim(mine, (z + d) % 8, 0, keepdims=False), 8, send_z, 0)


def scatter_out(part, x, z):
    part = part.reshape(4, 8, 32, D)
    mine = scatter_ring(lambda d: lax.dynamic_index_in_dim(part, (z + d) % 8, 1, keepdims=False), 8, send_z, 0)
    return scatter_ring(lambda d: lax.dynamic_index_in_dim(mine, (x + d) % 4, 0, keepdims=False), 4, send_x, 0)


def on_device(inputs, cotangent, joined, w_qkv, w_out):
    micro = lax.axis_index("zlo")
    stage = 2 * lax.axis_index("y") + lax.axis_index("core")
    x_index = lax.axis_index("x")
    z_place = 2 * lax.axis_index("zhi") + micro
    bin_index = 4 * x_index + lax.axis_index("zhi")
    flag = joined[micro, bin_index]
    near = lax.ppermute(w_qkv[0], NAMES, regroup(False))
    far = lax.ppermute(w_out[0], NAMES, regroup(False))
    full_qkv, full_out = gather_weights(near, far, x_index, z_place)
    block = lax.dynamic_index_in_dim(inputs, micro, 0, keepdims=False)
    hidden = jnp.concatenate([block, lax.ppermute(block, "core", [(1, 0)])])
    block = lax.dynamic_index_in_dim(cotangent, micro, 0, keepdims=False)
    upstream = jnp.concatenate([lax.ppermute(block, "core", [(0, 1)]), block])

    def info(layer):
        return jnp.stack([(stage == layer).astype(jnp.int32), flag])

    normed = jnp.zeros((ROWS, D), jnp.bfloat16)
    kept = jnp.zeros((ROWS, D), jnp.bfloat16)
    proj = jnp.zeros((ROWS, WCOLS), jnp.bfloat16)
    ctx = jnp.zeros((ROWS, HQ), jnp.bfloat16)
    for layer in range(LAYERS):
        final = layer == LAYERS - 1
        result, normed, proj, ctx, kept = forward_layer(
            final, info(layer), hidden, full_qkv, full_out, normed, proj, ctx, kept
        )
        if not final:
            hidden = lax.ppermute(result, STAGE, [(layer, layer + 1)])
    dproj = jnp.zeros((ROWS, WCOLS), jnp.bfloat16)
    ups = jnp.zeros((ROWS, D), jnp.bfloat16)
    for layer in reversed(range(LAYERS)):
        result, dproj, ups = backward_layer(
            layer == 0, info(layer), upstream, kept, proj, full_qkv, full_out, dproj, ups
        )
        if layer:
            upstream = lax.ppermute(result, STAGE, [(layer, layer - 1)])
    contract = (((0,), (0,)), ((), ()))
    part_out = lax.dot_general(ctx, ups, contract, preferred_element_type=jnp.float32).astype(jnp.bfloat16)
    part_qkv = lax.dot_general(normed, dproj, contract, preferred_element_type=jnp.float32).astype(jnp.bfloat16)
    grad_out = scatter_out(part_out, x_index, z_place)
    grad_qkv = scatter_qkv(part_qkv, x_index, z_place)
    grad_out = lax.ppermute(grad_out, NAMES, regroup(True)).astype(jnp.float32)
    grad_qkv = lax.ppermute(grad_qkv, NAMES, regroup(True)).astype(jnp.float32)
    return (grad_qkv[None], grad_out[None])


def solution(mesh):
    fine = jax.sharding.Mesh(mesh.devices.reshape(SIZES), NAMES)
    token = P(None, ("x", "zhi", "core"), None)
    weight = P(("zlo", "y"), ("x", "zhi", "core"), None)
    return jax.shard_map(
        on_device,
        mesh=fine,
        in_specs=(token, token, P(), weight, weight),
        out_specs=(weight, weight),
        check_vma=False,
    )
```

```python
import functools
import math

import jax
import jax.numpy as jnp
import numpy as np
from jax import lax
from jax.experimental import pallas as pl
from jax.experimental.pallas import tpu as pltpu
from jax.sharding import PartitionSpec as P

HEADS = 16
HEAD = 64
KVH = 4
GROUP = HEADS // KVH
ROWS = 256
HALF = 128
D = 2048
HQ = HEADS * HEAD
KV = KVH * HEAD
WCOLS = HQ + 2 * KV
CHUNK = 256
EPS = 1e-5
SCALE = 1.0 / math.sqrt(HEAD)
TO_EXP2 = SCALE * math.log2(math.e)
NT = (((1,), (1,)), ((), ()))
VMEM_LIMIT = 40 * 1024 * 1024
ANY = pl.BlockSpec(memory_space=pl.ANY)
SMEM = pl.BlockSpec(memory_space=pltpu.SMEM)
INSIDE = pl.BlockSpec(memory_space=pltpu.VMEM)


def dot_nt(left, right):
    return lax.dot_general(left, right, NT, preferred_element_type=jnp.float32)


def dot_nn(left, right):
    return jnp.dot(left, right, preferred_element_type=jnp.float32)


def cols(start, size):
    return pl.ds(pl.multiple_of(start, size), size)


def packed_halves(tile, upper):
    lane = lax.broadcasted_iota(jnp.int32, tile.shape, 1)
    wide = tile.astype(jnp.float32)
    kept = jnp.where((lane >= HEAD) == upper, wide, 0.0)
    turned = pltpu.roll(kept, HEAD, 1)
    low, high = (turned, kept) if upper else (kept, turned)
    return low.astype(jnp.bfloat16), high.astype(jnp.bfloat16)


def fill_keys(keys, key_s, joined):
    row = lax.broadcasted_iota(jnp.int32, (ROWS, 2 * HEAD), 0)
    lane = lax.broadcasted_iota(jnp.int32, (ROWS, 2 * HEAD), 1)
    hidden = jnp.where(joined > 0, 0.0, -1e30)
    other = jnp.logical_or(
        jnp.logical_and(lane == 3, row >= HALF), jnp.logical_and(lane == 4, row < HALF)
    )
    apart = jnp.where(other, hidden, 0.0)
    low_marks = jnp.where(lane < 3, -1.0, apart).astype(jnp.bfloat16)
    high_marks = jnp.where(jnp.logical_and(lane >= HEAD, lane < HEAD + 3), -1.0, apart).astype(jnp.bfloat16)
    for g in range(KVH):
        low, high = packed_halves(keys[:, g // 2 * 128 : g // 2 * 128 + 128], g % 2 == 1)
        key_s[g, :ROWS, :128] = low
        key_s[g, ROWS:, :128] = high
        key_s[g, :ROWS, 128:] = low_marks
        key_s[g, ROWS:, 128:] = high_marks


def fill_values(values, value_s, mark):
    lane = lax.broadcasted_iota(jnp.int32, (ROWS, 2 * HEAD), 1)
    low_marks = jnp.where(lane < HEAD, mark, 0.0).astype(jnp.bfloat16)
    high_marks = jnp.where(lane >= HEAD, mark, 0.0).astype(jnp.bfloat16)
    for g in range(KVH):
        low, high = packed_halves(values[:, g // 2 * 128 : g // 2 * 128 + 128], g % 2 == 1)
        value_s[g, :ROWS, :128] = low
        value_s[g, ROWS:, :128] = high
        value_s[g, :ROWS, 128:] = low_marks
        value_s[g, ROWS:, 128:] = high_marks


def stack_pairs(value):
    return jnp.concatenate([value[:, :128], value[:, 128:]], axis=0)


def forward_kernel(
    final, layer, place, h_in, wq_v, wo_v, a0, a1, a2, a3, a4,
    h_out, normed_out, proj_out, ctx_out, keep_out, marks_out,
    h_v, normed_v, proj_v, ctx_v, out_v, marks_v, key_s, value_s, in_sem, w_sem,
):
    del a0, a1, a2, a3, a4

    @pl.when(place[0] == layer)
    def _():
        h_copy = pltpu.make_async_copy(h_in, h_v, in_sem)
        h_copy.start()
        block = (lax.broadcasted_iota(jnp.int32, (2 * ROWS, 128), 0) // HALF) % 2
        lane = lax.broadcasted_iota(jnp.int32, (2 * ROWS, 128), 1)
        spot = lane % HEAD
        seen = jnp.where(jnp.logical_or(jnp.logical_and(lane == 3, block == 0), jnp.logical_and(lane == 4, block == 1)), 1.0, 0.0)
        h_copy.wait()
        keep = pltpu.make_async_copy(h_v, keep_out, w_sem.at[0])
        keep.start()
        wide = h_v[...].astype(jnp.float32)
        scale = lax.rsqrt(jnp.mean(wide * wide, axis=-1, keepdims=True) + EPS)
        normed_v[...] = (wide * scale).astype(jnp.bfloat16)
        normed_copy = pltpu.make_async_copy(normed_v, normed_out, w_sem.at[1])
        normed_copy.start()
        both = dot_nn(normed_v[...], wq_v[:, HQ:]).astype(jnp.bfloat16)
        proj_v[:, HQ:] = both
        fill_keys(both[:, :KV], key_s, place[1])
        fill_values(both[:, KV:], value_s, 1.0)

        def group(g, carry):
            c = cols(g * CHUNK, CHUNK)
            queries = dot_nn(normed_v[...], wq_v[:, c]).astype(jnp.bfloat16)
            proj_v[:, c] = queries
            left = jnp.concatenate([stack_pairs(queries), seen.astype(jnp.bfloat16)], axis=1)
            raw = dot_nt(left, key_s[g])
            top_low = jnp.max(raw[:, :ROWS], axis=1, keepdims=True)
            top_high = jnp.max(raw[:, ROWS:], axis=1, keepdims=True)
            weights = jnp.concatenate(
                [jnp.exp2((raw[:, :ROWS] - top_low) * TO_EXP2), jnp.exp2((raw[:, ROWS:] - top_high) * TO_EXP2)], axis=1
            ).astype(jnp.bfloat16)
            mixed = dot_nn(weights, value_s[g])
            total = mixed[:, 128:]
            context = (mixed[:, :128] / total).astype(jnp.bfloat16)
            ctx_v[:, c] = jnp.concatenate([context[:ROWS], context[ROWS:]], axis=1)
            level = jnp.where(lane < HEAD, top_low, top_high) + jnp.log2(total) * (1.0 / TO_EXP2)
            first = level.astype(jnp.bfloat16).astype(jnp.float32)
            second = (level - first).astype(jnp.bfloat16).astype(jnp.float32)
            third = level - first - second
            marks = jnp.where(
                spot == 0, first, jnp.where(spot == 1, second, jnp.where(spot == 2, third, seen))
            ).astype(jnp.bfloat16)
            marks_v[:, c] = jnp.concatenate([marks[:ROWS], marks[ROWS:]], axis=1)
            return carry

        lax.fori_loop(0, KVH, group, 0)
        copies = [
            pltpu.make_async_copy(proj_v, proj_out, w_sem.at[2]),
            pltpu.make_async_copy(ctx_v, ctx_out, w_sem.at[3]),
            pltpu.make_async_copy(marks_v, marks_out, w_sem.at[5]),
        ]
        for copy in copies:
            copy.start()

        def finish(i, carry):
            c = cols(i * CHUNK, CHUNK)
            out = h_v[:, c].astype(jnp.float32) + dot_nn(ctx_v[...], wo_v[:, c])
            out_v[:, c] = out.astype(jnp.bfloat16)
            return carry

        if not final:
            lax.fori_loop(0, 8, finish, 0)
            out_copy = pltpu.make_async_copy(out_v, h_out, w_sem.at[4])
            out_copy.start()
            out_copy.wait()
        keep.wait()
        normed_copy.wait()
        for copy in copies:
            copy.wait()


def bf16(*shape):
    return jax.ShapeDtypeStruct(shape, jnp.bfloat16)


def v16(*shape):
    return pltpu.VMEM(shape, jnp.bfloat16)


def v32(*shape):
    return pltpu.VMEM(shape, jnp.float32)


def forward_layer(layer, place, hidden, w_qkv, w_out, normed, proj, ctx, kept, marks):
    final = layer == 7
    return pl.pallas_call(
        functools.partial(forward_kernel, final, layer),
        out_shape=(
            bf16(ROWS, D), bf16(ROWS, D), bf16(ROWS, WCOLS), bf16(ROWS, HQ), bf16(ROWS, D), bf16(ROWS, HQ)
        ),
        in_specs=[SMEM, ANY, INSIDE, INSIDE] + [ANY] * 5,
        out_specs=(ANY,) * 6,
        input_output_aliases={4: 1, 5: 2, 6: 3, 7: 4, 8: 5},
        scratch_shapes=[
            v16(ROWS, D), v16(ROWS, D), v16(ROWS, WCOLS), v16(ROWS, HQ), v16(ROWS, D), v16(ROWS, HQ),
            v16(KVH, 2 * ROWS, 256), v16(KVH, 2 * ROWS, 256),
            pltpu.SemaphoreType.DMA, pltpu.SemaphoreType.DMA((6,)),
        ],
        compiler_params=pltpu.CompilerParams(vmem_limit_bytes=VMEM_LIMIT),
        cost_estimate=pl.CostEstimate(flops=3_000_000_000, bytes_accessed=14_000_000, transcendentals=2_000_000),
        name="forward_last" if final else "forward_layer",
    )(place, hidden, w_qkv, w_out, normed, proj, ctx, kept, marks)


def backward_kernel(
    last, layer, place, u_in, h_in, proj_in, ctx_in, marks_in, wq_v, wo_v, a0, a1,
    up_out, dproj_out, keep_out,
    u_v, h_v, proj_v, ctx_v, marks_v, dproj_v, dn_v, key_s, value_s, dkt_s, dvt_s, in_sem, w_sem,
):
    del a0, a1

    @pl.when(place[0] == layer)
    def _():
        u_copy = pltpu.make_async_copy(u_in, u_v, in_sem.at[0])
        u_copy.start()
        proj_copy = pltpu.make_async_copy(proj_in, proj_v, in_sem.at[1])
        h_copy = pltpu.make_async_copy(h_in, h_v, in_sem.at[2])
        ctx_copy = pltpu.make_async_copy(ctx_in, ctx_v, in_sem.at[3])
        marks_copy = pltpu.make_async_copy(marks_in, marks_v, in_sem.at[4])
        proj_copy.start()
        ctx_copy.start()
        marks_copy.start()
        if not last:
            h_copy.start()
        proj_copy.wait()
        fill_keys(proj_v[:, HQ : HQ + KV], key_s, place[1])
        fill_values(proj_v[:, HQ + KV :], value_s, -1.0)
        u_copy.wait()
        keep = pltpu.make_async_copy(u_v, keep_out, w_sem.at[0])
        keep.start()
        ctx_copy.wait()
        marks_copy.wait()

        def group(g, carry):
            c = cols(g * CHUNK, CHUNK)
            d_ctx = dot_nt(u_v[...], wo_v[c, :]).astype(jnp.bfloat16)
            queries = stack_pairs(proj_v[:, c])
            d_pairs = stack_pairs(d_ctx)
            left = jnp.concatenate([queries, stack_pairs(marks_v[:, c])], axis=1)
            weights = jnp.exp2(dot_nt(left, key_s[g]) * TO_EXP2)
            inner = d_pairs.astype(jnp.float32) * stack_pairs(ctx_v[:, c]).astype(jnp.float32)
            d_left = jnp.concatenate([d_pairs, inner.astype(jnp.bfloat16)], axis=1)
            d_scores = (weights * dot_nt(d_left, value_s[g])).astype(jnp.bfloat16)
            d_query = (dot_nn(d_scores, key_s[g][:, :128]) * SCALE).astype(jnp.bfloat16)
            dproj_v[:, c] = jnp.concatenate([d_query[:ROWS], d_query[ROWS:]], axis=1)
            d_key = dot_nn(queries.T, d_scores)
            d_value = dot_nn(d_pairs.T, weights.astype(jnp.bfloat16))
            rows = pl.ds(pl.multiple_of(g * HEAD, HEAD), HEAD)
            dkt_s[rows, :] = (d_key[:HEAD, :ROWS] + d_key[HEAD:, ROWS:]) * SCALE
            dvt_s[rows, :] = d_value[:HEAD, :ROWS] + d_value[HEAD:, ROWS:]
            return carry

        lax.fori_loop(0, KVH, group, 0)
        dproj_v[:, HQ : HQ + KV] = dkt_s[...].T.astype(jnp.bfloat16)
        dproj_v[:, HQ + KV :] = dvt_s[...].T.astype(jnp.bfloat16)
        dproj_copy = pltpu.make_async_copy(dproj_v, dproj_out, w_sem.at[1])
        dproj_copy.start()
        if not last:
            h_copy.wait()

            def widen(i, partial):
                c = cols(i * CHUNK, CHUNK)
                d_normed = dot_nt(dproj_v[...], wq_v[c, :])
                dn_v[:, c] = d_normed
                product = d_normed * h_v[:, c].astype(jnp.float32)
                return partial + product[:, :HALF] + product[:, HALF:]

            partial = lax.fori_loop(0, 8, widen, jnp.zeros((ROWS, HALF), jnp.float32))
            mean = jnp.sum(partial, axis=-1, keepdims=True) * (1.0 / D)
            wide = h_v[...].astype(jnp.float32)
            scale = lax.rsqrt(jnp.mean(wide * wide, axis=-1, keepdims=True) + EPS)
            pull = scale * scale * scale * mean

            def previous(i, carry):
                c = cols(i * CHUNK, CHUNK)
                out = u_v[:, c].astype(jnp.float32) + (scale * dn_v[:, c] - h_v[:, c].astype(jnp.float32) * pull)
                h_v[:, c] = out.astype(jnp.bfloat16)
                return carry

            lax.fori_loop(0, 8, previous, 0)
            up_copy = pltpu.make_async_copy(h_v, up_out, w_sem.at[2])
            up_copy.start()
            up_copy.wait()
        keep.wait()
        dproj_copy.wait()


def backward_layer(layer, place, upstream, kept, proj, ctx, marks, w_qkv, w_out, dproj, ups):
    last = layer == 0
    return pl.pallas_call(
        functools.partial(backward_kernel, last, layer),
        out_shape=(bf16(ROWS, D), bf16(ROWS, WCOLS), bf16(ROWS, D)),
        in_specs=[SMEM] + [ANY] * 5 + [INSIDE, INSIDE] + [ANY] * 2,
        out_specs=(ANY,) * 3,
        input_output_aliases={8: 1, 9: 2},
        scratch_shapes=[
            v16(ROWS, D), v16(ROWS, D), v16(ROWS, WCOLS), v16(ROWS, HQ), v16(ROWS, HQ), v16(ROWS, WCOLS), v32(ROWS, D),
            v16(KVH, 2 * ROWS, 256), v16(KVH, 2 * ROWS, 256), v32(KV, ROWS), v32(KV, ROWS),
            pltpu.SemaphoreType.DMA((5,)), pltpu.SemaphoreType.DMA((3,)),
        ],
        compiler_params=pltpu.CompilerParams(vmem_limit_bytes=VMEM_LIMIT),
        cost_estimate=pl.CostEstimate(flops=4_000_000_000, bytes_accessed=15_000_000, transcendentals=2_000_000),
        name="backward_last" if last else "backward_layer",
    )(place, upstream, kept, proj, ctx, marks, w_qkv, w_out, dproj, ups)


LAYERS = 8
FINE = (("zlo", 2), ("y", 4), ("x", 4), ("zhi", 4), ("core", 2))
NAMES = tuple(name for name, size in FINE)
SIZES = tuple(size for name, size in FINE)
STAGE = ("y", "core")


def regroup(back):
    pairs = []
    for zlo, y, x, zhi, core in np.ndindex(*SIZES):
        source = np.ravel_multi_index((zlo, y, x, zhi, core), SIZES)
        target = np.ravel_multi_index((core, zlo * 2 + y // 2, x, zhi, y % 2), SIZES)
        pairs.append((int(target), int(source)) if back else (int(source), int(target)))
    return pairs


def z_index(z):
    return (z % 2) * 4 + z // 2


def send_x(value, step):
    return lax.ppermute(value, "x", [(i, (i + step) % 4) for i in range(4)])


def send_z(value, step):
    return lax.ppermute(value, ("zlo", "zhi"), [(z_index(i), z_index((i + step) % 8)) for i in range(8)])


def gather_ring(own, count, send):
    below, above = [own], [own]
    for step in range(count // 2 - 1):
        below.append(send(below[-1], 1))
        above.append(send(above[-1], -1))
    half = own.shape[0] // 2
    far = [send(below[-1][:half], 1), send(above[-1][half:], -1)]
    return above + far + below[:0:-1]


def scatter_ring(take, count, send, axis):
    far = count // 2

    def halves(value):
        return jnp.split(value, 2, axis=axis)

    def add(own, came):
        return (own.astype(jnp.float32) + came.astype(jnp.float32)).astype(jnp.bfloat16)

    low, high = halves(take(far))
    up, down = send(low, 1), send(high, -1)
    for step in range(far - 1, 0, -1):
        if step == far - 1:
            low, high = halves(take(step))
            next_up = jnp.concatenate([add(low, up), high], axis=axis)
            low, high = halves(take(-step))
            next_down = jnp.concatenate([low, add(high, down)], axis=axis)
        else:
            next_up, next_down = add(take(step), up), add(take(-step), down)
        up, down = send(next_up, 1), send(next_down, -1)
    total = take(0).astype(jnp.float32) + up.astype(jnp.float32) + down.astype(jnp.float32)
    return total.astype(jnp.bfloat16)


def assemble_kernel(place, *refs):
    qkv_parts, out_parts, (full_qkv, full_out, sems) = refs[:5], refs[5:14], refs[14:]
    x, z = place[0], place[1]
    copies = []
    for ref, dx, first, pieces in zip(qkv_parts, (0, 1, 2, 2, 3), (0, 0, 0, 4, 0), (8, 8, 4, 4, 8)):
        for i in range(pieces):
            row = (lax.rem(x + dx, 4) * 8 + lax.rem(z + first + i, 8)) * 64
            target = full_qkv.at[pl.ds(pl.multiple_of(row, 64), 64), :]
            copies.append(pltpu.make_async_copy(ref.at[pl.ds(i * 64, 64), :], target, sems.at[len(copies)]))
    for ref, dz, first, pieces in zip(
        out_parts, (0, 1, 2, 3, 4, 4, 5, 6, 7), (0, 0, 0, 0, 0, 2, 0, 0, 0), (4, 4, 4, 4, 2, 2, 4, 4, 4)
    ):
        for i in range(pieces):
            row = (lax.rem(x + first + i, 4) * 8 + lax.rem(z + dz, 8)) * 32
            target = full_out.at[pl.ds(pl.multiple_of(row, 32), 32), :]
            copies.append(pltpu.make_async_copy(ref.at[pl.ds(i * 32, 32), :], target, sems.at[len(copies)]))
    for copy in copies:
        copy.start()
    for copy in copies:
        copy.wait()


def gather_weights(near, far, x, z):
    column = jnp.concatenate(gather_ring(near, 8, send_z))
    row = jnp.concatenate(gather_ring(far, 4, send_x))
    qkv_parts = gather_ring(column, 4, send_x)
    out_parts = gather_ring(row, 8, send_z)
    return pl.pallas_call(
        assemble_kernel,
        out_shape=(v16(D, WCOLS), v16(HQ, D)),
        in_specs=[SMEM] + [ANY] * 14,
        out_specs=(INSIDE, INSIDE),
        scratch_shapes=[pltpu.SemaphoreType.DMA((64,))],
        compiler_params=pltpu.CompilerParams(vmem_limit_bytes=4 * 1024 * 1024),
        cost_estimate=pl.CostEstimate(flops=0, bytes_accessed=21_000_000, transcendentals=0),
        name="assemble",
    )(jnp.stack([x, z]), *qkv_parts, *out_parts)


def scatter_qkv(part, x, z):
    part = part.reshape(4, 512, WCOLS)
    mine = scatter_ring(lambda d: lax.dynamic_index_in_dim(part, (x + d) % 4, 0, keepdims=False), 4, send_x, 0)
    mine = mine.reshape(8, 64, WCOLS)
    return scatter_ring(lambda d: lax.dynamic_index_in_dim(mine, (z + d) % 8, 0, keepdims=False), 8, send_z, 0)


def scatter_out(part, x, z):
    part = part.reshape(4, 8, 32, D)
    mine = scatter_ring(lambda d: lax.dynamic_index_in_dim(part, (z + d) % 8, 1, keepdims=False), 8, send_z, 0)
    return scatter_ring(lambda d: lax.dynamic_index_in_dim(mine, (x + d) % 4, 0, keepdims=False), 4, send_x, 0)


def on_device(inputs, cotangent, joined, w_qkv, w_out):
    micro = lax.axis_index("zlo")
    stage = 2 * lax.axis_index("y") + lax.axis_index("core")
    x_index = lax.axis_index("x")
    z_place = 2 * lax.axis_index("zhi") + micro
    bin_index = 4 * x_index + lax.axis_index("zhi")
    flag = joined[micro, bin_index]
    near = lax.ppermute(w_qkv[0], NAMES, regroup(False))
    far = lax.ppermute(w_out[0], NAMES, regroup(False))
    full_qkv, full_out = gather_weights(near, far, x_index, z_place)
    block = lax.dynamic_index_in_dim(inputs, micro, 0, keepdims=False)
    hidden = jnp.concatenate([block, lax.ppermute(block, "core", [(1, 0)])])
    block = lax.dynamic_index_in_dim(cotangent, micro, 0, keepdims=False)
    upstream = jnp.concatenate([lax.ppermute(block, "core", [(0, 1)]), block])

    place = jnp.stack([stage, flag])
    normed = jnp.zeros((ROWS, D), jnp.bfloat16)
    kept = jnp.zeros((ROWS, D), jnp.bfloat16)
    proj = jnp.zeros((ROWS, WCOLS), jnp.bfloat16)
    ctx = jnp.zeros((ROWS, HQ), jnp.bfloat16)
    marks = jnp.zeros((ROWS, HQ), jnp.bfloat16)
    for layer in range(LAYERS):
        result, normed, proj, ctx, kept, marks = forward_layer(
            layer, place, hidden, full_qkv, full_out, normed, proj, ctx, kept, marks
        )
        if layer < LAYERS - 1:
            hidden = lax.ppermute(result, STAGE, [(layer, layer + 1)])
    dproj = jnp.zeros((ROWS, WCOLS), jnp.bfloat16)
    ups = jnp.zeros((ROWS, D), jnp.bfloat16)
    for layer in reversed(range(LAYERS)):
        result, dproj, ups = backward_layer(
            layer, place, upstream, kept, proj, ctx, marks, full_qkv, full_out, dproj, ups
        )
        if layer:
            upstream = lax.ppermute(result, STAGE, [(layer, layer - 1)])
    contract = (((0,), (0,)), ((), ()))
    part_out = lax.dot_general(ctx, ups, contract, preferred_element_type=jnp.float32).astype(jnp.bfloat16)
    part_qkv = lax.dot_general(normed, dproj, contract, preferred_element_type=jnp.float32).astype(jnp.bfloat16)
    grad_out = scatter_out(part_out, x_index, z_place)
    grad_qkv = scatter_qkv(part_qkv, x_index, z_place)
    grad_out = lax.ppermute(grad_out, NAMES, regroup(True)).astype(jnp.float32)
    grad_qkv = lax.ppermute(grad_qkv, NAMES, regroup(True)).astype(jnp.float32)
    return (grad_qkv[None], grad_out[None])


def solution(mesh):
    fine = jax.sharding.Mesh(mesh.devices.reshape(SIZES), NAMES)
    token = P(None, ("x", "zhi", "core"), None)
    weight = P(("zlo", "y"), ("x", "zhi", "core"), None)
    return jax.shard_map(
        on_device,
        mesh=fine,
        in_specs=(token, token, P(), weight, weight),
        out_specs=(weight, weight),
        check_vma=False,
    )
```

```python
import functools
import math

import jax
import jax.numpy as jnp
import numpy as np
from jax import lax
from jax.experimental import pallas as pl
from jax.experimental.pallas import tpu as pltpu
from jax.sharding import PartitionSpec as P

HEADS = 16
HEAD = 64
KVH = 4
GROUP = HEADS // KVH
ROWS = 256
HALF = 128
D = 2048
HQ = HEADS * HEAD
KV = KVH * HEAD
WCOLS = HQ + 2 * KV
CHUNK = 256
EPS = 1e-5
SCALE = 1.0 / math.sqrt(HEAD)
TO_EXP2 = SCALE * math.log2(math.e)
NT = (((1,), (1,)), ((), ()))
VMEM_LIMIT = 16 * 1024 * 1024
ANY = pl.BlockSpec(memory_space=pl.ANY)
SMEM = pl.BlockSpec(memory_space=pltpu.SMEM)
INSIDE = pl.BlockSpec(memory_space=pltpu.VMEM)


def dot_nt(left, right):
    return lax.dot_general(left, right, NT, preferred_element_type=jnp.float32)


def dot_nn(left, right):
    return jnp.dot(left, right, preferred_element_type=jnp.float32)


def cols(start, size):
    return pl.ds(pl.multiple_of(start, size), size)


def packed_halves(tile, upper):
    lane = lax.broadcasted_iota(jnp.int32, tile.shape, 1)
    wide = tile.astype(jnp.float32)
    kept = jnp.where((lane >= HEAD) == upper, wide, 0.0)
    turned = pltpu.roll(kept, HEAD, 1)
    low, high = (turned, kept) if upper else (kept, turned)
    return low.astype(jnp.bfloat16), high.astype(jnp.bfloat16)


def fill_keys(keys, key_s, joined):
    row = lax.broadcasted_iota(jnp.int32, (ROWS, 2 * HEAD), 0)
    lane = lax.broadcasted_iota(jnp.int32, (ROWS, 2 * HEAD), 1)
    hidden = jnp.where(joined > 0, 0.0, -1e30)
    other = jnp.logical_or(
        jnp.logical_and(lane == 3, row >= HALF), jnp.logical_and(lane == 4, row < HALF)
    )
    apart = jnp.where(other, hidden, 0.0)
    low_marks = jnp.where(lane < 3, -1.0, apart).astype(jnp.bfloat16)
    high_marks = jnp.where(jnp.logical_and(lane >= HEAD, lane < HEAD + 3), -1.0, apart).astype(jnp.bfloat16)
    for g in range(KVH):
        low, high = packed_halves(keys[:, g // 2 * 128 : g // 2 * 128 + 128], g % 2 == 1)
        key_s[g, :ROWS, :128] = low
        key_s[g, ROWS:, :128] = high
        key_s[g, :ROWS, 128:] = low_marks
        key_s[g, ROWS:, 128:] = high_marks


def fill_values(values, value_s, mark):
    lane = lax.broadcasted_iota(jnp.int32, (ROWS, 2 * HEAD), 1)
    low_marks = jnp.where(lane < HEAD, mark, 0.0).astype(jnp.bfloat16)
    high_marks = jnp.where(lane >= HEAD, mark, 0.0).astype(jnp.bfloat16)
    for g in range(KVH):
        low, high = packed_halves(values[:, g // 2 * 128 : g // 2 * 128 + 128], g % 2 == 1)
        value_s[g, :ROWS, :128] = low
        value_s[g, ROWS:, :128] = high
        value_s[g, :ROWS, 128:] = low_marks
        value_s[g, ROWS:, 128:] = high_marks


def stack_pairs(value):
    return jnp.concatenate([value[:, :128], value[:, 128:]], axis=0)


def forward_kernel(
    final, layer, place, h_v, wq_v, wo_v, a0, a1, a2, a3, a4,
    out_v, normed_v, proj_v, ctx_v, keep_v, marks_v, key_s, value_s,
):
    del a0, a1, a2, a3, a4

    @pl.when(place[0] == layer)
    def _():
        block = (lax.broadcasted_iota(jnp.int32, (2 * ROWS, 128), 0) // HALF) % 2
        lane = lax.broadcasted_iota(jnp.int32, (2 * ROWS, 128), 1)
        spot = lane % HEAD
        seen = jnp.where(jnp.logical_or(jnp.logical_and(lane == 3, block == 0), jnp.logical_and(lane == 4, block == 1)), 1.0, 0.0)
        keep_v[...] = h_v[...]
        wide = h_v[...].astype(jnp.float32)
        scale = lax.rsqrt(jnp.mean(wide * wide, axis=-1, keepdims=True) + EPS)
        normed_v[...] = (wide * scale).astype(jnp.bfloat16)
        both = dot_nn(normed_v[...], wq_v[:, HQ:]).astype(jnp.bfloat16)
        proj_v[:, HQ:] = both
        fill_keys(both[:, :KV], key_s, place[1])
        fill_values(both[:, KV:], value_s, 1.0)

        def group(g, carry):
            c = cols(g * CHUNK, CHUNK)
            queries = dot_nn(normed_v[...], wq_v[:, c]).astype(jnp.bfloat16)
            proj_v[:, c] = queries
            left = jnp.concatenate([stack_pairs(queries), seen.astype(jnp.bfloat16)], axis=1)
            raw = dot_nt(left, key_s[g])
            top_low = jnp.max(raw[:, :ROWS], axis=1, keepdims=True)
            top_high = jnp.max(raw[:, ROWS:], axis=1, keepdims=True)
            weights = jnp.concatenate(
                [jnp.exp2((raw[:, :ROWS] - top_low) * TO_EXP2), jnp.exp2((raw[:, ROWS:] - top_high) * TO_EXP2)], axis=1
            ).astype(jnp.bfloat16)
            mixed = dot_nn(weights, value_s[g])
            total = mixed[:, 128:]
            context = (mixed[:, :128] / total).astype(jnp.bfloat16)
            ctx_v[:, c] = jnp.concatenate([context[:ROWS], context[ROWS:]], axis=1)
            level = jnp.where(lane < HEAD, top_low, top_high) + jnp.log2(total) * (1.0 / TO_EXP2)
            first = level.astype(jnp.bfloat16).astype(jnp.float32)
            second = (level - first).astype(jnp.bfloat16).astype(jnp.float32)
            third = level - first - second
            marks = jnp.where(
                spot == 0, first, jnp.where(spot == 1, second, jnp.where(spot == 2, third, seen))
            ).astype(jnp.bfloat16)
            marks_v[:, c] = jnp.concatenate([marks[:ROWS], marks[ROWS:]], axis=1)
            return carry

        lax.fori_loop(0, KVH, group, 0)
        def finish(i, carry):
            c = cols(i * CHUNK, CHUNK)
            out = h_v[:, c].astype(jnp.float32) + dot_nn(ctx_v[...], wo_v[:, c])
            out_v[:, c] = out.astype(jnp.bfloat16)
            return carry

        if not final:
            lax.fori_loop(0, 8, finish, 0)


def bf16(*shape):
    return jax.ShapeDtypeStruct(shape, jnp.bfloat16)


def inside(*arrays):
    return [pltpu.with_memory_space_constraint(array, pltpu.VMEM) for array in arrays]


def v16(*shape):
    return pltpu.VMEM(shape, jnp.bfloat16)


def v32(*shape):
    return pltpu.VMEM(shape, jnp.float32)


def forward_layer(layer, place, hidden, w_qkv, w_out, normed, proj, ctx, kept, marks):
    final = layer == 7
    return pl.pallas_call(
        functools.partial(forward_kernel, final, layer),
        out_shape=(v16(ROWS, D), v16(ROWS, D), v16(ROWS, WCOLS), v16(ROWS, HQ), v16(ROWS, D), v16(ROWS, HQ)),
        in_specs=[SMEM] + [INSIDE] * 8,
        out_specs=(INSIDE,) * 6,
        input_output_aliases={4: 1, 5: 2, 6: 3, 7: 4, 8: 5},
        scratch_shapes=[v16(KVH, 2 * ROWS, 256), v16(KVH, 2 * ROWS, 256)],
        compiler_params=pltpu.CompilerParams(vmem_limit_bytes=VMEM_LIMIT),
        cost_estimate=pl.CostEstimate(flops=3_000_000_000, bytes_accessed=14_000_000, transcendentals=2_000_000),
        name="forward_last" if final else "forward_layer",
    )(place, *inside(hidden, w_qkv, w_out, normed, proj, ctx, kept, marks))


def backward_kernel(
    last, layer, place, u_v, h_v, proj_v, ctx_v, marks_v, wq_v, wo_v, a0, a1,
    up_v, dproj_v, keep_v, dn_v, key_s, value_s, dkt_s, dvt_s,
):
    del a0, a1

    @pl.when(place[0] == layer)
    def _():
        keep_v[...] = u_v[...]
        fill_keys(proj_v[:, HQ : HQ + KV], key_s, place[1])
        fill_values(proj_v[:, HQ + KV :], value_s, -1.0)

        def group(g, carry):
            c = cols(g * CHUNK, CHUNK)
            d_ctx = dot_nt(u_v[...], wo_v[c, :]).astype(jnp.bfloat16)
            queries = stack_pairs(proj_v[:, c])
            d_pairs = stack_pairs(d_ctx)
            left = jnp.concatenate([queries, stack_pairs(marks_v[:, c])], axis=1)
            weights = jnp.exp2(dot_nt(left, key_s[g]) * TO_EXP2)
            inner = d_pairs.astype(jnp.float32) * stack_pairs(ctx_v[:, c]).astype(jnp.float32)
            d_left = jnp.concatenate([d_pairs, inner.astype(jnp.bfloat16)], axis=1)
            d_scores = (weights * dot_nt(d_left, value_s[g])).astype(jnp.bfloat16)
            d_query = (dot_nn(d_scores, key_s[g][:, :128]) * SCALE).astype(jnp.bfloat16)
            dproj_v[:, c] = jnp.concatenate([d_query[:ROWS], d_query[ROWS:]], axis=1)
            d_key = dot_nn(queries.T, d_scores)
            d_value = dot_nn(d_pairs.T, weights.astype(jnp.bfloat16))
            rows = pl.ds(pl.multiple_of(g * HEAD, HEAD), HEAD)
            dkt_s[rows, :] = (d_key[:HEAD, :ROWS] + d_key[HEAD:, ROWS:]) * SCALE
            dvt_s[rows, :] = d_value[:HEAD, :ROWS] + d_value[HEAD:, ROWS:]
            return carry

        lax.fori_loop(0, KVH, group, 0)
        dproj_v[:, HQ : HQ + KV] = dkt_s[...].T.astype(jnp.bfloat16)
        dproj_v[:, HQ + KV :] = dvt_s[...].T.astype(jnp.bfloat16)
        if not last:
            def widen(i, partial):
                c = cols(i * CHUNK, CHUNK)
                d_normed = dot_nt(dproj_v[...], wq_v[c, :])
                dn_v[:, c] = d_normed
                product = d_normed * h_v[:, c].astype(jnp.float32)
                return partial + product[:, :HALF] + product[:, HALF:]

            partial = lax.fori_loop(0, 8, widen, jnp.zeros((ROWS, HALF), jnp.float32))
            mean = jnp.sum(partial, axis=-1, keepdims=True) * (1.0 / D)
            wide = h_v[...].astype(jnp.float32)
            scale = lax.rsqrt(jnp.mean(wide * wide, axis=-1, keepdims=True) + EPS)
            pull = scale * scale * scale * mean

            def previous(i, carry):
                c = cols(i * CHUNK, CHUNK)
                out = u_v[:, c].astype(jnp.float32) + (scale * dn_v[:, c] - h_v[:, c].astype(jnp.float32) * pull)
                up_v[:, c] = out.astype(jnp.bfloat16)
                return carry

            lax.fori_loop(0, 8, previous, 0)


def backward_layer(layer, place, upstream, kept, proj, ctx, marks, w_qkv, w_out, dproj, ups):
    last = layer == 0
    spare = [place, place] if last else inside(kept, w_qkv)
    where = SMEM if last else INSIDE
    return pl.pallas_call(
        functools.partial(backward_kernel, last, layer),
        out_shape=(v16(ROWS, D), v16(ROWS, WCOLS), v16(ROWS, D)),
        in_specs=[SMEM, INSIDE, where, INSIDE, INSIDE, INSIDE, where, INSIDE, INSIDE, INSIDE],
        out_specs=(INSIDE,) * 3,
        input_output_aliases={8: 1, 9: 2},
        scratch_shapes=[
            v32(ROWS, D), v16(KVH, 2 * ROWS, 256), v16(KVH, 2 * ROWS, 256), v32(KV, ROWS), v32(KV, ROWS)
        ],
        compiler_params=pltpu.CompilerParams(vmem_limit_bytes=VMEM_LIMIT),
        cost_estimate=pl.CostEstimate(flops=4_000_000_000, bytes_accessed=15_000_000, transcendentals=2_000_000),
        name="backward_last" if last else "backward_layer",
    )(place, *inside(upstream), spare[0], *inside(proj, ctx, marks), spare[1], *inside(w_out, dproj, ups))


LAYERS = 8
FINE = (("zlo", 2), ("y", 4), ("x", 4), ("zhi", 4), ("core", 2))
NAMES = tuple(name for name, size in FINE)
SIZES = tuple(size for name, size in FINE)
STAGE = ("y", "core")


def regroup(back):
    pairs = []
    for zlo, y, x, zhi, core in np.ndindex(*SIZES):
        source = np.ravel_multi_index((zlo, y, x, zhi, core), SIZES)
        target = np.ravel_multi_index((core, zlo * 2 + y // 2, x, zhi, y % 2), SIZES)
        pairs.append((int(target), int(source)) if back else (int(source), int(target)))
    return pairs


def z_index(z):
    return (z % 2) * 4 + z // 2


def send_x(value, step):
    return lax.ppermute(value, "x", [(i, (i + step) % 4) for i in range(4)])


def send_z(value, step):
    return lax.ppermute(value, ("zlo", "zhi"), [(z_index(i), z_index((i + step) % 8)) for i in range(8)])


def gather_ring(own, count, send):
    below, above = [own], [own]
    for step in range(count // 2 - 1):
        below.append(send(below[-1], 1))
        above.append(send(above[-1], -1))
    half = own.shape[0] // 2
    far = [send(below[-1][:half], 1), send(above[-1][half:], -1)]
    return above + far + below[:0:-1]


def scatter_ring(take, count, send, axis):
    far = count // 2

    def halves(value):
        return jnp.split(value, 2, axis=axis)

    def add(own, came):
        return (own.astype(jnp.float32) + came.astype(jnp.float32)).astype(jnp.bfloat16)

    low, high = halves(take(far))
    up, down = send(low, 1), send(high, -1)
    for step in range(far - 1, 0, -1):
        if step == far - 1:
            low, high = halves(take(step))
            next_up = jnp.concatenate([add(low, up), high], axis=axis)
            low, high = halves(take(-step))
            next_down = jnp.concatenate([low, add(high, down)], axis=axis)
        else:
            next_up, next_down = add(take(step), up), add(take(-step), down)
        up, down = send(next_up, 1), send(next_down, -1)
    total = take(0).astype(jnp.float32) + up.astype(jnp.float32) + down.astype(jnp.float32)
    return total.astype(jnp.bfloat16)


def assemble_kernel(place, *refs):
    qkv_parts, out_parts, (full_qkv, full_out, sems) = refs[:5], refs[5:14], refs[14:]
    x, z = place[0], place[1]
    copies = []
    for ref, dx, first, pieces in zip(qkv_parts, (0, 1, 2, 2, 3), (0, 0, 0, 4, 0), (8, 8, 4, 4, 8)):
        for i in range(pieces):
            row = (lax.rem(x + dx, 4) * 8 + lax.rem(z + first + i, 8)) * 64
            target = full_qkv.at[pl.ds(pl.multiple_of(row, 64), 64), :]
            copies.append(pltpu.make_async_copy(ref.at[pl.ds(i * 64, 64), :], target, sems.at[len(copies)]))
    for ref, dz, first, pieces in zip(
        out_parts, (0, 1, 2, 3, 4, 4, 5, 6, 7), (0, 0, 0, 0, 0, 2, 0, 0, 0), (4, 4, 4, 4, 2, 2, 4, 4, 4)
    ):
        for i in range(pieces):
            row = (lax.rem(x + first + i, 4) * 8 + lax.rem(z + dz, 8)) * 32
            target = full_out.at[pl.ds(pl.multiple_of(row, 32), 32), :]
            copies.append(pltpu.make_async_copy(ref.at[pl.ds(i * 32, 32), :], target, sems.at[len(copies)]))
    for copy in copies:
        copy.start()
    for copy in copies:
        copy.wait()


def gather_weights(near, far, x, z):
    column = jnp.concatenate(gather_ring(near, 8, send_z))
    row = jnp.concatenate(gather_ring(far, 4, send_x))
    qkv_parts = gather_ring(column, 4, send_x)
    out_parts = gather_ring(row, 8, send_z)
    return pl.pallas_call(
        assemble_kernel,
        out_shape=(v16(D, WCOLS), v16(HQ, D)),
        in_specs=[SMEM] + [ANY] * 14,
        out_specs=(INSIDE, INSIDE),
        scratch_shapes=[pltpu.SemaphoreType.DMA((64,))],
        compiler_params=pltpu.CompilerParams(vmem_limit_bytes=4 * 1024 * 1024),
        cost_estimate=pl.CostEstimate(flops=0, bytes_accessed=21_000_000, transcendentals=0),
        name="assemble",
    )(jnp.stack([x, z]), *qkv_parts, *out_parts)


def scatter_qkv(part, turns, spins):
    part = part.reshape(4, 512, WCOLS)
    mine = scatter_ring(lambda d: lax.dynamic_index_in_dim(part, turns[d % 4], 0, keepdims=False, allow_negative_indices=False), 4, send_x, 0)
    mine = mine.reshape(8, 64, WCOLS)
    return scatter_ring(lambda d: lax.dynamic_index_in_dim(mine, spins[d % 8], 0, keepdims=False, allow_negative_indices=False), 8, send_z, 0)


def scatter_out(part, turns, spins):
    part = part.reshape(4, 8, 32, D)
    mine = scatter_ring(lambda d: lax.dynamic_index_in_dim(part, spins[d % 8], 1, keepdims=False, allow_negative_indices=False), 8, send_z, 0)
    return scatter_ring(lambda d: lax.dynamic_index_in_dim(mine, turns[d % 4], 0, keepdims=False, allow_negative_indices=False), 4, send_x, 0)


def on_device(inputs, cotangent, joined, w_qkv, w_out):
    micro = lax.axis_index("zlo")
    stage = 2 * lax.axis_index("y") + lax.axis_index("core")
    x_index = lax.axis_index("x")
    z_place = 2 * lax.axis_index("zhi") + micro
    bin_index = 4 * x_index + lax.axis_index("zhi")
    flag = joined[micro, bin_index]
    near = lax.ppermute(w_qkv[0], NAMES, regroup(False))
    far = lax.ppermute(w_out[0], NAMES, regroup(False))
    full_qkv, full_out = gather_weights(near, far, x_index, z_place)
    block = lax.dynamic_index_in_dim(inputs, micro, 0, keepdims=False)
    hidden = jnp.concatenate([block, lax.ppermute(block, "core", [(1, 0)])])
    block = lax.dynamic_index_in_dim(cotangent, micro, 0, keepdims=False)
    upstream = jnp.concatenate([lax.ppermute(block, "core", [(0, 1)]), block])

    place = jnp.stack([stage, flag])
    turns = [((x_index + d) % 4) for d in range(4)]
    spins = [((z_place + d) % 8) for d in range(8)]
    place, turns, spins = lax.optimization_barrier((place, turns, spins))
    normed = jnp.zeros((ROWS, D), jnp.bfloat16)
    kept = jnp.zeros((ROWS, D), jnp.bfloat16)
    proj = jnp.zeros((ROWS, WCOLS), jnp.bfloat16)
    ctx = jnp.zeros((ROWS, HQ), jnp.bfloat16)
    marks = jnp.zeros((ROWS, HQ), jnp.bfloat16)
    for layer in range(LAYERS):
        result, normed, proj, ctx, kept, marks = forward_layer(
            layer, place, hidden, full_qkv, full_out, normed, proj, ctx, kept, marks
        )
        if layer < LAYERS - 1:
            hidden = lax.ppermute(result, STAGE, [(layer, layer + 1)])
    dproj = jnp.zeros((ROWS, WCOLS), jnp.bfloat16)
    ups = jnp.zeros((ROWS, D), jnp.bfloat16)
    for layer in reversed(range(LAYERS)):
        result, dproj, ups = backward_layer(
            layer, place, upstream, kept, proj, ctx, marks, full_qkv, full_out, dproj, ups
        )
        if layer:
            upstream = lax.ppermute(result, STAGE, [(layer, layer - 1)])
    ups, dproj, turns, spins = lax.optimization_barrier((ups, dproj, turns, spins))
    contract = (((0,), (0,)), ((), ()))
    part_out = lax.dot_general(ctx, ups, contract, preferred_element_type=jnp.float32).astype(jnp.bfloat16)
    part_qkv = lax.dot_general(normed, dproj, contract, preferred_element_type=jnp.float32).astype(jnp.bfloat16)
    grad_out = scatter_out(part_out, turns, spins)
    grad_qkv = scatter_qkv(part_qkv, turns, spins)
    grad_out = lax.ppermute(grad_out, NAMES, regroup(True)).astype(jnp.float32)
    grad_qkv = lax.ppermute(grad_qkv, NAMES, regroup(True)).astype(jnp.float32)
    return (grad_qkv[None], grad_out[None])


def solution(mesh):
    fine = jax.sharding.Mesh(mesh.devices.reshape(SIZES), NAMES)
    token = P(None, ("x", "zhi", "core"), None)
    weight = P(("zlo", "y"), ("x", "zhi", "core"), None)
    return jax.shard_map(
        on_device,
        mesh=fine,
        in_specs=(token, token, P(), weight, weight),
        out_specs=(weight, weight),
        check_vma=False,
    )
```

```python
import functools
import math

import jax
import jax.numpy as jnp
import numpy as np
from jax import lax
from jax.experimental import pallas as pl
from jax.experimental.pallas import tpu as pltpu
from jax.sharding import PartitionSpec as P

HEADS = 16
HEAD = 64
KVH = 4
GROUP = HEADS // KVH
ROWS = 256
HALF = 128
D = 2048
HQ = HEADS * HEAD
KV = KVH * HEAD
WCOLS = HQ + 2 * KV
CHUNK = 256
EPS = 1e-5
SCALE = 1.0 / math.sqrt(HEAD)
TO_EXP2 = SCALE * math.log2(math.e)
NT = (((1,), (1,)), ((), ()))
VMEM_LIMIT = 16 * 1024 * 1024
ANY = pl.BlockSpec(memory_space=pl.ANY)
SMEM = pl.BlockSpec(memory_space=pltpu.SMEM)
INSIDE = pl.BlockSpec(memory_space=pltpu.VMEM)


def dot_nt(left, right):
    return lax.dot_general(left, right, NT, preferred_element_type=jnp.float32)


def dot_nn(left, right):
    return jnp.dot(left, right, preferred_element_type=jnp.float32)


def cols(start, size):
    return pl.ds(pl.multiple_of(start, size), size)


def packed_halves(tile, upper):
    lane = lax.broadcasted_iota(jnp.int32, tile.shape, 1)
    wide = tile.astype(jnp.float32)
    kept = jnp.where((lane >= HEAD) == upper, wide, 0.0)
    turned = pltpu.roll(kept, HEAD, 1)
    low, high = (turned, kept) if upper else (kept, turned)
    return low.astype(jnp.bfloat16), high.astype(jnp.bfloat16)


def fill_keys(keys, key_s, joined):
    row = lax.broadcasted_iota(jnp.int32, (ROWS, 2 * HEAD), 0)
    lane = lax.broadcasted_iota(jnp.int32, (ROWS, 2 * HEAD), 1)
    hidden = jnp.where(joined > 0, 0.0, -1e30)
    other = jnp.logical_or(
        jnp.logical_and(lane == 3, row >= HALF), jnp.logical_and(lane == 4, row < HALF)
    )
    apart = jnp.where(other, hidden, 0.0)
    low_marks = jnp.where(lane < 3, -1.0, apart).astype(jnp.bfloat16)
    high_marks = jnp.where(jnp.logical_and(lane >= HEAD, lane < HEAD + 3), -1.0, apart).astype(jnp.bfloat16)
    for g in range(KVH):
        low, high = packed_halves(keys[:, g // 2 * 128 : g // 2 * 128 + 128], g % 2 == 1)
        key_s[g, :ROWS, :128] = low
        key_s[g, ROWS:, :128] = high
        key_s[g, :ROWS, 128:] = low_marks
        key_s[g, ROWS:, 128:] = high_marks


def fill_values(values, value_s, mark):
    lane = lax.broadcasted_iota(jnp.int32, (ROWS, 2 * HEAD), 1)
    low_marks = jnp.where(lane < HEAD, mark, 0.0).astype(jnp.bfloat16)
    high_marks = jnp.where(lane >= HEAD, mark, 0.0).astype(jnp.bfloat16)
    for g in range(KVH):
        low, high = packed_halves(values[:, g // 2 * 128 : g // 2 * 128 + 128], g % 2 == 1)
        value_s[g, :ROWS, :128] = low
        value_s[g, ROWS:, :128] = high
        value_s[g, :ROWS, 128:] = low_marks
        value_s[g, ROWS:, 128:] = high_marks


def stack_pairs(value):
    return jnp.concatenate([value[:, :128], value[:, 128:]], axis=0)


def forward_kernel(
    final, place, h_v, wq_v, wo_v, a0, a1, a2, a3, a4,
    out_v, normed_v, proj_v, ctx_v, keep_v, marks_v, key_s, value_s,
):
    del a0, a1, a2, a3, a4

    @pl.when(place[0] == 0)
    def _():
        block = (lax.broadcasted_iota(jnp.int32, (2 * ROWS, 128), 0) // HALF) % 2
        lane = lax.broadcasted_iota(jnp.int32, (2 * ROWS, 128), 1)
        spot = lane % HEAD
        seen = jnp.where(jnp.logical_or(jnp.logical_and(lane == 3, block == 0), jnp.logical_and(lane == 4, block == 1)), 1.0, 0.0)
        keep_v[...] = h_v[...]
        wide = h_v[...].astype(jnp.float32)
        scale = lax.rsqrt(jnp.mean(wide * wide, axis=-1, keepdims=True) + EPS)
        normed_v[...] = (wide * scale).astype(jnp.bfloat16)
        both = dot_nn(normed_v[...], wq_v[:, HQ:]).astype(jnp.bfloat16)
        proj_v[:, HQ:] = both
        fill_keys(both[:, :KV], key_s, place[1])
        fill_values(both[:, KV:], value_s, 1.0)

        def group(g, carry):
            c = cols(g * CHUNK, CHUNK)
            queries = dot_nn(normed_v[...], wq_v[:, c]).astype(jnp.bfloat16)
            proj_v[:, c] = queries
            left = jnp.concatenate([stack_pairs(queries), seen.astype(jnp.bfloat16)], axis=1)
            raw = dot_nt(left, key_s[g])
            top_low = jnp.max(raw[:, :ROWS], axis=1, keepdims=True)
            top_high = jnp.max(raw[:, ROWS:], axis=1, keepdims=True)
            weights = jnp.concatenate(
                [jnp.exp2((raw[:, :ROWS] - top_low) * TO_EXP2), jnp.exp2((raw[:, ROWS:] - top_high) * TO_EXP2)], axis=1
            ).astype(jnp.bfloat16)
            mixed = dot_nn(weights, value_s[g])
            total = mixed[:, 128:]
            context = (mixed[:, :128] / total).astype(jnp.bfloat16)
            ctx_v[:, c] = jnp.concatenate([context[:ROWS], context[ROWS:]], axis=1)
            level = jnp.where(lane < HEAD, top_low, top_high) + jnp.log2(total) * (1.0 / TO_EXP2)
            first = level.astype(jnp.bfloat16).astype(jnp.float32)
            second = (level - first).astype(jnp.bfloat16).astype(jnp.float32)
            third = level - first - second
            marks = jnp.where(
                spot == 0, first, jnp.where(spot == 1, second, jnp.where(spot == 2, third, seen))
            ).astype(jnp.bfloat16)
            marks_v[:, c] = jnp.concatenate([marks[:ROWS], marks[ROWS:]], axis=1)
            return carry

        lax.fori_loop(0, KVH, group, 0)
        def finish(i, carry):
            c = cols(i * CHUNK, CHUNK)
            out = h_v[:, c].astype(jnp.float32) + dot_nn(ctx_v[...], wo_v[:, c])
            out_v[:, c] = out.astype(jnp.bfloat16)
            return carry

        if not final:
            lax.fori_loop(0, 8, finish, 0)


def bf16(*shape):
    return jax.ShapeDtypeStruct(shape, jnp.bfloat16)


def inside(*arrays):
    return [pltpu.with_memory_space_constraint(array, pltpu.VMEM) for array in arrays]


def v16(*shape):
    return pltpu.VMEM(shape, jnp.bfloat16)


def v32(*shape):
    return pltpu.VMEM(shape, jnp.float32)


def forward_layer(layer, place, hidden, w_qkv, w_out, normed, proj, ctx, kept, marks):
    final = layer == 7
    return pl.pallas_call(
        functools.partial(forward_kernel, final),
        out_shape=(v16(ROWS, D), v16(ROWS, D), v16(ROWS, WCOLS), v16(ROWS, HQ), v16(ROWS, D), v16(ROWS, HQ)),
        in_specs=[SMEM] + [INSIDE] * 8,
        out_specs=(INSIDE,) * 6,
        input_output_aliases={4: 1, 5: 2, 6: 3, 7: 4, 8: 5},
        scratch_shapes=[v16(KVH, 2 * ROWS, 256), v16(KVH, 2 * ROWS, 256)],
        compiler_params=pltpu.CompilerParams(vmem_limit_bytes=VMEM_LIMIT),
        cost_estimate=pl.CostEstimate(flops=3_000_000_000, bytes_accessed=14_000_000, transcendentals=2_000_000),
        name="forward_last" if final else "forward_layer",
    )(place, *inside(hidden, w_qkv, w_out, normed, proj, ctx, kept, marks))


def backward_kernel(
    last, place, u_v, h_v, proj_v, ctx_v, marks_v, wq_v, wo_v, a0, a1,
    up_v, dproj_v, keep_v, dn_v, key_s, value_s, dkt_s, dvt_s,
):
    del a0, a1

    @pl.when(place[0] == 0)
    def _():
        keep_v[...] = u_v[...]
        fill_keys(proj_v[:, HQ : HQ + KV], key_s, place[1])
        fill_values(proj_v[:, HQ + KV :], value_s, -1.0)

        def group(g, carry):
            c = cols(g * CHUNK, CHUNK)
            d_ctx = dot_nt(u_v[...], wo_v[c, :]).astype(jnp.bfloat16)
            queries = stack_pairs(proj_v[:, c])
            d_pairs = stack_pairs(d_ctx)
            left = jnp.concatenate([queries, stack_pairs(marks_v[:, c])], axis=1)
            weights = jnp.exp2(dot_nt(left, key_s[g]) * TO_EXP2)
            inner = d_pairs.astype(jnp.float32) * stack_pairs(ctx_v[:, c]).astype(jnp.float32)
            d_left = jnp.concatenate([d_pairs, inner.astype(jnp.bfloat16)], axis=1)
            d_scores = (weights * dot_nt(d_left, value_s[g])).astype(jnp.bfloat16)
            d_query = (dot_nn(d_scores, key_s[g][:, :128]) * SCALE).astype(jnp.bfloat16)
            dproj_v[:, c] = jnp.concatenate([d_query[:ROWS], d_query[ROWS:]], axis=1)
            d_key = dot_nn(queries.T, d_scores)
            d_value = dot_nn(d_pairs.T, weights.astype(jnp.bfloat16))
            rows = pl.ds(pl.multiple_of(g * HEAD, HEAD), HEAD)
            dkt_s[rows, :] = (d_key[:HEAD, :ROWS] + d_key[HEAD:, ROWS:]) * SCALE
            dvt_s[rows, :] = d_value[:HEAD, :ROWS] + d_value[HEAD:, ROWS:]
            return carry

        lax.fori_loop(0, KVH, group, 0)
        dproj_v[:, HQ : HQ + KV] = dkt_s[...].T.astype(jnp.bfloat16)
        dproj_v[:, HQ + KV :] = dvt_s[...].T.astype(jnp.bfloat16)
        if not last:
            def widen(i, partial):
                c = cols(i * CHUNK, CHUNK)
                d_normed = dot_nt(dproj_v[...], wq_v[c, :])
                dn_v[:, c] = d_normed
                product = d_normed * h_v[:, c].astype(jnp.float32)
                return partial + product[:, :HALF] + product[:, HALF:]

            partial = lax.fori_loop(0, 8, widen, jnp.zeros((ROWS, HALF), jnp.float32))
            mean = jnp.sum(partial, axis=-1, keepdims=True) * (1.0 / D)
            wide = h_v[...].astype(jnp.float32)
            scale = lax.rsqrt(jnp.mean(wide * wide, axis=-1, keepdims=True) + EPS)
            pull = scale * scale * scale * mean

            def previous(i, carry):
                c = cols(i * CHUNK, CHUNK)
                out = u_v[:, c].astype(jnp.float32) + (scale * dn_v[:, c] - h_v[:, c].astype(jnp.float32) * pull)
                up_v[:, c] = out.astype(jnp.bfloat16)
                return carry

            lax.fori_loop(0, 8, previous, 0)


def backward_layer(layer, place, upstream, kept, proj, ctx, marks, w_qkv, w_out, dproj, ups):
    last = layer == 0
    spare = [place, place] if last else inside(kept, w_qkv)
    where = SMEM if last else INSIDE
    return pl.pallas_call(
        functools.partial(backward_kernel, last),
        out_shape=(v16(ROWS, D), v16(ROWS, WCOLS), v16(ROWS, D)),
        in_specs=[SMEM, INSIDE, where, INSIDE, INSIDE, INSIDE, where, INSIDE, INSIDE, INSIDE],
        out_specs=(INSIDE,) * 3,
        input_output_aliases={8: 1, 9: 2},
        scratch_shapes=[
            v32(ROWS, D), v16(KVH, 2 * ROWS, 256), v16(KVH, 2 * ROWS, 256), v32(KV, ROWS), v32(KV, ROWS)
        ],
        compiler_params=pltpu.CompilerParams(vmem_limit_bytes=VMEM_LIMIT),
        cost_estimate=pl.CostEstimate(flops=4_000_000_000, bytes_accessed=15_000_000, transcendentals=2_000_000),
        name="backward_last" if last else "backward_layer",
    )(place, *inside(upstream), spare[0], *inside(proj, ctx, marks), spare[1], *inside(w_out, dproj, ups))


LAYERS = 8
FINE = (("zlo", 2), ("y", 4), ("x", 4), ("zhi", 4), ("core", 2))
NAMES = tuple(name for name, size in FINE)
SIZES = tuple(size for name, size in FINE)
STAGE = ("y", "core")


def regroup(back):
    pairs = []
    for zlo, y, x, zhi, core in np.ndindex(*SIZES):
        source = np.ravel_multi_index((zlo, y, x, zhi, core), SIZES)
        target = np.ravel_multi_index((core, zlo * 2 + y // 2, x, zhi, y % 2), SIZES)
        pairs.append((int(target), int(source)) if back else (int(source), int(target)))
    return pairs


def z_index(z):
    return (z % 2) * 4 + z // 2


def send_x(value, step):
    return lax.ppermute(value, "x", [(i, (i + step) % 4) for i in range(4)])


def send_z(value, step):
    return lax.ppermute(value, ("zlo", "zhi"), [(z_index(i), z_index((i + step) % 8)) for i in range(8)])


def gather_ring(own, count, send):
    below, above = [own], [own]
    for step in range(count // 2 - 1):
        below.append(send(below[-1], 1))
        above.append(send(above[-1], -1))
    half = own.shape[0] // 2
    far = [send(below[-1][:half], 1), send(above[-1][half:], -1)]
    return above + far + below[:0:-1]


def add(own, came):
    return (own.astype(jnp.float32) + came.astype(jnp.float32)).astype(jnp.bfloat16)


def scatter_ring(take, count, send):
    far = count // 2
    up, down = send(take(far, 0), 1), send(take(far, 1), -1)
    for step in range(far - 1, 0, -1):
        if step == far - 1:
            next_up = jnp.concatenate([add(take(step, 0), up), take(step, 1)])
            next_down = jnp.concatenate([take(-step, 0), add(take(-step, 1), down)])
        else:
            next_up, next_down = add(take(step), up), add(take(-step), down)
        up, down = send(next_up, 1), send(next_down, -1)
    total = take(0).astype(jnp.float32) + up.astype(jnp.float32) + down.astype(jnp.float32)
    return total.astype(jnp.bfloat16)


def scatter_direct(take, send):
    total = take(0).astype(jnp.float32)
    for came in [send(take(step), step) for step in (2, 1, -1)]:
        total = total + came.astype(jnp.float32)
    return total.astype(jnp.bfloat16)


def gather_direct(own, send):
    far, above, below = send(own, 2), send(own, -1), send(own, 1)
    return [own, above, far, below]


def taker(value, spots, axis, split):
    def take(d, half=None):
        spot = spots[d % len(spots)]
        start, size = [0] * value.ndim, list(value.shape)
        start[axis], size[axis] = spot, 1
        if half is not None:
            size[split] //= 2
            start[split] = half * size[split]
        block = lax.dynamic_slice(value, start, size, allow_negative_indices=False)
        return block.reshape([n for dim, n in enumerate(size) if dim != axis])

    return take


def assemble_kernel(place, *refs):
    qkv_parts, out_parts, (full_qkv, full_out, sems) = refs[:5], refs[5:14], refs[14:]
    x, z = place[0], place[1]
    copies = []
    for ref, dx, first, pieces in zip(qkv_parts, (0, 1, 2, 2, 3), (0, 0, 0, 4, 0), (8, 8, 4, 4, 8)):
        for i in range(pieces):
            row = (lax.rem(x + dx, 4) * 8 + lax.rem(z + first + i, 8)) * 64
            target = full_qkv.at[pl.ds(pl.multiple_of(row, 64), 64), :]
            copies.append(pltpu.make_async_copy(ref.at[pl.ds(i * 64, 64), :], target, sems.at[len(copies)]))
    for ref, dz, first, pieces in zip(
        out_parts, (0, 1, 2, 3, 4, 4, 5, 6, 7), (0, 0, 0, 0, 0, 2, 0, 0, 0), (4, 4, 4, 4, 2, 2, 4, 4, 4)
    ):
        for i in range(pieces):
            row = (lax.rem(x + first + i, 4) * 8 + lax.rem(z + dz, 8)) * 32
            target = full_out.at[pl.ds(pl.multiple_of(row, 32), 32), :]
            copies.append(pltpu.make_async_copy(ref.at[pl.ds(i * 32, 32), :], target, sems.at[len(copies)]))
    for copy in copies:
        copy.start()
    for copy in copies:
        copy.wait()


def gather_weights(near, far, x, z):
    column = jnp.concatenate(gather_ring(near, 8, send_z))
    row = jnp.concatenate(gather_direct(far, send_x))
    qkv_parts = gather_ring(column, 4, send_x)
    out_parts = gather_ring(row, 8, send_z)
    return pl.pallas_call(
        assemble_kernel,
        out_shape=(v16(D, WCOLS), v16(HQ, D)),
        in_specs=[SMEM] + [ANY] * 14,
        out_specs=(INSIDE, INSIDE),
        scratch_shapes=[pltpu.SemaphoreType.DMA((64,))],
        compiler_params=pltpu.CompilerParams(vmem_limit_bytes=4 * 1024 * 1024),
        cost_estimate=pl.CostEstimate(flops=0, bytes_accessed=21_000_000, transcendentals=0),
        name="assemble",
    )(jnp.stack([x, z]), *qkv_parts, *out_parts)


def scatter_qkv(part, turns, spins):
    mine = scatter_ring(taker(part.reshape(4, 512, WCOLS), turns, 0, 1), 4, send_x)
    return scatter_ring(taker(mine.reshape(8, 64, WCOLS), spins, 0, 1), 8, send_z)


def scatter_out(part, turns, spins):
    mine = scatter_ring(taker(part.reshape(4, 8, 32, D), spins, 1, 0), 8, send_z)
    return scatter_direct(taker(mine, turns, 0, 1), send_x)


def on_device(inputs, cotangent, joined, w_qkv, w_out):
    micro = lax.axis_index("zlo")
    stage = 2 * lax.axis_index("y") + lax.axis_index("core")
    x_index = lax.axis_index("x")
    z_place = 2 * lax.axis_index("zhi") + micro
    bin_index = 4 * x_index + lax.axis_index("zhi")
    flag = joined[micro, bin_index]
    near = lax.ppermute(w_qkv[0], NAMES, regroup(False))
    far = lax.ppermute(w_out[0], NAMES, regroup(False))
    full_qkv, full_out = gather_weights(near, far, x_index, z_place)
    block = lax.dynamic_index_in_dim(inputs, micro, 0, keepdims=False)
    hidden = jnp.concatenate([block, lax.ppermute(block, "core", [(1, 0)])])
    block = lax.dynamic_index_in_dim(cotangent, micro, 0, keepdims=False)
    upstream = jnp.concatenate([lax.ppermute(block, "core", [(0, 1)]), block])

    places = [jnp.stack([stage - layer, flag]) for layer in range(LAYERS)]
    turns = [((x_index + d) % 4) for d in range(4)]
    spins = [((z_place + d) % 8) for d in range(8)]
    places, turns, spins = lax.optimization_barrier((places, turns, spins))
    normed = jnp.zeros((ROWS, D), jnp.bfloat16)
    kept = jnp.zeros((ROWS, D), jnp.bfloat16)
    proj = jnp.zeros((ROWS, WCOLS), jnp.bfloat16)
    ctx = jnp.zeros((ROWS, HQ), jnp.bfloat16)
    marks = jnp.zeros((ROWS, HQ), jnp.bfloat16)
    for layer in range(LAYERS):
        result, normed, proj, ctx, kept, marks = forward_layer(
            layer, places[layer], hidden, full_qkv, full_out, normed, proj, ctx, kept, marks
        )
        if layer < LAYERS - 1:
            hidden = lax.ppermute(result, STAGE, [(layer, layer + 1)])
    dproj = jnp.zeros((ROWS, WCOLS), jnp.bfloat16)
    ups = jnp.zeros((ROWS, D), jnp.bfloat16)
    contract = (((0,), (0,)), ((), ()))
    for layer in reversed(range(LAYERS)):
        if layer == 0:
            arrived = jnp.where(stage == 0, upstream, ups)
            part_out = lax.dot_general(ctx, arrived, contract, preferred_element_type=jnp.float32).astype(jnp.bfloat16)
            part_out, upstream = lax.optimization_barrier((part_out, upstream))
        result, dproj, ups = backward_layer(
            layer, places[layer], upstream, kept, proj, ctx, marks, full_qkv, full_out, dproj, ups
        )
        if layer:
            upstream = lax.ppermute(result, STAGE, [(layer, layer - 1)])
    part_qkv = lax.dot_general(normed, dproj, contract, preferred_element_type=jnp.float32).astype(jnp.bfloat16)
    grad_out = scatter_out(part_out, turns, spins)
    grad_qkv = scatter_qkv(part_qkv, turns, spins)
    grad_out = lax.ppermute(grad_out, NAMES, regroup(True)).astype(jnp.float32)
    grad_qkv = lax.ppermute(grad_qkv, NAMES, regroup(True)).astype(jnp.float32)
    return (grad_qkv[None], grad_out[None])


def solution(mesh):
    fine = jax.sharding.Mesh(mesh.devices.reshape(SIZES), NAMES)
    token = P(None, ("x", "zhi", "core"), None)
    weight = P(("zlo", "y"), ("x", "zhi", "core"), None)
    return jax.shard_map(
        on_device,
        mesh=fine,
        in_specs=(token, token, P(), weight, weight),
        out_specs=(weight, weight),
        check_vma=False,
    )
```

```python
import functools
import math

import jax
import jax.numpy as jnp
import numpy as np
from jax import lax
from jax.experimental import pallas as pl
from jax.experimental.pallas import tpu as pltpu
from jax.sharding import PartitionSpec as P

HEADS = 16
HEAD = 64
KVH = 4
GROUP = HEADS // KVH
ROWS = 256
HALF = 128
D = 2048
HQ = HEADS * HEAD
KV = KVH * HEAD
WCOLS = HQ + 2 * KV
CHUNK = 256
EPS = 1e-5
SCALE = 1.0 / math.sqrt(HEAD)
TO_EXP2 = SCALE * math.log2(math.e)
NT = (((1,), (1,)), ((), ()))
VMEM_LIMIT = 16 * 1024 * 1024
ANY = pl.BlockSpec(memory_space=pl.ANY)
SMEM = pl.BlockSpec(memory_space=pltpu.SMEM)
INSIDE = pl.BlockSpec(memory_space=pltpu.VMEM)


def dot_nt(left, right):
    return lax.dot_general(left, right, NT, preferred_element_type=jnp.float32)


def dot_nn(left, right):
    return jnp.dot(left, right, preferred_element_type=jnp.float32)


def cols(start, size):
    return pl.ds(pl.multiple_of(start, size), size)


def packed_halves(tile, upper):
    lane = lax.broadcasted_iota(jnp.int32, tile.shape, 1)
    wide = tile.astype(jnp.float32)
    kept = jnp.where((lane >= HEAD) == upper, wide, 0.0)
    turned = pltpu.roll(kept, HEAD, 1)
    low, high = (turned, kept) if upper else (kept, turned)
    return low.astype(jnp.bfloat16), high.astype(jnp.bfloat16)


def fill_keys(keys, key_s, joined):
    row = lax.broadcasted_iota(jnp.int32, (ROWS, 2 * HEAD), 0)
    lane = lax.broadcasted_iota(jnp.int32, (ROWS, 2 * HEAD), 1)
    hidden = jnp.where(joined > 0, 0.0, -1e30)
    other = jnp.logical_or(
        jnp.logical_and(lane == 3, row >= HALF), jnp.logical_and(lane == 4, row < HALF)
    )
    apart = jnp.where(other, hidden, 0.0)
    low_marks = jnp.where(lane < 3, -1.0, apart).astype(jnp.bfloat16)
    high_marks = jnp.where(jnp.logical_and(lane >= HEAD, lane < HEAD + 3), -1.0, apart).astype(jnp.bfloat16)
    for g in range(KVH):
        low, high = packed_halves(keys[:, g // 2 * 128 : g // 2 * 128 + 128], g % 2 == 1)
        key_s[g, :ROWS, :128] = low
        key_s[g, ROWS:, :128] = high
        key_s[g, :ROWS, 128:] = low_marks
        key_s[g, ROWS:, 128:] = high_marks


def fill_values(values, value_s, mark):
    lane = lax.broadcasted_iota(jnp.int32, (ROWS, 2 * HEAD), 1)
    low_marks = jnp.where(lane < HEAD, mark, 0.0).astype(jnp.bfloat16)
    high_marks = jnp.where(lane >= HEAD, mark, 0.0).astype(jnp.bfloat16)
    for g in range(KVH):
        low, high = packed_halves(values[:, g // 2 * 128 : g // 2 * 128 + 128], g % 2 == 1)
        value_s[g, :ROWS, :128] = low
        value_s[g, ROWS:, :128] = high
        value_s[g, :ROWS, 128:] = low_marks
        value_s[g, ROWS:, 128:] = high_marks


def stack_pairs(value):
    return jnp.concatenate([value[:, :128], value[:, 128:]], axis=0)


def forward_kernel(
    final, place, h_v, wq_v, wo_v, a0, a1, a2, a3, a4,
    out_v, normed_v, proj_v, ctx_v, keep_v, marks_v, key_s, value_s,
):
    del a0, a1, a2, a3, a4

    @pl.when(place[0] == 0)
    def _():
        block = (lax.broadcasted_iota(jnp.int32, (2 * ROWS, 128), 0) // HALF) % 2
        lane = lax.broadcasted_iota(jnp.int32, (2 * ROWS, 128), 1)
        spot = lane % HEAD
        seen = jnp.where(jnp.logical_or(jnp.logical_and(lane == 3, block == 0), jnp.logical_and(lane == 4, block == 1)), 1.0, 0.0)
        keep_v[...] = h_v[...]
        wide = h_v[...].astype(jnp.float32)
        scale = lax.rsqrt(jnp.mean(wide * wide, axis=-1, keepdims=True) + EPS)
        normed_v[...] = (wide * scale).astype(jnp.bfloat16)
        both = dot_nn(normed_v[...], wq_v[:, HQ:]).astype(jnp.bfloat16)
        proj_v[:, HQ:] = both
        fill_keys(both[:, :KV], key_s, place[1])
        fill_values(both[:, KV:], value_s, 1.0)

        def group(g, carry):
            c = cols(g * CHUNK, CHUNK)
            queries = dot_nn(normed_v[...], wq_v[:, c]).astype(jnp.bfloat16)
            proj_v[:, c] = queries
            left = jnp.concatenate([stack_pairs(queries), seen.astype(jnp.bfloat16)], axis=1)
            raw = dot_nt(left, key_s[g])
            top_low = jnp.max(raw[:, :ROWS], axis=1, keepdims=True)
            top_high = jnp.max(raw[:, ROWS:], axis=1, keepdims=True)
            weights = jnp.concatenate(
                [jnp.exp2((raw[:, :ROWS] - top_low) * TO_EXP2), jnp.exp2((raw[:, ROWS:] - top_high) * TO_EXP2)], axis=1
            ).astype(jnp.bfloat16)
            mixed = dot_nn(weights, value_s[g])
            total = mixed[:, 128:]
            context = (mixed[:, :128] / total).astype(jnp.bfloat16)
            ctx_v[:, c] = jnp.concatenate([context[:ROWS], context[ROWS:]], axis=1)
            level = jnp.where(lane < HEAD, top_low, top_high) + jnp.log2(total) * (1.0 / TO_EXP2)
            first = level.astype(jnp.bfloat16).astype(jnp.float32)
            second = (level - first).astype(jnp.bfloat16).astype(jnp.float32)
            third = level - first - second
            marks = jnp.where(
                spot == 0, first, jnp.where(spot == 1, second, jnp.where(spot == 2, third, seen))
            ).astype(jnp.bfloat16)
            marks_v[:, c] = jnp.concatenate([marks[:ROWS], marks[ROWS:]], axis=1)
            return carry

        lax.fori_loop(0, KVH, group, 0)
        def finish(i, carry):
            c = cols(i * CHUNK, CHUNK)
            out = h_v[:, c].astype(jnp.float32) + dot_nn(ctx_v[...], wo_v[:, c])
            out_v[:, c] = out.astype(jnp.bfloat16)
            return carry

        if not final:
            lax.fori_loop(0, 8, finish, 0)


def bf16(*shape):
    return jax.ShapeDtypeStruct(shape, jnp.bfloat16)


def inside(*arrays):
    return [pltpu.with_memory_space_constraint(array, pltpu.VMEM) for array in arrays]


def v16(*shape):
    return pltpu.VMEM(shape, jnp.bfloat16)


def v32(*shape):
    return pltpu.VMEM(shape, jnp.float32)


def forward_layer(layer, place, hidden, w_qkv, w_out, normed, proj, ctx, kept, marks):
    final = layer == 7
    return pl.pallas_call(
        functools.partial(forward_kernel, final),
        out_shape=(v16(ROWS, D), v16(ROWS, D), v16(ROWS, WCOLS), v16(ROWS, HQ), v16(ROWS, D), v16(ROWS, HQ)),
        in_specs=[SMEM] + [INSIDE] * 8,
        out_specs=(INSIDE,) * 6,
        input_output_aliases={4: 1, 5: 2, 6: 3, 7: 4, 8: 5},
        scratch_shapes=[v16(KVH, 2 * ROWS, 256), v16(KVH, 2 * ROWS, 256)],
        compiler_params=pltpu.CompilerParams(vmem_limit_bytes=VMEM_LIMIT),
        cost_estimate=pl.CostEstimate(flops=3_000_000_000, bytes_accessed=14_000_000, transcendentals=2_000_000),
        name="forward_last" if final else "forward_layer",
    )(place, *inside(hidden, w_qkv, w_out, normed, proj, ctx, kept, marks))


def backward_kernel(
    last, place, u_v, h_v, proj_v, ctx_v, marks_v, wq_v, wo_v, a0, a1,
    up_v, dproj_v, keep_v, dn_v, key_s, value_s, dkt_s, dvt_s,
):
    del a0, a1

    @pl.when(place[0] == 0)
    def _():
        keep_v[...] = u_v[...]
        fill_keys(proj_v[:, HQ : HQ + KV], key_s, place[1])
        fill_values(proj_v[:, HQ + KV :], value_s, -1.0)

        def group(g, carry):
            c = cols(g * CHUNK, CHUNK)
            d_ctx = dot_nt(u_v[...], wo_v[c, :]).astype(jnp.bfloat16)
            queries = stack_pairs(proj_v[:, c])
            d_pairs = stack_pairs(d_ctx)
            left = jnp.concatenate([queries, stack_pairs(marks_v[:, c])], axis=1)
            weights = jnp.exp2(dot_nt(left, key_s[g]) * TO_EXP2)
            inner = d_pairs.astype(jnp.float32) * stack_pairs(ctx_v[:, c]).astype(jnp.float32)
            d_left = jnp.concatenate([d_pairs, inner.astype(jnp.bfloat16)], axis=1)
            d_scores = (weights * dot_nt(d_left, value_s[g])).astype(jnp.bfloat16)
            d_query = (dot_nn(d_scores, key_s[g][:, :128]) * SCALE).astype(jnp.bfloat16)
            dproj_v[:, c] = jnp.concatenate([d_query[:ROWS], d_query[ROWS:]], axis=1)
            d_key = dot_nn(queries.T, d_scores)
            d_value = dot_nn(d_pairs.T, weights.astype(jnp.bfloat16))
            rows = pl.ds(pl.multiple_of(g * HEAD, HEAD), HEAD)
            dkt_s[rows, :] = (d_key[:HEAD, :ROWS] + d_key[HEAD:, ROWS:]) * SCALE
            dvt_s[rows, :] = d_value[:HEAD, :ROWS] + d_value[HEAD:, ROWS:]
            return carry

        lax.fori_loop(0, KVH, group, 0)
        dproj_v[:, HQ : HQ + KV] = dkt_s[...].T.astype(jnp.bfloat16)
        dproj_v[:, HQ + KV :] = dvt_s[...].T.astype(jnp.bfloat16)
        if not last:
            def widen(i, partial):
                c = cols(i * CHUNK, CHUNK)
                d_normed = dot_nt(dproj_v[...], wq_v[c, :])
                dn_v[:, c] = d_normed
                product = d_normed * h_v[:, c].astype(jnp.float32)
                return partial + product[:, :HALF] + product[:, HALF:]

            partial = lax.fori_loop(0, 8, widen, jnp.zeros((ROWS, HALF), jnp.float32))
            mean = jnp.sum(partial, axis=-1, keepdims=True) * (1.0 / D)
            wide = h_v[...].astype(jnp.float32)
            scale = lax.rsqrt(jnp.mean(wide * wide, axis=-1, keepdims=True) + EPS)
            pull = scale * scale * scale * mean

            def previous(i, carry):
                c = cols(i * CHUNK, CHUNK)
                out = u_v[:, c].astype(jnp.float32) + (scale * dn_v[:, c] - h_v[:, c].astype(jnp.float32) * pull)
                up_v[:, c] = out.astype(jnp.bfloat16)
                return carry

            lax.fori_loop(0, 8, previous, 0)


def backward_layer(layer, place, upstream, kept, proj, ctx, marks, w_qkv, w_out, dproj, ups):
    last = layer == 0
    spare = [place, place] if last else inside(kept, w_qkv)
    where = SMEM if last else INSIDE
    return pl.pallas_call(
        functools.partial(backward_kernel, last),
        out_shape=(v16(ROWS, D), v16(ROWS, WCOLS), v16(ROWS, D)),
        in_specs=[SMEM, INSIDE, where, INSIDE, INSIDE, INSIDE, where, INSIDE, INSIDE, INSIDE],
        out_specs=(INSIDE,) * 3,
        input_output_aliases={8: 1, 9: 2},
        scratch_shapes=[
            v32(ROWS, D), v16(KVH, 2 * ROWS, 256), v16(KVH, 2 * ROWS, 256), v32(KV, ROWS), v32(KV, ROWS)
        ],
        compiler_params=pltpu.CompilerParams(vmem_limit_bytes=VMEM_LIMIT),
        cost_estimate=pl.CostEstimate(flops=4_000_000_000, bytes_accessed=15_000_000, transcendentals=2_000_000),
        name="backward_last" if last else "backward_layer",
    )(place, *inside(upstream), spare[0], *inside(proj, ctx, marks), spare[1], *inside(w_out, dproj, ups))


LAYERS = 8
FINE = (("zlo", 2), ("y", 4), ("x", 4), ("zhi", 4), ("core", 2))
NAMES = tuple(name for name, size in FINE)
SIZES = tuple(size for name, size in FINE)
STAGE = ("y", "core")


def regroup(back):
    pairs = []
    for zlo, y, x, zhi, core in np.ndindex(*SIZES):
        source = np.ravel_multi_index((zlo, y, x, zhi, core), SIZES)
        target = np.ravel_multi_index((core, zlo * 2 + y // 2, x, zhi, y % 2), SIZES)
        pairs.append((int(target), int(source)) if back else (int(source), int(target)))
    return pairs


def z_index(z):
    return (z % 2) * 4 + z // 2


def send_x(value, step):
    return lax.ppermute(value, "x", [(i, (i + step) % 4) for i in range(4)])


def send_z(value, step):
    return lax.ppermute(value, ("zlo", "zhi"), [(z_index(i), z_index((i + step) % 8)) for i in range(8)])


def gather_ring(own, count, send):
    below, above = [own], [own]
    for step in range(count // 2 - 1):
        below.append(send(below[-1], 1))
        above.append(send(above[-1], -1))
    half = own.shape[0] // 2
    far = [send(below[-1][:half], 1), send(above[-1][half:], -1)]
    return above + far + below[:0:-1]


def add(own, came):
    return (own.astype(jnp.float32) + came.astype(jnp.float32)).astype(jnp.bfloat16)


def scatter_direct(take, send, steps):
    total = take(0).astype(jnp.float32)
    for came in [send(take(step), step) for step in steps]:
        total = total + came.astype(jnp.float32)
    return total.astype(jnp.bfloat16)


def gather_direct(own, send):
    far, above, below = send(own, 2), send(own, -1), send(own, 1)
    return [own, above, far, below]


def taker(value, spots, axis, split):
    def take(d, half=None):
        spot = spots[d % len(spots)]
        start, size = [0] * value.ndim, list(value.shape)
        start[axis], size[axis] = spot, 1
        if half is not None:
            size[split] //= 2
            start[split] = half * size[split]
        block = lax.dynamic_slice(value, start, size, allow_negative_indices=False)
        return block.reshape([n for dim, n in enumerate(size) if dim != axis])

    return take


def assemble_kernel(place, *refs):
    qkv_parts, out_parts, (full_qkv, full_out, sems) = refs[:5], refs[5:14], refs[14:]
    x, z = place[0], place[1]
    copies = []
    for ref, dx, first, pieces in zip(qkv_parts, (0, 1, 2, 2, 3), (0, 0, 0, 4, 0), (8, 8, 4, 4, 8)):
        for i in range(pieces):
            row = (lax.rem(x + dx, 4) * 8 + lax.rem(z + first + i, 8)) * 64
            target = full_qkv.at[pl.ds(pl.multiple_of(row, 64), 64), :]
            copies.append(pltpu.make_async_copy(ref.at[pl.ds(i * 64, 64), :], target, sems.at[len(copies)]))
    for ref, dz, first, pieces in zip(
        out_parts, (0, 1, 2, 3, 4, 4, 5, 6, 7), (0, 0, 0, 0, 0, 2, 0, 0, 0), (4, 4, 4, 4, 2, 2, 4, 4, 4)
    ):
        for i in range(pieces):
            row = (lax.rem(x + first + i, 4) * 8 + lax.rem(z + dz, 8)) * 32
            target = full_out.at[pl.ds(pl.multiple_of(row, 32), 32), :]
            copies.append(pltpu.make_async_copy(ref.at[pl.ds(i * 32, 32), :], target, sems.at[len(copies)]))
    for copy in copies:
        copy.start()
    for copy in copies:
        copy.wait()


def gather_weights(near, far, x, z):
    column = jnp.concatenate(gather_ring(near, 8, send_z))
    row = jnp.concatenate(gather_direct(far, send_x))
    qkv_parts = gather_ring(column, 4, send_x)
    out_parts = gather_ring(row, 8, send_z)
    return pl.pallas_call(
        assemble_kernel,
        out_shape=(v16(D, WCOLS), v16(HQ, D)),
        in_specs=[SMEM] + [ANY] * 14,
        out_specs=(INSIDE, INSIDE),
        scratch_shapes=[pltpu.SemaphoreType.DMA((64,))],
        compiler_params=pltpu.CompilerParams(vmem_limit_bytes=4 * 1024 * 1024),
        cost_estimate=pl.CostEstimate(flops=0, bytes_accessed=21_000_000, transcendentals=0),
        name="assemble",
    )(jnp.stack([x, z]), *qkv_parts, *out_parts)


def sum_of(*terms):
    return sum(term.astype(jnp.float32) for term in terms).astype(jnp.bfloat16)


def scatter_start(part_out, spins):
    take = taker(part_out.reshape(4, 8, 32, D), spins, 1, 0)
    return take, send_z(take(4, 0), 1), send_z(take(4, 1), -1)


def scatter_both(part_qkv, started, turns, spins):
    take_z, up_z, down_z = started
    take_x = taker(part_qkv.reshape(4, 512, WCOLS), turns, 0, 1)
    up_x, down_x = send_x(take_x(2, 0), 1), send_x(take_x(2, 1), -1)
    out_up = jnp.concatenate([add(take_z(3, 0), up_z), take_z(3, 1)])
    out_down = jnp.concatenate([take_z(-3, 0), add(take_z(-3, 1), down_z)])
    up_z, down_z = send_z(out_up, 1), send_z(out_down, -1)
    qkv_up = jnp.concatenate([add(take_x(1, 0), up_x), take_x(1, 1)])
    qkv_down = jnp.concatenate([take_x(-1, 0), add(take_x(-1, 1), down_x)])
    out_up, out_down = add(take_z(2), up_z), add(take_z(-2), down_z)
    qkv_up, qkv_down, out_up, out_down = lax.optimization_barrier((qkv_up, qkv_down, out_up, out_down))
    up_x, down_x = send_x(qkv_up, 1), send_x(qkv_down, -1)
    up_z, down_z = send_z(out_up, 1), send_z(out_down, -1)
    up_z, down_z = send_z(add(take_z(1), up_z), 1), send_z(add(take_z(-1), down_z), -1)
    mine_out = sum_of(take_z(0), up_z, down_z)
    mine_qkv = sum_of(take_x(0), up_x, down_x)
    grad_out = scatter_direct(taker(mine_out, turns, 0, 1), send_x, (2, 1, -1))
    grad_qkv = scatter_direct(
        taker(mine_qkv.reshape(8, 64, WCOLS), spins, 0, 1), send_z, (4, 3, -3, 2, -2, 1, -1)
    )
    return grad_qkv, grad_out


def on_device(inputs, cotangent, joined, w_qkv, w_out):
    micro = lax.axis_index("zlo")
    stage = 2 * lax.axis_index("y") + lax.axis_index("core")
    x_index = lax.axis_index("x")
    z_place = 2 * lax.axis_index("zhi") + micro
    bin_index = 4 * x_index + lax.axis_index("zhi")
    flag = joined[micro, bin_index]
    near = lax.ppermute(w_qkv[0], NAMES, regroup(False))
    far = lax.ppermute(w_out[0], NAMES, regroup(False))
    full_qkv, full_out = gather_weights(near, far, x_index, z_place)
    block = lax.dynamic_index_in_dim(inputs, micro, 0, keepdims=False)
    hidden = jnp.concatenate([block, lax.ppermute(block, "core", [(1, 0)])])
    block = lax.dynamic_index_in_dim(cotangent, micro, 0, keepdims=False)
    upstream = jnp.concatenate([lax.ppermute(block, "core", [(0, 1)]), block])

    places = [jnp.stack([stage - layer, flag]) for layer in range(LAYERS)]
    turns = [((x_index + d) % 4) for d in range(4)]
    spins = [((z_place + d) % 8) for d in range(8)]
    places, turns, spins = lax.optimization_barrier((places, turns, spins))
    normed = jnp.zeros((ROWS, D), jnp.bfloat16)
    kept = jnp.zeros((ROWS, D), jnp.bfloat16)
    proj = jnp.zeros((ROWS, WCOLS), jnp.bfloat16)
    ctx = jnp.zeros((ROWS, HQ), jnp.bfloat16)
    marks = jnp.zeros((ROWS, HQ), jnp.bfloat16)
    for layer in range(LAYERS):
        result, normed, proj, ctx, kept, marks = forward_layer(
            layer, places[layer], hidden, full_qkv, full_out, normed, proj, ctx, kept, marks
        )
        if layer < LAYERS - 1:
            hidden = lax.ppermute(result, STAGE, [(layer, layer + 1)])
    dproj = jnp.zeros((ROWS, WCOLS), jnp.bfloat16)
    ups = jnp.zeros((ROWS, D), jnp.bfloat16)
    contract = (((0,), (0,)), ((), ()))
    for layer in reversed(range(LAYERS)):
        if layer == 0:
            arrived = jnp.where(stage == 0, upstream, ups)
            part_out = lax.dot_general(ctx, arrived, contract, preferred_element_type=jnp.float32).astype(jnp.bfloat16)
            part_out, upstream = lax.optimization_barrier((part_out, upstream))
            started = scatter_start(part_out, spins)
        result, dproj, ups = backward_layer(
            layer, places[layer], upstream, kept, proj, ctx, marks, full_qkv, full_out, dproj, ups
        )
        if layer:
            upstream = lax.ppermute(result, STAGE, [(layer, layer - 1)])
    part_qkv = lax.dot_general(normed, dproj, contract, preferred_element_type=jnp.float32).astype(jnp.bfloat16)
    grad_qkv, grad_out = scatter_both(part_qkv, started, turns, spins)
    grad_out = lax.ppermute(grad_out, NAMES, regroup(True)).astype(jnp.float32)
    grad_qkv = lax.ppermute(grad_qkv, NAMES, regroup(True)).astype(jnp.float32)
    return (grad_qkv[None], grad_out[None])


def solution(mesh):
    fine = jax.sharding.Mesh(mesh.devices.reshape(SIZES), NAMES)
    token = P(None, ("x", "zhi", "core"), None)
    weight = P(("zlo", "y"), ("x", "zhi", "core"), None)
    return jax.shard_map(
        on_device,
        mesh=fine,
        in_specs=(token, token, P(), weight, weight),
        out_specs=(weight, weight),
        check_vma=False,
    )
```

```python
import functools
import math

import jax
import jax.numpy as jnp
import numpy as np
from jax import lax
from jax.experimental import pallas as pl
from jax.experimental.pallas import tpu as pltpu
from jax.sharding import PartitionSpec as P

HEADS = 16
HEAD = 64
KVH = 4
GROUP = HEADS // KVH
ROWS = 256
HALF = 128
D = 2048
HQ = HEADS * HEAD
KV = KVH * HEAD
WCOLS = HQ + 2 * KV
CHUNK = 256
EPS = 1e-5
SCALE = 1.0 / math.sqrt(HEAD)
TO_EXP2 = SCALE * math.log2(math.e)
NT = (((1,), (1,)), ((), ()))
VMEM_LIMIT = 16 * 1024 * 1024
ANY = pl.BlockSpec(memory_space=pl.ANY)
SMEM = pl.BlockSpec(memory_space=pltpu.SMEM)
INSIDE = pl.BlockSpec(memory_space=pltpu.VMEM)


def dot_nt(left, right):
    return lax.dot_general(left, right, NT, preferred_element_type=jnp.float32)


def dot_nn(left, right):
    return jnp.dot(left, right, preferred_element_type=jnp.float32)


def cols(start, size):
    return pl.ds(pl.multiple_of(start, size), size)


def packed_halves(tile, upper):
    lane = lax.broadcasted_iota(jnp.int32, tile.shape, 1)
    wide = tile.astype(jnp.float32)
    kept = jnp.where((lane >= HEAD) == upper, wide, 0.0)
    turned = pltpu.roll(kept, HEAD, 1)
    low, high = (turned, kept) if upper else (kept, turned)
    return low.astype(jnp.bfloat16), high.astype(jnp.bfloat16)


def fill_keys(keys, key_s, joined):
    row = lax.broadcasted_iota(jnp.int32, (ROWS, 2 * HEAD), 0)
    lane = lax.broadcasted_iota(jnp.int32, (ROWS, 2 * HEAD), 1)
    hidden = jnp.where(joined > 0, 0.0, -1e30)
    other = jnp.logical_or(
        jnp.logical_and(lane == 3, row >= HALF), jnp.logical_and(lane == 4, row < HALF)
    )
    apart = jnp.where(other, hidden, 0.0)
    low_marks = jnp.where(lane < 3, -1.0, apart).astype(jnp.bfloat16)
    high_marks = jnp.where(jnp.logical_and(lane >= HEAD, lane < HEAD + 3), -1.0, apart).astype(jnp.bfloat16)
    for g in range(KVH):
        low, high = packed_halves(keys[:, g // 2 * 128 : g // 2 * 128 + 128], g % 2 == 1)
        key_s[g, :ROWS, :128] = low
        key_s[g, ROWS:, :128] = high
        key_s[g, :ROWS, 128:] = low_marks
        key_s[g, ROWS:, 128:] = high_marks


def fill_values(values, value_s, mark):
    lane = lax.broadcasted_iota(jnp.int32, (ROWS, 2 * HEAD), 1)
    low_marks = jnp.where(lane < HEAD, mark, 0.0).astype(jnp.bfloat16)
    high_marks = jnp.where(lane >= HEAD, mark, 0.0).astype(jnp.bfloat16)
    for g in range(KVH):
        low, high = packed_halves(values[:, g // 2 * 128 : g // 2 * 128 + 128], g % 2 == 1)
        value_s[g, :ROWS, :128] = low
        value_s[g, ROWS:, :128] = high
        value_s[g, :ROWS, 128:] = low_marks
        value_s[g, ROWS:, 128:] = high_marks


def stack_pairs(value):
    return jnp.concatenate([value[:, :128], value[:, 128:]], axis=0)


def forward_kernel(
    final, place, h_v, wq_v, wo_v, a0, a1, a2, a3, a4,
    out_v, normed_v, proj_v, ctx_v, keep_v, marks_v, key_s, value_s,
):
    del a0, a1, a2, a3, a4

    @pl.when(place[0] == 0)
    def _():
        block = (lax.broadcasted_iota(jnp.int32, (2 * ROWS, 128), 0) // HALF) % 2
        lane = lax.broadcasted_iota(jnp.int32, (2 * ROWS, 128), 1)
        spot = lane % HEAD
        seen = jnp.where(jnp.logical_or(jnp.logical_and(lane == 3, block == 0), jnp.logical_and(lane == 4, block == 1)), 1.0, 0.0)
        keep_v[...] = h_v[...]
        wide = h_v[...].astype(jnp.float32)
        scale = lax.rsqrt(jnp.mean(wide * wide, axis=-1, keepdims=True) + EPS)
        normed_v[...] = (wide * scale).astype(jnp.bfloat16)
        both = dot_nn(normed_v[...], wq_v[:, HQ:]).astype(jnp.bfloat16)
        proj_v[:, HQ:] = both
        fill_keys(both[:, :KV], key_s, place[1])
        fill_values(both[:, KV:], value_s, 1.0)

        def group(g, carry):
            c = cols(g * CHUNK, CHUNK)
            queries = dot_nn(normed_v[...], wq_v[:, c]).astype(jnp.bfloat16)
            proj_v[:, c] = queries
            left = jnp.concatenate([stack_pairs(queries), seen.astype(jnp.bfloat16)], axis=1)
            raw = dot_nt(left, key_s[g])
            top_low = jnp.max(raw[:, :ROWS], axis=1, keepdims=True)
            top_high = jnp.max(raw[:, ROWS:], axis=1, keepdims=True)
            weights = jnp.concatenate(
                [jnp.exp2((raw[:, :ROWS] - top_low) * TO_EXP2), jnp.exp2((raw[:, ROWS:] - top_high) * TO_EXP2)], axis=1
            ).astype(jnp.bfloat16)
            mixed = dot_nn(weights, value_s[g])
            total = mixed[:, 128:]
            context = (mixed[:, :128] / total).astype(jnp.bfloat16)
            ctx_v[:, c] = jnp.concatenate([context[:ROWS], context[ROWS:]], axis=1)
            level = jnp.where(lane < HEAD, top_low, top_high) + jnp.log2(total) * (1.0 / TO_EXP2)
            first = level.astype(jnp.bfloat16).astype(jnp.float32)
            second = (level - first).astype(jnp.bfloat16).astype(jnp.float32)
            third = level - first - second
            marks = jnp.where(
                spot == 0, first, jnp.where(spot == 1, second, jnp.where(spot == 2, third, seen))
            ).astype(jnp.bfloat16)
            marks_v[:, c] = jnp.concatenate([marks[:ROWS], marks[ROWS:]], axis=1)
            return carry

        lax.fori_loop(0, KVH, group, 0, unroll=2)
        def finish(i, carry):
            c = cols(i * CHUNK, CHUNK)
            out = h_v[:, c].astype(jnp.float32) + dot_nn(ctx_v[...], wo_v[:, c])
            out_v[:, c] = out.astype(jnp.bfloat16)
            return carry

        if not final:
            lax.fori_loop(0, 8, finish, 0, unroll=True)


def bf16(*shape):
    return jax.ShapeDtypeStruct(shape, jnp.bfloat16)


def inside(*arrays):
    return [pltpu.with_memory_space_constraint(array, pltpu.VMEM) for array in arrays]


def v16(*shape):
    return pltpu.VMEM(shape, jnp.bfloat16)


def v32(*shape):
    return pltpu.VMEM(shape, jnp.float32)


def forward_layer(layer, place, hidden, w_qkv, w_out, normed, proj, ctx, kept, marks):
    final = layer == 7
    return pl.pallas_call(
        functools.partial(forward_kernel, final),
        out_shape=(v16(ROWS, D), v16(ROWS, D), v16(ROWS, WCOLS), v16(ROWS, HQ), v16(ROWS, D), v16(ROWS, HQ)),
        in_specs=[SMEM] + [INSIDE] * 8,
        out_specs=(INSIDE,) * 6,
        input_output_aliases={4: 1, 5: 2, 6: 3, 7: 4, 8: 5},
        scratch_shapes=[v16(KVH, 2 * ROWS, 256), v16(KVH, 2 * ROWS, 256)],
        compiler_params=pltpu.CompilerParams(vmem_limit_bytes=VMEM_LIMIT),
        cost_estimate=pl.CostEstimate(flops=3_000_000_000, bytes_accessed=14_000_000, transcendentals=2_000_000),
        name="forward_last" if final else "forward_layer",
    )(place, *inside(hidden, w_qkv, w_out, normed, proj, ctx, kept, marks))


def backward_kernel(
    last, place, u_v, h_v, proj_v, ctx_v, marks_v, wq_v, wo_v, a0, a1,
    up_v, dproj_v, keep_v, dn_v, key_s, value_s, dkt_s, dvt_s,
):
    del a0, a1

    @pl.when(place[0] == 0)
    def _():
        keep_v[...] = u_v[...]
        fill_keys(proj_v[:, HQ : HQ + KV], key_s, place[1])
        fill_values(proj_v[:, HQ + KV :], value_s, -1.0)

        def group(g, carry):
            c = cols(g * CHUNK, CHUNK)
            d_ctx = dot_nt(u_v[...], wo_v[c, :]).astype(jnp.bfloat16)
            queries = stack_pairs(proj_v[:, c])
            d_pairs = stack_pairs(d_ctx)
            left = jnp.concatenate([queries, stack_pairs(marks_v[:, c])], axis=1)
            weights = jnp.exp2(dot_nt(left, key_s[g]) * TO_EXP2)
            inner = d_pairs.astype(jnp.float32) * stack_pairs(ctx_v[:, c]).astype(jnp.float32)
            d_left = jnp.concatenate([d_pairs, inner.astype(jnp.bfloat16)], axis=1)
            d_scores = (weights * dot_nt(d_left, value_s[g])).astype(jnp.bfloat16)
            d_query = (dot_nn(d_scores, key_s[g][:, :128]) * SCALE).astype(jnp.bfloat16)
            dproj_v[:, c] = jnp.concatenate([d_query[:ROWS], d_query[ROWS:]], axis=1)
            d_key = dot_nn(queries.T, d_scores)
            d_value = dot_nn(d_pairs.T, weights.astype(jnp.bfloat16))
            rows = pl.ds(pl.multiple_of(g * HEAD, HEAD), HEAD)
            dkt_s[rows, :] = (d_key[:HEAD, :ROWS] + d_key[HEAD:, ROWS:]) * SCALE
            dvt_s[rows, :] = d_value[:HEAD, :ROWS] + d_value[HEAD:, ROWS:]
            return carry

        lax.fori_loop(0, KVH, group, 0, unroll=2)
        dproj_v[:, HQ : HQ + KV] = dkt_s[...].T.astype(jnp.bfloat16)
        dproj_v[:, HQ + KV :] = dvt_s[...].T.astype(jnp.bfloat16)
        if not last:
            def widen(i, partial):
                c = cols(i * CHUNK, CHUNK)
                d_normed = dot_nt(dproj_v[...], wq_v[c, :])
                dn_v[:, c] = d_normed
                product = d_normed * h_v[:, c].astype(jnp.float32)
                return partial + product[:, :HALF] + product[:, HALF:]

            partial = lax.fori_loop(0, 8, widen, jnp.zeros((ROWS, HALF), jnp.float32), unroll=True)
            mean = jnp.sum(partial, axis=-1, keepdims=True) * (1.0 / D)
            wide = h_v[...].astype(jnp.float32)
            scale = lax.rsqrt(jnp.mean(wide * wide, axis=-1, keepdims=True) + EPS)
            pull = scale * scale * scale * mean

            def previous(i, carry):
                c = cols(i * CHUNK, CHUNK)
                out = u_v[:, c].astype(jnp.float32) + (scale * dn_v[:, c] - h_v[:, c].astype(jnp.float32) * pull)
                up_v[:, c] = out.astype(jnp.bfloat16)
                return carry

            lax.fori_loop(0, 8, previous, 0, unroll=True)


def backward_layer(layer, place, upstream, kept, proj, ctx, marks, w_qkv, w_out, dproj, ups):
    last = layer == 0
    spare = [place, place] if last else inside(kept, w_qkv)
    where = SMEM if last else INSIDE
    return pl.pallas_call(
        functools.partial(backward_kernel, last),
        out_shape=(v16(ROWS, D), v16(ROWS, WCOLS), v16(ROWS, D)),
        in_specs=[SMEM, INSIDE, where, INSIDE, INSIDE, INSIDE, where, INSIDE, INSIDE, INSIDE],
        out_specs=(INSIDE,) * 3,
        input_output_aliases={8: 1, 9: 2},
        scratch_shapes=[
            v32(ROWS, D), v16(KVH, 2 * ROWS, 256), v16(KVH, 2 * ROWS, 256), v32(KV, ROWS), v32(KV, ROWS)
        ],
        compiler_params=pltpu.CompilerParams(vmem_limit_bytes=VMEM_LIMIT),
        cost_estimate=pl.CostEstimate(flops=4_000_000_000, bytes_accessed=15_000_000, transcendentals=2_000_000),
        name="backward_last" if last else "backward_layer",
    )(place, *inside(upstream), spare[0], *inside(proj, ctx, marks), spare[1], *inside(w_out, dproj, ups))


LAYERS = 8
FINE = (("zlo", 2), ("y", 4), ("x", 4), ("zhi", 4), ("core", 2))
NAMES = tuple(name for name, size in FINE)
SIZES = tuple(size for name, size in FINE)
STAGE = ("y", "core")


def regroup(back):
    pairs = []
    for zlo, y, x, zhi, core in np.ndindex(*SIZES):
        source = np.ravel_multi_index((zlo, y, x, zhi, core), SIZES)
        target = np.ravel_multi_index((core, zlo * 2 + y // 2, x, zhi, y % 2), SIZES)
        pairs.append((int(target), int(source)) if back else (int(source), int(target)))
    return pairs


def z_index(z):
    return (z % 2) * 4 + z // 2


def send_x(value, step):
    return lax.ppermute(value, "x", [(i, (i + step) % 4) for i in range(4)])


def send_z(value, step):
    return lax.ppermute(value, ("zlo", "zhi"), [(z_index(i), z_index((i + step) % 8)) for i in range(8)])


def gather_ring(own, count, send):
    below, above = [own], [own]
    for step in range(count // 2 - 1):
        below.append(send(below[-1], 1))
        above.append(send(above[-1], -1))
    half = own.shape[0] // 2
    far = [send(below[-1][:half], 1), send(above[-1][half:], -1)]
    return above + far + below[:0:-1]


def add(own, came):
    return (own.astype(jnp.float32) + came.astype(jnp.float32)).astype(jnp.bfloat16)


def scatter_direct(take, send, steps):
    total = take(0).astype(jnp.float32)
    for came in [send(take(step), step) for step in steps]:
        total = total + came.astype(jnp.float32)
    return total.astype(jnp.bfloat16)


def gather_direct(own, send):
    far, above, below = send(own, 2), send(own, -1), send(own, 1)
    return [own, above, far, below]


def taker(value, spots, axis, split):
    def take(d, half=None):
        spot = spots[d % len(spots)]
        start, size = [0] * value.ndim, list(value.shape)
        start[axis], size[axis] = spot, 1
        if half is not None:
            size[split] //= 2
            start[split] = half * size[split]
        block = lax.dynamic_slice(value, start, size, allow_negative_indices=False)
        return block.reshape([n for dim, n in enumerate(size) if dim != axis])

    return take


def assemble_kernel(qkv_plan, out_plan, place, *refs):
    count = len(qkv_plan) + len(out_plan)
    parts, (full_qkv, full_out, sems) = refs[:count], refs[-3:]
    x, z = place[0], place[1]
    copies = []
    for ref, (dx, first, pieces) in zip(parts, qkv_plan):
        for i in range(pieces):
            row = (lax.rem(x + dx, 4) * 8 + lax.rem(z + first + i, 8)) * 64
            target = full_qkv.at[pl.ds(pl.multiple_of(row, 64), 64), :]
            copies.append(pltpu.make_async_copy(ref.at[pl.ds(i * 64, 64), :], target, sems.at[len(copies)]))
    for ref, (dz, first, pieces) in zip(parts[len(qkv_plan) :], out_plan):
        for i in range(pieces):
            row = (lax.rem(x + first + i, 4) * 8 + lax.rem(z + dz, 8)) * 32
            target = full_out.at[pl.ds(pl.multiple_of(row, 32), 32), :]
            copies.append(pltpu.make_async_copy(ref.at[pl.ds(i * 32, 32), :], target, sems.at[len(copies)]))
    for copy in copies:
        copy.start()
    for copy in copies:
        copy.wait()


def assemble(place, qkv, out, before):
    qkv_plan, out_plan = [plan for plan, part in qkv], [plan for plan, part in out]
    count = len(qkv) + len(out)
    return pl.pallas_call(
        functools.partial(assemble_kernel, qkv_plan, out_plan),
        out_shape=(v16(D, WCOLS), v16(HQ, D)),
        in_specs=[SMEM] + [ANY] * count + [INSIDE] * len(before),
        out_specs=(INSIDE, INSIDE),
        input_output_aliases={count + 1: 0, count + 2: 1} if before else {},
        scratch_shapes=[pltpu.SemaphoreType.DMA((64,))],
        compiler_params=pltpu.CompilerParams(vmem_limit_bytes=4 * 1024 * 1024),
        cost_estimate=pl.CostEstimate(flops=0, bytes_accessed=6_000_000 if before else 18_000_000, transcendentals=0),
        name="assemble_rest" if before else "assemble",
    )(place, *[part for plan, part in qkv], *[part for plan, part in out], *inside(*before))


def gather_weights(near, far, x, z):
    column = jnp.concatenate(gather_ring(near, 8, send_z))
    row = jnp.concatenate(gather_direct(far, send_x))
    qkv_parts = gather_ring(column, 4, send_x)
    out_parts = gather_ring(row, 8, send_z)
    qkv = list(zip([(0, 0, 8), (1, 0, 8), (2, 0, 4), (2, 4, 4), (3, 0, 8)], qkv_parts))
    spots = [(0, 0, 4), (1, 0, 4), (2, 0, 4), (3, 0, 4), (4, 0, 2), (4, 2, 2), (5, 0, 4), (6, 0, 4), (7, 0, 4)]
    out = list(zip(spots, out_parts))
    place = jnp.stack([x, z])
    early = assemble(place, [qkv[0], qkv[1], qkv[4]], out[:3] + out[7:], ())
    return assemble(place, qkv[2:4], out[3:7], early)


def sum_of(*terms):
    return sum(term.astype(jnp.float32) for term in terms).astype(jnp.bfloat16)


def scatter_start(part_out, spins):
    take = taker(part_out.reshape(4, 8, 32, D), spins, 1, 0)
    return take, send_z(take(4, 0), 1), send_z(take(4, 1), -1)


def scatter_both(part_qkv, started, turns, spins):
    take_z, up_z, down_z = started
    take_x = taker(part_qkv.reshape(4, 512, WCOLS), turns, 0, 1)
    up_x, down_x = send_x(take_x(2, 0), 1), send_x(take_x(2, 1), -1)
    out_up = jnp.concatenate([add(take_z(3, 0), up_z), take_z(3, 1)])
    out_down = jnp.concatenate([take_z(-3, 0), add(take_z(-3, 1), down_z)])
    up_z, down_z = send_z(out_up, 1), send_z(out_down, -1)
    qkv_up = jnp.concatenate([add(take_x(1, 0), up_x), take_x(1, 1)])
    qkv_down = jnp.concatenate([take_x(-1, 0), add(take_x(-1, 1), down_x)])
    out_up, out_down = add(take_z(2), up_z), add(take_z(-2), down_z)
    qkv_up, qkv_down, out_up, out_down = lax.optimization_barrier((qkv_up, qkv_down, out_up, out_down))
    up_x, down_x = send_x(qkv_up, 1), send_x(qkv_down, -1)
    up_z, down_z = send_z(out_up, 1), send_z(out_down, -1)
    up_z, down_z = send_z(add(take_z(1), up_z), 1), send_z(add(take_z(-1), down_z), -1)
    mine_out = sum_of(take_z(0), up_z, down_z)
    mine_qkv = sum_of(take_x(0), up_x, down_x)
    grad_out = scatter_direct(taker(mine_out, turns, 0, 1), send_x, (2, 1, -1))
    grad_qkv = scatter_direct(
        taker(mine_qkv.reshape(8, 64, WCOLS), spins, 0, 1), send_z, (4, 3, -3, 2, -2, 1, -1)
    )
    return grad_qkv, grad_out


def on_device(inputs, cotangent, joined, w_qkv, w_out):
    micro = lax.axis_index("zlo")
    stage = 2 * lax.axis_index("y") + lax.axis_index("core")
    x_index = lax.axis_index("x")
    z_place = 2 * lax.axis_index("zhi") + micro
    bin_index = 4 * x_index + lax.axis_index("zhi")
    flag = joined[micro, bin_index]
    near = lax.ppermute(w_qkv[0], NAMES, regroup(False))
    far = lax.ppermute(w_out[0], NAMES, regroup(False))
    full_qkv, full_out = gather_weights(near, far, x_index, z_place)
    block = lax.dynamic_index_in_dim(inputs, micro, 0, keepdims=False)
    hidden = jnp.concatenate([block, lax.ppermute(block, "core", [(1, 0)])])
    block = lax.dynamic_index_in_dim(cotangent, micro, 0, keepdims=False)
    upstream = jnp.concatenate([lax.ppermute(block, "core", [(0, 1)]), block])

    places = [jnp.stack([stage - layer, flag]) for layer in range(LAYERS)]
    turns = [((x_index + d) % 4) for d in range(4)]
    spins = [((z_place + d) % 8) for d in range(8)]
    places, turns, spins = lax.optimization_barrier((places, turns, spins))
    normed = jnp.zeros((ROWS, D), jnp.bfloat16)
    kept = jnp.zeros((ROWS, D), jnp.bfloat16)
    proj = jnp.zeros((ROWS, WCOLS), jnp.bfloat16)
    ctx = jnp.zeros((ROWS, HQ), jnp.bfloat16)
    marks = jnp.zeros((ROWS, HQ), jnp.bfloat16)
    for layer in range(LAYERS):
        result, normed, proj, ctx, kept, marks = forward_layer(
            layer, places[layer], hidden, full_qkv, full_out, normed, proj, ctx, kept, marks
        )
        if layer < LAYERS - 1:
            hidden = lax.ppermute(result, STAGE, [(layer, layer + 1)])
    dproj = jnp.zeros((ROWS, WCOLS), jnp.bfloat16)
    ups = jnp.zeros((ROWS, D), jnp.bfloat16)
    contract = (((0,), (0,)), ((), ()))
    for layer in reversed(range(LAYERS)):
        if layer == 0:
            arrived = jnp.where(stage == 0, upstream, ups)
            part_out = lax.dot_general(ctx, arrived, contract, preferred_element_type=jnp.float32).astype(jnp.bfloat16)
            part_out, upstream = lax.optimization_barrier((part_out, upstream))
            started = scatter_start(part_out, spins)
        result, dproj, ups = backward_layer(
            layer, places[layer], upstream, kept, proj, ctx, marks, full_qkv, full_out, dproj, ups
        )
        if layer:
            upstream = lax.ppermute(result, STAGE, [(layer, layer - 1)])
    part_qkv = lax.dot_general(normed, dproj, contract, preferred_element_type=jnp.float32).astype(jnp.bfloat16)
    grad_qkv, grad_out = scatter_both(part_qkv, started, turns, spins)
    grad_out = lax.ppermute(grad_out, NAMES, regroup(True)).astype(jnp.float32)
    grad_qkv = lax.ppermute(grad_qkv, NAMES, regroup(True)).astype(jnp.float32)
    return (grad_qkv[None], grad_out[None])


def solution(mesh):
    fine = jax.sharding.Mesh(mesh.devices.reshape(SIZES), NAMES)
    token = P(None, ("x", "zhi", "core"), None)
    weight = P(("zlo", "y"), ("x", "zhi", "core"), None)
    return jax.shard_map(
        on_device,
        mesh=fine,
        in_specs=(token, token, P(), weight, weight),
        out_specs=(weight, weight),
        check_vma=False,
    )
```

```python
import functools
import math

import jax
import jax.numpy as jnp
import numpy as np
from jax import lax
from jax.experimental import pallas as pl
from jax.experimental.pallas import tpu as pltpu
from jax.sharding import PartitionSpec as P

HEADS = 16
HEAD = 64
KVH = 4
GROUP = HEADS // KVH
ROWS = 256
HALF = 128
D = 2048
HQ = HEADS * HEAD
KV = KVH * HEAD
WCOLS = HQ + 2 * KV
CHUNK = 256
EPS = 1e-5
SCALE = 1.0 / math.sqrt(HEAD)
TO_EXP2 = SCALE * math.log2(math.e)
NT = (((1,), (1,)), ((), ()))
VMEM_LIMIT = 16 * 1024 * 1024
ANY = pl.BlockSpec(memory_space=pl.ANY)
SMEM = pl.BlockSpec(memory_space=pltpu.SMEM)
INSIDE = pl.BlockSpec(memory_space=pltpu.VMEM)


def dot_nt(left, right):
    return lax.dot_general(left, right, NT, preferred_element_type=jnp.float32)


def dot_nn(left, right):
    return jnp.dot(left, right, preferred_element_type=jnp.float32)


def cols(start, size):
    return pl.ds(pl.multiple_of(start, size), size)


def packed_halves(tile, upper):
    lane = lax.broadcasted_iota(jnp.int32, tile.shape, 1)
    wide = tile.astype(jnp.float32)
    kept = jnp.where((lane >= HEAD) == upper, wide, 0.0)
    turned = pltpu.roll(kept, HEAD, 1)
    low, high = (turned, kept) if upper else (kept, turned)
    return low.astype(jnp.bfloat16), high.astype(jnp.bfloat16)


def fill_keys(keys, key_s, joined):
    row = lax.broadcasted_iota(jnp.int32, (ROWS, 2 * HEAD), 0)
    lane = lax.broadcasted_iota(jnp.int32, (ROWS, 2 * HEAD), 1)
    hidden = jnp.where(joined > 0, 0.0, -1e30)
    other = jnp.logical_or(
        jnp.logical_and(lane == 3, row >= HALF), jnp.logical_and(lane == 4, row < HALF)
    )
    apart = jnp.where(other, hidden, 0.0)
    low_marks = jnp.where(lane < 3, -1.0, apart).astype(jnp.bfloat16)
    high_marks = jnp.where(jnp.logical_and(lane >= HEAD, lane < HEAD + 3), -1.0, apart).astype(jnp.bfloat16)
    for g in range(KVH):
        low, high = packed_halves(keys[:, g // 2 * 128 : g // 2 * 128 + 128], g % 2 == 1)
        key_s[g, :ROWS, :128] = low
        key_s[g, ROWS:, :128] = high
        key_s[g, :ROWS, 128:] = low_marks
        key_s[g, ROWS:, 128:] = high_marks


def fill_values(values, value_s, mark):
    lane = lax.broadcasted_iota(jnp.int32, (ROWS, 2 * HEAD), 1)
    low_marks = jnp.where(lane < HEAD, mark, 0.0).astype(jnp.bfloat16)
    high_marks = jnp.where(lane >= HEAD, mark, 0.0).astype(jnp.bfloat16)
    for g in range(KVH):
        low, high = packed_halves(values[:, g // 2 * 128 : g // 2 * 128 + 128], g % 2 == 1)
        value_s[g, :ROWS, :128] = low
        value_s[g, ROWS:, :128] = high
        value_s[g, :ROWS, 128:] = low_marks
        value_s[g, ROWS:, 128:] = high_marks


def stack_pairs(value):
    return jnp.concatenate([value[:, :128], value[:, 128:]], axis=0)


def forward_kernel(
    final, place, h_v, wq_v, wo_v, a0, a1, a2, a3, a4,
    out_v, normed_v, proj_v, ctx_v, keep_v, marks_v, key_s, value_s,
):
    del a0, a1, a2, a3, a4

    @pl.when(place[0] == 0)
    def _():
        block = (lax.broadcasted_iota(jnp.int32, (2 * ROWS, 128), 0) // HALF) % 2
        lane = lax.broadcasted_iota(jnp.int32, (2 * ROWS, 128), 1)
        spot = lane % HEAD
        seen = jnp.where(jnp.logical_or(jnp.logical_and(lane == 3, block == 0), jnp.logical_and(lane == 4, block == 1)), 1.0, 0.0)
        keep_v[...] = h_v[...]
        wide = h_v[...].astype(jnp.float32)
        scale = lax.rsqrt(jnp.mean(wide * wide, axis=-1, keepdims=True) + EPS)
        normed_v[...] = (wide * scale).astype(jnp.bfloat16)
        both = dot_nn(normed_v[...], wq_v[:, HQ:]).astype(jnp.bfloat16)
        proj_v[:, HQ:] = both
        fill_keys(both[:, :KV], key_s, place[1])
        fill_values(both[:, KV:], value_s, 1.0)

        def group(g, carry):
            c = cols(g * CHUNK, CHUNK)
            queries = dot_nn(normed_v[...], wq_v[:, c]).astype(jnp.bfloat16)
            proj_v[:, c] = queries
            left = jnp.concatenate([stack_pairs(queries), seen.astype(jnp.bfloat16)], axis=1)
            raw = dot_nt(left, key_s[g])
            top_low = jnp.max(raw[:, :ROWS], axis=1, keepdims=True)
            top_high = jnp.max(raw[:, ROWS:], axis=1, keepdims=True)
            weights = jnp.concatenate(
                [jnp.exp2((raw[:, :ROWS] - top_low) * TO_EXP2), jnp.exp2((raw[:, ROWS:] - top_high) * TO_EXP2)], axis=1
            ).astype(jnp.bfloat16)
            mixed = dot_nn(weights, value_s[g])
            total = mixed[:, 128:]
            context = (mixed[:, :128] / total).astype(jnp.bfloat16)
            ctx_v[:, c] = jnp.concatenate([context[:ROWS], context[ROWS:]], axis=1)
            level = jnp.where(lane < HEAD, top_low, top_high) + jnp.log2(total) * (1.0 / TO_EXP2)
            first = level.astype(jnp.bfloat16).astype(jnp.float32)
            second = (level - first).astype(jnp.bfloat16).astype(jnp.float32)
            third = level - first - second
            marks = jnp.where(
                spot == 0, first, jnp.where(spot == 1, second, jnp.where(spot == 2, third, seen))
            ).astype(jnp.bfloat16)
            marks_v[:, c] = jnp.concatenate([marks[:ROWS], marks[ROWS:]], axis=1)
            return carry

        lax.fori_loop(0, KVH, group, 0, unroll=True)
        def finish(i, carry):
            c = cols(i * CHUNK, CHUNK)
            out = h_v[:, c].astype(jnp.float32) + dot_nn(ctx_v[...], wo_v[:, c])
            out_v[:, c] = out.astype(jnp.bfloat16)
            return carry

        if not final:
            lax.fori_loop(0, 8, finish, 0, unroll=True)


def bf16(*shape):
    return jax.ShapeDtypeStruct(shape, jnp.bfloat16)


def inside(*arrays):
    return [pltpu.with_memory_space_constraint(array, pltpu.VMEM) for array in arrays]


def v16(*shape):
    return pltpu.VMEM(shape, jnp.bfloat16)


def v32(*shape):
    return pltpu.VMEM(shape, jnp.float32)


def forward_layer(layer, place, hidden, w_qkv, w_out, normed, proj, ctx, kept, marks):
    final = layer == 7
    return pl.pallas_call(
        functools.partial(forward_kernel, final),
        out_shape=(v16(ROWS, D), v16(ROWS, D), v16(ROWS, WCOLS), v16(ROWS, HQ), v16(ROWS, D), v16(ROWS, HQ)),
        in_specs=[SMEM] + [INSIDE] * 8,
        out_specs=(INSIDE,) * 6,
        input_output_aliases={4: 1, 5: 2, 6: 3, 7: 4, 8: 5},
        scratch_shapes=[v16(KVH, 2 * ROWS, 256), v16(KVH, 2 * ROWS, 256)],
        compiler_params=pltpu.CompilerParams(vmem_limit_bytes=VMEM_LIMIT),
        cost_estimate=pl.CostEstimate(flops=3_000_000_000, bytes_accessed=14_000_000, transcendentals=2_000_000),
        name="forward_last" if final else "forward_layer",
    )(place, *inside(hidden, w_qkv, w_out, normed, proj, ctx, kept, marks))


def backward_kernel(
    last, place, u_v, h_v, proj_v, ctx_v, marks_v, wq_v, wo_v, a0, a1,
    up_v, dproj_v, keep_v, dn_v, key_s, value_s, dkt_s, dvt_s,
):
    del a0, a1

    @pl.when(place[0] == 0)
    def _():
        keep_v[...] = u_v[...]
        fill_keys(proj_v[:, HQ : HQ + KV], key_s, place[1])
        fill_values(proj_v[:, HQ + KV :], value_s, -1.0)

        def group(g, carry):
            c = cols(g * CHUNK, CHUNK)
            d_ctx = dot_nt(u_v[...], wo_v[c, :]).astype(jnp.bfloat16)
            queries = stack_pairs(proj_v[:, c])
            d_pairs = stack_pairs(d_ctx)
            left = jnp.concatenate([queries, stack_pairs(marks_v[:, c])], axis=1)
            weights = jnp.exp2(dot_nt(left, key_s[g]) * TO_EXP2)
            inner = d_pairs.astype(jnp.float32) * stack_pairs(ctx_v[:, c]).astype(jnp.float32)
            d_left = jnp.concatenate([d_pairs, inner.astype(jnp.bfloat16)], axis=1)
            d_scores = (weights * dot_nt(d_left, value_s[g])).astype(jnp.bfloat16)
            d_query = (dot_nn(d_scores, key_s[g][:, :128]) * SCALE).astype(jnp.bfloat16)
            dproj_v[:, c] = jnp.concatenate([d_query[:ROWS], d_query[ROWS:]], axis=1)
            d_key = dot_nn(queries.T, d_scores)
            d_value = dot_nn(d_pairs.T, weights.astype(jnp.bfloat16))
            rows = pl.ds(pl.multiple_of(g * HEAD, HEAD), HEAD)
            dkt_s[rows, :] = (d_key[:HEAD, :ROWS] + d_key[HEAD:, ROWS:]) * SCALE
            dvt_s[rows, :] = d_value[:HEAD, :ROWS] + d_value[HEAD:, ROWS:]
            return carry

        lax.fori_loop(0, KVH, group, 0, unroll=True)
        dproj_v[:, HQ : HQ + KV] = dkt_s[...].T.astype(jnp.bfloat16)
        dproj_v[:, HQ + KV :] = dvt_s[...].T.astype(jnp.bfloat16)
        if not last:
            def widen(i, partial):
                c = cols(i * CHUNK, CHUNK)
                d_normed = dot_nt(dproj_v[...], wq_v[c, :])
                dn_v[:, c] = d_normed
                product = d_normed * h_v[:, c].astype(jnp.float32)
                return partial + product[:, :HALF] + product[:, HALF:]

            partial = lax.fori_loop(0, 8, widen, jnp.zeros((ROWS, HALF), jnp.float32), unroll=True)
            mean = jnp.sum(partial, axis=-1, keepdims=True) * (1.0 / D)
            wide = h_v[...].astype(jnp.float32)
            scale = lax.rsqrt(jnp.mean(wide * wide, axis=-1, keepdims=True) + EPS)
            pull = scale * scale * scale * mean

            def previous(i, carry):
                c = cols(i * CHUNK, CHUNK)
                out = u_v[:, c].astype(jnp.float32) + (scale * dn_v[:, c] - h_v[:, c].astype(jnp.float32) * pull)
                up_v[:, c] = out.astype(jnp.bfloat16)
                return carry

            lax.fori_loop(0, 8, previous, 0, unroll=True)


def backward_layer(layer, place, upstream, kept, proj, ctx, marks, w_qkv, w_out, dproj, ups):
    last = layer == 0
    spare = [place, place] if last else inside(kept, w_qkv)
    where = SMEM if last else INSIDE
    return pl.pallas_call(
        functools.partial(backward_kernel, last),
        out_shape=(v16(ROWS, D), v16(ROWS, WCOLS), v16(ROWS, D)),
        in_specs=[SMEM, INSIDE, where, INSIDE, INSIDE, INSIDE, where, INSIDE, INSIDE, INSIDE],
        out_specs=(INSIDE,) * 3,
        input_output_aliases={8: 1, 9: 2},
        scratch_shapes=[
            v32(ROWS, D), v16(KVH, 2 * ROWS, 256), v16(KVH, 2 * ROWS, 256), v32(KV, ROWS), v32(KV, ROWS)
        ],
        compiler_params=pltpu.CompilerParams(vmem_limit_bytes=VMEM_LIMIT),
        cost_estimate=pl.CostEstimate(flops=4_000_000_000, bytes_accessed=15_000_000, transcendentals=2_000_000),
        name="backward_last" if last else "backward_layer",
    )(place, *inside(upstream), spare[0], *inside(proj, ctx, marks), spare[1], *inside(w_out, dproj, ups))


LAYERS = 8
FINE = (("zlo", 2), ("y", 4), ("x", 4), ("zhi", 4), ("core", 2))
NAMES = tuple(name for name, size in FINE)
SIZES = tuple(size for name, size in FINE)
STAGE = ("y", "core")


def regroup(back):
    pairs = []
    for zlo, y, x, zhi, core in np.ndindex(*SIZES):
        source = np.ravel_multi_index((zlo, y, x, zhi, core), SIZES)
        target = np.ravel_multi_index((core, zlo * 2 + y // 2, x, zhi, y % 2), SIZES)
        pairs.append((int(target), int(source)) if back else (int(source), int(target)))
    return pairs


def z_index(z):
    return (z % 2) * 4 + z // 2


def send_x(value, step):
    return lax.ppermute(value, "x", [(i, (i + step) % 4) for i in range(4)])


def send_z(value, step):
    return lax.ppermute(value, ("zlo", "zhi"), [(z_index(i), z_index((i + step) % 8)) for i in range(8)])


def gather_ring(own, count, send):
    below, above = [own], [own]
    for step in range(count // 2 - 1):
        below.append(send(below[-1], 1))
        above.append(send(above[-1], -1))
    half = own.shape[0] // 2
    far = [send(below[-1][:half], 1), send(above[-1][half:], -1)]
    return above + far + below[:0:-1]


def add(own, came):
    return (own.astype(jnp.float32) + came.astype(jnp.float32)).astype(jnp.bfloat16)


def scatter_direct(take, send, steps):
    total = take(0).astype(jnp.float32)
    for came in [send(take(step), step) for step in steps]:
        total = total + came.astype(jnp.float32)
    return total.astype(jnp.bfloat16)


def gather_direct(own, send):
    far, above, below = send(own, 2), send(own, -1), send(own, 1)
    return [own, above, far, below]


def taker(value, spots, axis, split):
    def take(d, half=None):
        spot = spots[d % len(spots)]
        start, size = [0] * value.ndim, list(value.shape)
        start[axis], size[axis] = spot, 1
        if half is not None:
            size[split] //= 2
            start[split] = half * size[split]
        block = lax.dynamic_slice(value, start, size, allow_negative_indices=False)
        return block.reshape([n for dim, n in enumerate(size) if dim != axis])

    return take


def assemble_kernel(qkv_plan, out_plan, place, *refs):
    count = len(qkv_plan) + len(out_plan)
    parts, (full_qkv, full_out, sems) = refs[:count], refs[-3:]
    x, z = place[0], place[1]
    copies = []
    for ref, (dx, first, pieces) in zip(parts, qkv_plan):
        for i in range(pieces):
            row = (lax.rem(x + dx, 4) * 8 + lax.rem(z + first + i, 8)) * 64
            target = full_qkv.at[pl.ds(pl.multiple_of(row, 64), 64), :]
            copies.append(pltpu.make_async_copy(ref.at[pl.ds(i * 64, 64), :], target, sems.at[len(copies)]))
    for ref, (dz, first, pieces) in zip(parts[len(qkv_plan) :], out_plan):
        for i in range(pieces):
            row = (lax.rem(x + first + i, 4) * 8 + lax.rem(z + dz, 8)) * 32
            target = full_out.at[pl.ds(pl.multiple_of(row, 32), 32), :]
            copies.append(pltpu.make_async_copy(ref.at[pl.ds(i * 32, 32), :], target, sems.at[len(copies)]))
    for copy in copies:
        copy.start()
    for copy in copies:
        copy.wait()


def assemble(place, qkv, out, before):
    qkv_plan, out_plan = [plan for plan, part in qkv], [plan for plan, part in out]
    count = len(qkv) + len(out)
    return pl.pallas_call(
        functools.partial(assemble_kernel, qkv_plan, out_plan),
        out_shape=(v16(D, WCOLS), v16(HQ, D)),
        in_specs=[SMEM] + [ANY] * count + [INSIDE] * len(before),
        out_specs=(INSIDE, INSIDE),
        input_output_aliases={count + 1: 0, count + 2: 1} if before else {},
        scratch_shapes=[pltpu.SemaphoreType.DMA((64,))],
        compiler_params=pltpu.CompilerParams(vmem_limit_bytes=4 * 1024 * 1024),
        cost_estimate=pl.CostEstimate(flops=0, bytes_accessed=6_000_000 if before else 18_000_000, transcendentals=0),
        name="assemble_rest" if before else "assemble",
    )(place, *[part for plan, part in qkv], *[part for plan, part in out], *inside(*before))


def gather_weights(near, far, x, z):
    column = jnp.concatenate(gather_ring(near, 8, send_z))
    row = jnp.concatenate(gather_direct(far, send_x))
    qkv_parts = gather_ring(column, 4, send_x)
    out_parts = gather_ring(row, 8, send_z)
    qkv = list(zip([(0, 0, 8), (1, 0, 8), (2, 0, 4), (2, 4, 4), (3, 0, 8)], qkv_parts))
    spots = [(0, 0, 4), (1, 0, 4), (2, 0, 4), (3, 0, 4), (4, 0, 2), (4, 2, 2), (5, 0, 4), (6, 0, 4), (7, 0, 4)]
    out = list(zip(spots, out_parts))
    place = jnp.stack([x, z])
    early = assemble(place, [qkv[0], qkv[1], qkv[4]], out[:3] + out[7:], ())
    return assemble(place, qkv[2:4], out[3:7], early)


def sum_of(*terms):
    return sum(term.astype(jnp.float32) for term in terms).astype(jnp.bfloat16)


def scatter_start(part_out, spins):
    take = taker(part_out.reshape(4, 8, 32, D), spins, 1, 0)
    return take, send_z(take(4, 0), 1), send_z(take(4, 1), -1)


def scatter_both(part_qkv, started, turns, spins):
    take_z, up_z, down_z = started
    take_x = taker(part_qkv.reshape(4, 512, WCOLS), turns, 0, 1)
    up_x, down_x = send_x(take_x(2, 0), 1), send_x(take_x(2, 1), -1)
    out_up = jnp.concatenate([add(take_z(3, 0), up_z), take_z(3, 1)])
    out_down = jnp.concatenate([take_z(-3, 0), add(take_z(-3, 1), down_z)])
    up_z, down_z = send_z(out_up, 1), send_z(out_down, -1)
    qkv_up = jnp.concatenate([add(take_x(1, 0), up_x), take_x(1, 1)])
    qkv_down = jnp.concatenate([take_x(-1, 0), add(take_x(-1, 1), down_x)])
    out_up, out_down = add(take_z(2), up_z), add(take_z(-2), down_z)
    qkv_up, qkv_down, out_up, out_down = lax.optimization_barrier((qkv_up, qkv_down, out_up, out_down))
    up_x, down_x = send_x(qkv_up, 1), send_x(qkv_down, -1)
    up_z, down_z = send_z(out_up, 1), send_z(out_down, -1)
    up_z, down_z = send_z(add(take_z(1), up_z), 1), send_z(add(take_z(-1), down_z), -1)
    mine_out = sum_of(take_z(0), up_z, down_z)
    mine_qkv = sum_of(take_x(0), up_x, down_x)
    grad_out = scatter_direct(taker(mine_out, turns, 0, 1), send_x, (2, 1, -1))
    grad_qkv = scatter_direct(
        taker(mine_qkv.reshape(8, 64, WCOLS), spins, 0, 1), send_z, (4, 3, -3, 2, -2, 1, -1)
    )
    return grad_qkv, grad_out


def on_device(inputs, cotangent, joined, w_qkv, w_out):
    micro = lax.axis_index("zlo")
    stage = 2 * lax.axis_index("y") + lax.axis_index("core")
    x_index = lax.axis_index("x")
    z_place = 2 * lax.axis_index("zhi") + micro
    bin_index = 4 * x_index + lax.axis_index("zhi")
    flag = joined[micro, bin_index]
    near = lax.ppermute(w_qkv[0], NAMES, regroup(False))
    near, later = lax.optimization_barrier((near, w_out[0]))
    far = lax.ppermute(later, NAMES, regroup(False))
    full_qkv, full_out = gather_weights(near, far, x_index, z_place)
    block = lax.dynamic_index_in_dim(inputs, micro, 0, keepdims=False)
    hidden = jnp.concatenate([block, lax.ppermute(block, "core", [(1, 0)])])
    block = lax.dynamic_index_in_dim(cotangent, micro, 0, keepdims=False)
    upstream = jnp.concatenate([lax.ppermute(block, "core", [(0, 1)]), block])

    places = [jnp.stack([stage - layer, flag]) for layer in range(LAYERS)]
    turns = [((x_index + d) % 4) for d in range(4)]
    spins = [((z_place + d) % 8) for d in range(8)]
    places, turns, spins = lax.optimization_barrier((places, turns, spins))
    normed = jnp.zeros((ROWS, D), jnp.bfloat16)
    kept = jnp.zeros((ROWS, D), jnp.bfloat16)
    proj = jnp.zeros((ROWS, WCOLS), jnp.bfloat16)
    ctx = jnp.zeros((ROWS, HQ), jnp.bfloat16)
    marks = jnp.zeros((ROWS, HQ), jnp.bfloat16)
    for layer in range(LAYERS):
        result, normed, proj, ctx, kept, marks = forward_layer(
            layer, places[layer], hidden, full_qkv, full_out, normed, proj, ctx, kept, marks
        )
        if layer < LAYERS - 1:
            hidden = lax.ppermute(result, STAGE, [(layer, layer + 1)])
    dproj = jnp.zeros((ROWS, WCOLS), jnp.bfloat16)
    ups = jnp.zeros((ROWS, D), jnp.bfloat16)
    contract = (((0,), (0,)), ((), ()))
    for layer in reversed(range(LAYERS)):
        if layer == 0:
            arrived = jnp.where(stage == 0, upstream, ups)
            part_out = lax.dot_general(ctx, arrived, contract, preferred_element_type=jnp.float32).astype(jnp.bfloat16)
            part_out, upstream = lax.optimization_barrier((part_out, upstream))
            started = scatter_start(part_out, spins)
        result, dproj, ups = backward_layer(
            layer, places[layer], upstream, kept, proj, ctx, marks, full_qkv, full_out, dproj, ups
        )
        if layer:
            upstream = lax.ppermute(result, STAGE, [(layer, layer - 1)])
    part_qkv = lax.dot_general(normed, dproj, contract, preferred_element_type=jnp.float32).astype(jnp.bfloat16)
    grad_qkv, grad_out = scatter_both(part_qkv, started, turns, spins)
    grad_out = lax.ppermute(grad_out, NAMES, regroup(True)).astype(jnp.float32)
    grad_qkv = lax.ppermute(grad_qkv, NAMES, regroup(True)).astype(jnp.float32)
    return (grad_qkv[None], grad_out[None])


def solution(mesh):
    fine = jax.sharding.Mesh(mesh.devices.reshape(SIZES), NAMES)
    token = P(None, ("x", "zhi", "core"), None)
    weight = P(("zlo", "y"), ("x", "zhi", "core"), None)
    return jax.shard_map(
        on_device,
        mesh=fine,
        in_specs=(token, token, P(), weight, weight),
        out_specs=(weight, weight),
        check_vma=False,
    )
```

```python
import functools
import math

import jax
import jax.numpy as jnp
import numpy as np
from jax import lax
from jax.experimental import pallas as pl
from jax.experimental.pallas import tpu as pltpu
from jax.sharding import PartitionSpec as P

HEADS = 16
HEAD = 64
KVH = 4
GROUP = HEADS // KVH
ROWS = 256
HALF = 128
D = 2048
HQ = HEADS * HEAD
KV = KVH * HEAD
WCOLS = HQ + 2 * KV
CHUNK = 256
EPS = 1e-5
SCALE = 1.0 / math.sqrt(HEAD)
TO_EXP2 = SCALE * math.log2(math.e)
NT = (((1,), (1,)), ((), ()))
VMEM_LIMIT = 16 * 1024 * 1024
ANY = pl.BlockSpec(memory_space=pl.ANY)
SMEM = pl.BlockSpec(memory_space=pltpu.SMEM)
INSIDE = pl.BlockSpec(memory_space=pltpu.VMEM)


def dot_nt(left, right):
    return lax.dot_general(left, right, NT, preferred_element_type=jnp.float32)


def dot_nn(left, right):
    return jnp.dot(left, right, preferred_element_type=jnp.float32)


def cols(start, size):
    return pl.ds(pl.multiple_of(start, size), size)


def packed_halves(tile, upper):
    lane = lax.broadcasted_iota(jnp.int32, tile.shape, 1)
    wide = tile.astype(jnp.float32)
    kept = jnp.where((lane >= HEAD) == upper, wide, 0.0)
    turned = pltpu.roll(kept, HEAD, 1)
    low, high = (turned, kept) if upper else (kept, turned)
    return low.astype(jnp.bfloat16), high.astype(jnp.bfloat16)


def fill_keys(keys, key_s, joined):
    row = lax.broadcasted_iota(jnp.int32, (ROWS, 2 * HEAD), 0)
    lane = lax.broadcasted_iota(jnp.int32, (ROWS, 2 * HEAD), 1)
    hidden = jnp.where(joined > 0, 0.0, -1e30)
    other = jnp.logical_or(
        jnp.logical_and(lane == 3, row >= HALF), jnp.logical_and(lane == 4, row < HALF)
    )
    apart = jnp.where(other, hidden, 0.0)
    low_marks = jnp.where(lane < 3, -1.0, apart).astype(jnp.bfloat16)
    high_marks = jnp.where(jnp.logical_and(lane >= HEAD, lane < HEAD + 3), -1.0, apart).astype(jnp.bfloat16)
    for g in range(KVH):
        low, high = packed_halves(keys[:, g // 2 * 128 : g // 2 * 128 + 128], g % 2 == 1)
        key_s[g, :ROWS, :128] = low
        key_s[g, ROWS:, :128] = high
        key_s[g, :ROWS, 128:] = low_marks
        key_s[g, ROWS:, 128:] = high_marks


def fill_values(values, value_s, mark):
    lane = lax.broadcasted_iota(jnp.int32, (ROWS, 2 * HEAD), 1)
    low_marks = jnp.where(lane < HEAD, mark, 0.0).astype(jnp.bfloat16)
    high_marks = jnp.where(lane >= HEAD, mark, 0.0).astype(jnp.bfloat16)
    for g in range(KVH):
        low, high = packed_halves(values[:, g // 2 * 128 : g // 2 * 128 + 128], g % 2 == 1)
        value_s[g, :ROWS, :128] = low
        value_s[g, ROWS:, :128] = high
        value_s[g, :ROWS, 128:] = low_marks
        value_s[g, ROWS:, 128:] = high_marks


def stack_pairs(value):
    return jnp.concatenate([value[:, :128], value[:, 128:]], axis=0)


def forward_kernel(
    final, place, h_v, wq_v, wo_v, a0, a1, a2, a3, a4,
    out_v, normed_v, proj_v, ctx_v, keep_v, marks_v, key_s, value_s,
):
    del a0, a1, a2, a3, a4

    @pl.when(place[0] == 0)
    def _():
        block = (lax.broadcasted_iota(jnp.int32, (2 * ROWS, 128), 0) // HALF) % 2
        lane = lax.broadcasted_iota(jnp.int32, (2 * ROWS, 128), 1)
        spot = lane % HEAD
        seen = jnp.where(jnp.logical_or(jnp.logical_and(lane == 3, block == 0), jnp.logical_and(lane == 4, block == 1)), 1.0, 0.0)
        keep_v[...] = h_v[...]
        wide = h_v[...].astype(jnp.float32)
        scale = lax.rsqrt(jnp.mean(wide * wide, axis=-1, keepdims=True) + EPS)
        normed_v[...] = (wide * scale).astype(jnp.bfloat16)
        both = dot_nn(normed_v[...], wq_v[:, HQ:]).astype(jnp.bfloat16)
        proj_v[:, HQ:] = both
        fill_keys(both[:, :KV], key_s, place[1])
        fill_values(both[:, KV:], value_s, 1.0)

        def group(g, carry):
            c = cols(g * CHUNK, CHUNK)
            queries = dot_nn(normed_v[...], wq_v[:, c]).astype(jnp.bfloat16)
            proj_v[:, c] = queries
            left = jnp.concatenate([stack_pairs(queries), seen.astype(jnp.bfloat16)], axis=1)
            raw = dot_nt(left, key_s[g])
            top_low = jnp.max(raw[:, :ROWS], axis=1, keepdims=True)
            top_high = jnp.max(raw[:, ROWS:], axis=1, keepdims=True)
            weights = jnp.concatenate(
                [jnp.exp2((raw[:, :ROWS] - top_low) * TO_EXP2), jnp.exp2((raw[:, ROWS:] - top_high) * TO_EXP2)], axis=1
            ).astype(jnp.bfloat16)
            mixed = dot_nn(weights, value_s[g])
            total = mixed[:, 128:]
            context = (mixed[:, :128] / total).astype(jnp.bfloat16)
            ctx_v[:, c] = jnp.concatenate([context[:ROWS], context[ROWS:]], axis=1)
            level = jnp.where(lane < HEAD, top_low, top_high) + jnp.log2(total) * (1.0 / TO_EXP2)
            first = level.astype(jnp.bfloat16).astype(jnp.float32)
            second = (level - first).astype(jnp.bfloat16).astype(jnp.float32)
            third = level - first - second
            marks = jnp.where(
                spot == 0, first, jnp.where(spot == 1, second, jnp.where(spot == 2, third, seen))
            ).astype(jnp.bfloat16)
            marks_v[:, c] = jnp.concatenate([marks[:ROWS], marks[ROWS:]], axis=1)
            return carry

        lax.fori_loop(0, KVH, group, 0, unroll=True)
        def finish(i, carry):
            c = cols(i * CHUNK, CHUNK)
            out = h_v[:, c].astype(jnp.float32) + dot_nn(ctx_v[...], wo_v[:, c])
            out_v[:, c] = out.astype(jnp.bfloat16)
            return carry

        if not final:
            lax.fori_loop(0, 8, finish, 0, unroll=True)


def bf16(*shape):
    return jax.ShapeDtypeStruct(shape, jnp.bfloat16)


def inside(*arrays):
    return [pltpu.with_memory_space_constraint(array, pltpu.VMEM) for array in arrays]


def v16(*shape):
    return pltpu.VMEM(shape, jnp.bfloat16)


def v32(*shape):
    return pltpu.VMEM(shape, jnp.float32)


def forward_layer(layer, place, hidden, w_qkv, w_out, normed, proj, ctx, kept, marks):
    final = layer == 7
    return pl.pallas_call(
        functools.partial(forward_kernel, final),
        out_shape=(v16(ROWS, D), v16(ROWS, D), v16(ROWS, WCOLS), v16(ROWS, HQ), v16(ROWS, D), v16(ROWS, HQ)),
        in_specs=[SMEM] + [INSIDE] * 8,
        out_specs=(INSIDE,) * 6,
        input_output_aliases={4: 1, 5: 2, 6: 3, 7: 4, 8: 5},
        scratch_shapes=[v16(KVH, 2 * ROWS, 256), v16(KVH, 2 * ROWS, 256)],
        compiler_params=pltpu.CompilerParams(vmem_limit_bytes=VMEM_LIMIT),
        cost_estimate=pl.CostEstimate(flops=3_000_000_000, bytes_accessed=14_000_000, transcendentals=2_000_000),
        name="forward_last" if final else "forward_layer",
    )(place, *inside(hidden, w_qkv, w_out, normed, proj, ctx, kept, marks))


def backward_kernel(
    last, place, u_v, h_v, proj_v, ctx_v, marks_v, wq_v, wo_v, a0, a1,
    up_v, dproj_v, keep_v, dn_v, key_s, value_s, dkt_s, dvt_s,
):
    del a0, a1

    @pl.when(place[0] == 0)
    def _():
        keep_v[...] = u_v[...]
        fill_keys(proj_v[:, HQ : HQ + KV], key_s, place[1])
        fill_values(proj_v[:, HQ + KV :], value_s, -1.0)

        def group(g, carry):
            c = cols(g * CHUNK, CHUNK)
            d_ctx = dot_nt(u_v[...], wo_v[c, :]).astype(jnp.bfloat16)
            queries = stack_pairs(proj_v[:, c])
            d_pairs = stack_pairs(d_ctx)
            left = jnp.concatenate([queries, stack_pairs(marks_v[:, c])], axis=1)
            weights = jnp.exp2(dot_nt(left, key_s[g]) * TO_EXP2)
            inner = d_pairs.astype(jnp.float32) * stack_pairs(ctx_v[:, c]).astype(jnp.float32)
            d_left = jnp.concatenate([d_pairs, inner.astype(jnp.bfloat16)], axis=1)
            d_scores = (weights * dot_nt(d_left, value_s[g])).astype(jnp.bfloat16)
            d_query = (dot_nn(d_scores, key_s[g][:, :128]) * SCALE).astype(jnp.bfloat16)
            dproj_v[:, c] = jnp.concatenate([d_query[:ROWS], d_query[ROWS:]], axis=1)
            d_key = dot_nn(queries.T, d_scores)
            d_value = dot_nn(d_pairs.T, weights.astype(jnp.bfloat16))
            rows = pl.ds(pl.multiple_of(g * HEAD, HEAD), HEAD)
            dkt_s[rows, :] = (d_key[:HEAD, :ROWS] + d_key[HEAD:, ROWS:]) * SCALE
            dvt_s[rows, :] = d_value[:HEAD, :ROWS] + d_value[HEAD:, ROWS:]
            return carry

        lax.fori_loop(0, KVH, group, 0, unroll=True)
        dproj_v[:, HQ : HQ + KV] = dkt_s[...].T.astype(jnp.bfloat16)
        dproj_v[:, HQ + KV :] = dvt_s[...].T.astype(jnp.bfloat16)
        if not last:
            def widen(i, partial):
                c = cols(i * CHUNK, CHUNK)
                d_normed = dot_nt(dproj_v[...], wq_v[c, :])
                dn_v[:, c] = d_normed
                product = d_normed * h_v[:, c].astype(jnp.float32)
                return partial + product[:, :HALF] + product[:, HALF:]

            partial = lax.fori_loop(0, 8, widen, jnp.zeros((ROWS, HALF), jnp.float32), unroll=True)
            mean = jnp.sum(partial, axis=-1, keepdims=True) * (1.0 / D)
            wide = h_v[...].astype(jnp.float32)
            scale = lax.rsqrt(jnp.mean(wide * wide, axis=-1, keepdims=True) + EPS)
            pull = scale * scale * scale * mean

            def previous(i, carry):
                c = cols(i * CHUNK, CHUNK)
                out = u_v[:, c].astype(jnp.float32) + (scale * dn_v[:, c] - h_v[:, c].astype(jnp.float32) * pull)
                up_v[:, c] = out.astype(jnp.bfloat16)
                return carry

            lax.fori_loop(0, 8, previous, 0, unroll=True)


def backward_layer(layer, place, upstream, kept, proj, ctx, marks, w_qkv, w_out, dproj, ups):
    last = layer == 0
    spare = [place, place] if last else inside(kept, w_qkv)
    where = SMEM if last else INSIDE
    return pl.pallas_call(
        functools.partial(backward_kernel, last),
        out_shape=(v16(ROWS, D), v16(ROWS, WCOLS), v16(ROWS, D)),
        in_specs=[SMEM, INSIDE, where, INSIDE, INSIDE, INSIDE, where, INSIDE, INSIDE, INSIDE],
        out_specs=(INSIDE,) * 3,
        input_output_aliases={8: 1, 9: 2},
        scratch_shapes=[
            v32(ROWS, D), v16(KVH, 2 * ROWS, 256), v16(KVH, 2 * ROWS, 256), v32(KV, ROWS), v32(KV, ROWS)
        ],
        compiler_params=pltpu.CompilerParams(vmem_limit_bytes=VMEM_LIMIT),
        cost_estimate=pl.CostEstimate(flops=4_000_000_000, bytes_accessed=15_000_000, transcendentals=2_000_000),
        name="backward_last" if last else "backward_layer",
    )(place, *inside(upstream), spare[0], *inside(proj, ctx, marks), spare[1], *inside(w_out, dproj, ups))


LAYERS = 8
FINE = (("zlo", 2), ("y", 4), ("x", 4), ("zhi", 4), ("core", 2))
NAMES = tuple(name for name, size in FINE)
SIZES = tuple(size for name, size in FINE)
STAGE = ("y", "core")


def regroup(back):
    pairs = []
    for zlo, y, x, zhi, core in np.ndindex(*SIZES):
        source = np.ravel_multi_index((zlo, y, x, zhi, core), SIZES)
        target = np.ravel_multi_index((core, zlo * 2 + y // 2, x, zhi, y % 2), SIZES)
        pairs.append((int(target), int(source)) if back else (int(source), int(target)))
    return pairs


def z_index(z):
    return (z % 2) * 4 + z // 2


def send_x(value, step):
    return lax.ppermute(value, "x", [(i, (i + step) % 4) for i in range(4)])


def send_z(value, step):
    return lax.ppermute(value, ("zlo", "zhi"), [(z_index(i), z_index((i + step) % 8)) for i in range(8)])


def gather_ring(own, count, send):
    below, above = [own], [own]
    for step in range(count // 2 - 1):
        below.append(send(below[-1], 1))
        above.append(send(above[-1], -1))
    half = own.shape[0] // 2
    far = [send(below[-1][:half], 1), send(above[-1][half:], -1)]
    return above + far + below[:0:-1]


def add(own, came):
    return (own.astype(jnp.float32) + came.astype(jnp.float32)).astype(jnp.bfloat16)


def scatter_direct(take, send, steps):
    total = take(0).astype(jnp.float32)
    for came in [send(take(step), step) for step in steps]:
        total = total + came.astype(jnp.float32)
    return total.astype(jnp.bfloat16)


def gather_direct(own, send):
    far, above, below = send(own, 2), send(own, -1), send(own, 1)
    return [own, above, far, below]


def taker(value, spots, axis, split):
    def take(d, half=None):
        spot = spots[d % len(spots)]
        start, size = [0] * value.ndim, list(value.shape)
        start[axis], size[axis] = spot, 1
        if half is not None:
            size[split] //= 2
            start[split] = half * size[split]
        block = lax.dynamic_slice(value, start, size, allow_negative_indices=False)
        return block.reshape([n for dim, n in enumerate(size) if dim != axis])

    return take


def assemble_kernel(qkv_plan, out_plan, place, *refs):
    count = len(qkv_plan) + len(out_plan)
    parts, (full_qkv, full_out, sems) = refs[:count], refs[-3:]
    x, z = place[0], place[1]
    copies = []
    for ref, (dx, first, pieces) in zip(parts, qkv_plan):
        for i in range(pieces):
            row = (lax.rem(x + dx, 4) * 8 + lax.rem(z + first + i, 8)) * 64
            target = full_qkv.at[pl.ds(pl.multiple_of(row, 64), 64), :]
            copies.append(pltpu.make_async_copy(ref.at[pl.ds(i * 64, 64), :], target, sems.at[len(copies)]))
    for ref, (dz, first, pieces) in zip(parts[len(qkv_plan) :], out_plan):
        for i in range(pieces):
            row = (lax.rem(x + first + i, 4) * 8 + lax.rem(z + dz, 8)) * 32
            target = full_out.at[pl.ds(pl.multiple_of(row, 32), 32), :]
            copies.append(pltpu.make_async_copy(ref.at[pl.ds(i * 32, 32), :], target, sems.at[len(copies)]))
    for copy in copies:
        copy.start()
    for copy in copies:
        copy.wait()


def assemble(place, qkv, out, before):
    qkv_plan, out_plan = [plan for plan, part in qkv], [plan for plan, part in out]
    count = len(qkv) + len(out)
    return pl.pallas_call(
        functools.partial(assemble_kernel, qkv_plan, out_plan),
        out_shape=(v16(D, WCOLS), v16(HQ, D)),
        in_specs=[SMEM] + [ANY] * count + [INSIDE] * len(before),
        out_specs=(INSIDE, INSIDE),
        input_output_aliases={count + 1: 0, count + 2: 1} if before else {},
        scratch_shapes=[pltpu.SemaphoreType.DMA((64,))],
        compiler_params=pltpu.CompilerParams(vmem_limit_bytes=4 * 1024 * 1024),
        cost_estimate=pl.CostEstimate(flops=0, bytes_accessed=6_000_000 if before else 18_000_000, transcendentals=0),
        name="assemble_rest" if before else "assemble",
    )(place, *[part for plan, part in qkv], *[part for plan, part in out], *inside(*before))


def gather_weights(near, far, x, z):
    column = jnp.concatenate(gather_ring(near, 8, send_z))
    row = jnp.concatenate(gather_direct(far, send_x))
    qkv_parts = gather_ring(column, 4, send_x)
    out_parts = gather_ring(row, 8, send_z)
    qkv = list(zip([(0, 0, 8), (1, 0, 8), (2, 0, 4), (2, 4, 4), (3, 0, 8)], qkv_parts))
    spots = [(0, 0, 4), (1, 0, 4), (2, 0, 4), (3, 0, 4), (4, 0, 2), (4, 2, 2), (5, 0, 4), (6, 0, 4), (7, 0, 4)]
    out = list(zip(spots, out_parts))
    place = jnp.stack([x, z])
    early = assemble(place, [qkv[0], qkv[1], qkv[4]], out[:3] + out[7:], ())
    return assemble(place, qkv[2:4], out[3:7], early)


def sum_of(*terms):
    return sum(term.astype(jnp.float32) for term in terms).astype(jnp.bfloat16)


def scatter_start(part_out, spins):
    take = taker(part_out.reshape(4, 8, 32, D), spins, 1, 0)
    return take, send_z(take(4, 0), 1), send_z(take(4, 1), -1)


def scatter_both(part_qkv, started, turns, spins):
    take_z, up_z, down_z = started
    take_x = taker(part_qkv.reshape(4, 512, WCOLS), turns, 0, 1)
    up_x, down_x = send_x(take_x(2, 0), 1), send_x(take_x(2, 1), -1)
    out_up = jnp.concatenate([add(take_z(3, 0), up_z), take_z(3, 1)])
    out_down = jnp.concatenate([take_z(-3, 0), add(take_z(-3, 1), down_z)])
    up_z, down_z = send_z(out_up, 1), send_z(out_down, -1)
    qkv_up = jnp.concatenate([add(take_x(1, 0), up_x), take_x(1, 1)])
    qkv_down = jnp.concatenate([take_x(-1, 0), add(take_x(-1, 1), down_x)])
    out_up, out_down = add(take_z(2), up_z), add(take_z(-2), down_z)
    qkv_up, qkv_down, out_up, out_down = lax.optimization_barrier((qkv_up, qkv_down, out_up, out_down))
    up_x, down_x = send_x(qkv_up, 1), send_x(qkv_down, -1)
    up_z, down_z = send_z(out_up, 1), send_z(out_down, -1)
    up_z, down_z = send_z(add(take_z(1), up_z), 1), send_z(add(take_z(-1), down_z), -1)
    mine_out = sum_of(take_z(0), up_z, down_z)
    mine_qkv = sum_of(take_x(0), up_x, down_x)
    grad_out = scatter_direct(taker(mine_out, turns, 0, 1), send_x, (2, 1, -1))
    grad_qkv = scatter_direct(
        taker(mine_qkv.reshape(8, 64, WCOLS), spins, 0, 1), send_z, (4, 3, -3, 2, -2, 1, -1)
    )
    return grad_qkv, grad_out


def on_device(inputs, cotangent, joined, w_qkv, w_out):
    micro = lax.axis_index("zlo")
    stage = 2 * lax.axis_index("y") + lax.axis_index("core")
    x_index = lax.axis_index("x")
    z_place = 2 * lax.axis_index("zhi") + micro
    bin_index = 4 * x_index + lax.axis_index("zhi")
    flag = joined[micro, bin_index]
    near = lax.ppermute(w_qkv[0], NAMES, regroup(False))
    far = lax.ppermute(w_out[0], NAMES, regroup(False))
    full_qkv, full_out = gather_weights(near, far, x_index, z_place)
    block = lax.dynamic_index_in_dim(inputs, micro, 0, keepdims=False)
    hidden = jnp.concatenate([block, lax.ppermute(block, "core", [(1, 0)])])
    block = lax.dynamic_index_in_dim(cotangent, micro, 0, keepdims=False)
    upstream = jnp.concatenate([lax.ppermute(block, "core", [(0, 1)]), block])

    places = [jnp.stack([stage - layer, flag]) for layer in range(LAYERS)]
    turns = [((x_index + d) % 4) for d in range(4)]
    spins = [((z_place + d) % 8) for d in range(8)]
    places, turns, spins = lax.optimization_barrier((places, turns, spins))
    normed = jnp.zeros((ROWS, D), jnp.bfloat16)
    kept = jnp.zeros((ROWS, D), jnp.bfloat16)
    proj = jnp.zeros((ROWS, WCOLS), jnp.bfloat16)
    ctx = jnp.zeros((ROWS, HQ), jnp.bfloat16)
    marks = jnp.zeros((ROWS, HQ), jnp.bfloat16)
    for layer in range(LAYERS):
        result, normed, proj, ctx, kept, marks = forward_layer(
            layer, places[layer], hidden, full_qkv, full_out, normed, proj, ctx, kept, marks
        )
        if layer < LAYERS - 1:
            hidden = lax.ppermute(result, STAGE, [(layer, layer + 1)])
    dproj = jnp.zeros((ROWS, WCOLS), jnp.bfloat16)
    ups = jnp.zeros((ROWS, D), jnp.bfloat16)
    contract = (((0,), (0,)), ((), ()))
    for layer in reversed(range(LAYERS)):
        if layer == 0:
            arrived = jnp.where(stage == 0, upstream, ups)
            part_out = lax.dot_general(ctx, arrived, contract, preferred_element_type=jnp.float32).astype(jnp.bfloat16)
            part_out, upstream = lax.optimization_barrier((part_out, upstream))
            started = scatter_start(part_out, spins)
        result, dproj, ups = backward_layer(
            layer, places[layer], upstream, kept, proj, ctx, marks, full_qkv, full_out, dproj, ups
        )
        if layer:
            upstream = lax.ppermute(result, STAGE, [(layer, layer - 1)])
    part_qkv = lax.dot_general(normed, dproj, contract, preferred_element_type=jnp.float32).astype(jnp.bfloat16)
    grad_qkv, grad_out = scatter_both(part_qkv, started, turns, spins)
    grad_out = lax.ppermute(grad_out, NAMES, regroup(True)).astype(jnp.float32)
    grad_qkv = lax.ppermute(grad_qkv, NAMES, regroup(True)).astype(jnp.float32)
    return (grad_qkv[None], grad_out[None])


def solution(mesh):
    fine = jax.sharding.Mesh(mesh.devices.reshape(SIZES), NAMES)
    token = P(None, ("x", "zhi", "core"), None)
    weight = P(("zlo", "y"), ("x", "zhi", "core"), None)
    return jax.shard_map(
        on_device,
        mesh=fine,
        in_specs=(token, token, P(), weight, weight),
        out_specs=(weight, weight),
        check_vma=False,
    )
```

```python
import functools
import math

import jax
import jax.numpy as jnp
import numpy as np
from jax import lax
from jax.experimental import pallas as pl
from jax.experimental.pallas import tpu as pltpu
from jax.sharding import PartitionSpec as P

HEADS = 16
HEAD = 64
KVH = 4
GROUP = HEADS // KVH
ROWS = 256
HALF = 128
D = 2048
HQ = HEADS * HEAD
KV = KVH * HEAD
WCOLS = HQ + 2 * KV
CHUNK = 256
EPS = 1e-5
SCALE = 1.0 / math.sqrt(HEAD)
TO_EXP2 = SCALE * math.log2(math.e)
NT = (((1,), (1,)), ((), ()))
VMEM_LIMIT = 16 * 1024 * 1024
ANY = pl.BlockSpec(memory_space=pl.ANY)
SMEM = pl.BlockSpec(memory_space=pltpu.SMEM)
INSIDE = pl.BlockSpec(memory_space=pltpu.VMEM)


def dot_nt(left, right):
    return lax.dot_general(left, right, NT, preferred_element_type=jnp.float32)


def dot_nn(left, right):
    return jnp.dot(left, right, preferred_element_type=jnp.float32)


def cols(start, size):
    return pl.ds(pl.multiple_of(start, size), size)


def packed_halves(tile, upper):
    lane = lax.broadcasted_iota(jnp.int32, tile.shape, 1)
    wide = tile.astype(jnp.float32)
    kept = jnp.where((lane >= HEAD) == upper, wide, 0.0)
    turned = pltpu.roll(kept, HEAD, 1)
    low, high = (turned, kept) if upper else (kept, turned)
    return low.astype(jnp.bfloat16), high.astype(jnp.bfloat16)


def fill_keys(keys, key_s, joined):
    row = lax.broadcasted_iota(jnp.int32, (ROWS, 2 * HEAD), 0)
    lane = lax.broadcasted_iota(jnp.int32, (ROWS, 2 * HEAD), 1)
    hidden = jnp.where(joined > 0, 0.0, -1e30)
    other = jnp.logical_or(
        jnp.logical_and(lane == 3, row >= HALF), jnp.logical_and(lane == 4, row < HALF)
    )
    apart = jnp.where(other, hidden, 0.0)
    low_marks = jnp.where(lane < 3, -1.0, apart).astype(jnp.bfloat16)
    high_marks = jnp.where(jnp.logical_and(lane >= HEAD, lane < HEAD + 3), -1.0, apart).astype(jnp.bfloat16)
    for g in range(KVH):
        low, high = packed_halves(keys[:, g // 2 * 128 : g // 2 * 128 + 128], g % 2 == 1)
        key_s[g, :ROWS, :128] = low
        key_s[g, ROWS:, :128] = high
        key_s[g, :ROWS, 128:] = low_marks
        key_s[g, ROWS:, 128:] = high_marks


def fill_values(values, value_s, mark):
    lane = lax.broadcasted_iota(jnp.int32, (ROWS, 2 * HEAD), 1)
    low_marks = jnp.where(lane < HEAD, mark, 0.0).astype(jnp.bfloat16)
    high_marks = jnp.where(lane >= HEAD, mark, 0.0).astype(jnp.bfloat16)
    for g in range(KVH):
        low, high = packed_halves(values[:, g // 2 * 128 : g // 2 * 128 + 128], g % 2 == 1)
        value_s[g, :ROWS, :128] = low
        value_s[g, ROWS:, :128] = high
        value_s[g, :ROWS, 128:] = low_marks
        value_s[g, ROWS:, 128:] = high_marks


def stack_pairs(value):
    return jnp.concatenate([value[:, :128], value[:, 128:]], axis=0)


def forward_kernel(
    final, place, h_v, wq_v, wo_v, a0, a1, a2, a3, a4,
    out_v, normed_v, proj_v, ctx_v, keep_v, marks_v, key_s, value_s,
):
    del a0, a1, a2, a3, a4

    @pl.when(place[0] == 0)
    def _():
        block = (lax.broadcasted_iota(jnp.int32, (2 * ROWS, 128), 0) // HALF) % 2
        lane = lax.broadcasted_iota(jnp.int32, (2 * ROWS, 128), 1)
        spot = lane % HEAD
        seen = jnp.where(jnp.logical_or(jnp.logical_and(lane == 3, block == 0), jnp.logical_and(lane == 4, block == 1)), 1.0, 0.0)
        keep_v[...] = h_v[...]
        wide = h_v[...].astype(jnp.float32)
        scale = lax.rsqrt(jnp.mean(wide * wide, axis=-1, keepdims=True) + EPS)
        normed_v[...] = (wide * scale).astype(jnp.bfloat16)
        both = dot_nn(normed_v[...], wq_v[:, HQ:]).astype(jnp.bfloat16)
        proj_v[:, HQ:] = both
        fill_keys(both[:, :KV], key_s, place[1])
        fill_values(both[:, KV:], value_s, 1.0)

        def group(g, carry):
            c = cols(g * CHUNK, CHUNK)
            queries = dot_nn(normed_v[...], wq_v[:, c]).astype(jnp.bfloat16)
            proj_v[:, c] = queries
            left = jnp.concatenate([stack_pairs(queries), seen.astype(jnp.bfloat16)], axis=1)
            raw = dot_nt(left, key_s[g])
            top_low = jnp.max(raw[:, :ROWS], axis=1, keepdims=True)
            top_high = jnp.max(raw[:, ROWS:], axis=1, keepdims=True)
            weights = jnp.concatenate(
                [jnp.exp2((raw[:, :ROWS] - top_low) * TO_EXP2), jnp.exp2((raw[:, ROWS:] - top_high) * TO_EXP2)], axis=1
            ).astype(jnp.bfloat16)
            mixed = dot_nn(weights, value_s[g])
            total = mixed[:, 128:]
            context = (mixed[:, :128] / total).astype(jnp.bfloat16)
            ctx_v[:, c] = jnp.concatenate([context[:ROWS], context[ROWS:]], axis=1)
            level = jnp.where(lane < HEAD, top_low, top_high) + jnp.log2(total) * (1.0 / TO_EXP2)
            first = level.astype(jnp.bfloat16).astype(jnp.float32)
            second = (level - first).astype(jnp.bfloat16).astype(jnp.float32)
            third = level - first - second
            marks = jnp.where(
                spot == 0, first, jnp.where(spot == 1, second, jnp.where(spot == 2, third, seen))
            ).astype(jnp.bfloat16)
            marks_v[:, c] = jnp.concatenate([marks[:ROWS], marks[ROWS:]], axis=1)
            return carry

        lax.fori_loop(0, KVH, group, 0, unroll=True)
        def finish(i, carry):
            c = cols(i * CHUNK, CHUNK)
            out = h_v[:, c].astype(jnp.float32) + dot_nn(ctx_v[...], wo_v[:, c])
            out_v[:, c] = out.astype(jnp.bfloat16)
            return carry

        if not final:
            lax.fori_loop(0, 8, finish, 0, unroll=True)


def bf16(*shape):
    return jax.ShapeDtypeStruct(shape, jnp.bfloat16)


def inside(*arrays):
    return [pltpu.with_memory_space_constraint(array, pltpu.VMEM) for array in arrays]


def v16(*shape):
    return pltpu.VMEM(shape, jnp.bfloat16)


def v32(*shape):
    return pltpu.VMEM(shape, jnp.float32)


def forward_layer(layer, place, hidden, w_qkv, w_out, normed, proj, ctx, kept, marks):
    final = layer == 7
    return pl.pallas_call(
        functools.partial(forward_kernel, final),
        out_shape=(v16(ROWS, D), v16(ROWS, D), v16(ROWS, WCOLS), v16(ROWS, HQ), v16(ROWS, D), v16(ROWS, HQ)),
        in_specs=[SMEM] + [INSIDE] * 8,
        out_specs=(INSIDE,) * 6,
        input_output_aliases={4: 1, 5: 2, 6: 3, 7: 4, 8: 5},
        scratch_shapes=[v16(KVH, 2 * ROWS, 256), v16(KVH, 2 * ROWS, 256)],
        compiler_params=pltpu.CompilerParams(vmem_limit_bytes=VMEM_LIMIT),
        cost_estimate=pl.CostEstimate(flops=3_000_000_000, bytes_accessed=14_000_000, transcendentals=2_000_000),
        name="forward_last" if final else "forward_layer",
    )(place, *inside(hidden, w_qkv, w_out, normed, proj, ctx, kept, marks))


def backward_kernel(
    last, place, u_v, h_v, proj_v, ctx_v, marks_v, wq_v, wo_v, a0, a1,
    up_v, dproj_v, keep_v, dn_v, key_s, value_s, dkt_s, dvt_s,
):
    del a0, a1

    @pl.when(place[0] == 0)
    def _():
        keep_v[...] = u_v[...]
        fill_keys(proj_v[:, HQ : HQ + KV], key_s, place[1])
        fill_values(proj_v[:, HQ + KV :], value_s, -1.0)

        def group(g, carry):
            c = cols(g * CHUNK, CHUNK)
            d_ctx = dot_nt(u_v[...], wo_v[c, :]).astype(jnp.bfloat16)
            queries = stack_pairs(proj_v[:, c])
            d_pairs = stack_pairs(d_ctx)
            left = jnp.concatenate([queries, stack_pairs(marks_v[:, c])], axis=1)
            weights = jnp.exp2(dot_nt(left, key_s[g]) * TO_EXP2)
            inner = d_pairs.astype(jnp.float32) * stack_pairs(ctx_v[:, c]).astype(jnp.float32)
            d_left = jnp.concatenate([d_pairs, inner.astype(jnp.bfloat16)], axis=1)
            d_scores = (weights * dot_nt(d_left, value_s[g])).astype(jnp.bfloat16)
            d_query = (dot_nn(d_scores, key_s[g][:, :128]) * SCALE).astype(jnp.bfloat16)
            dproj_v[:, c] = jnp.concatenate([d_query[:ROWS], d_query[ROWS:]], axis=1)
            d_key = dot_nn(queries.T, d_scores)
            d_value = dot_nn(d_pairs.T, weights.astype(jnp.bfloat16))
            rows = pl.ds(pl.multiple_of(g * HEAD, HEAD), HEAD)
            dkt_s[rows, :] = (d_key[:HEAD, :ROWS] + d_key[HEAD:, ROWS:]) * SCALE
            dvt_s[rows, :] = d_value[:HEAD, :ROWS] + d_value[HEAD:, ROWS:]
            return carry

        lax.fori_loop(0, KVH, group, 0, unroll=True)
        dproj_v[:, HQ : HQ + KV] = dkt_s[...].T.astype(jnp.bfloat16)
        dproj_v[:, HQ + KV :] = dvt_s[...].T.astype(jnp.bfloat16)
        if not last:
            def widen(i, partial):
                c = cols(i * CHUNK, CHUNK)
                d_normed = dot_nt(dproj_v[...], wq_v[c, :])
                dn_v[:, c] = d_normed
                product = d_normed * h_v[:, c].astype(jnp.float32)
                return partial + product[:, :HALF] + product[:, HALF:]

            partial = lax.fori_loop(0, 8, widen, jnp.zeros((ROWS, HALF), jnp.float32), unroll=True)
            mean = jnp.sum(partial, axis=-1, keepdims=True) * (1.0 / D)
            wide = h_v[...].astype(jnp.float32)
            scale = lax.rsqrt(jnp.mean(wide * wide, axis=-1, keepdims=True) + EPS)
            pull = scale * scale * scale * mean

            def previous(i, carry):
                c = cols(i * CHUNK, CHUNK)
                out = u_v[:, c].astype(jnp.float32) + (scale * dn_v[:, c] - h_v[:, c].astype(jnp.float32) * pull)
                up_v[:, c] = out.astype(jnp.bfloat16)
                return carry

            lax.fori_loop(0, 8, previous, 0, unroll=True)


def backward_layer(layer, place, upstream, kept, proj, ctx, marks, w_qkv, w_out, dproj, ups):
    last = layer == 0
    spare = [place, place] if last else inside(kept, w_qkv)
    where = SMEM if last else INSIDE
    return pl.pallas_call(
        functools.partial(backward_kernel, last),
        out_shape=(v16(ROWS, D), v16(ROWS, WCOLS), v16(ROWS, D)),
        in_specs=[SMEM, INSIDE, where, INSIDE, INSIDE, INSIDE, where, INSIDE, INSIDE, INSIDE],
        out_specs=(INSIDE,) * 3,
        input_output_aliases={8: 1, 9: 2},
        scratch_shapes=[
            v32(ROWS, D), v16(KVH, 2 * ROWS, 256), v16(KVH, 2 * ROWS, 256), v32(KV, ROWS), v32(KV, ROWS)
        ],
        compiler_params=pltpu.CompilerParams(vmem_limit_bytes=VMEM_LIMIT),
        cost_estimate=pl.CostEstimate(flops=4_000_000_000, bytes_accessed=15_000_000, transcendentals=2_000_000),
        name="backward_last" if last else "backward_layer",
    )(place, *inside(upstream), spare[0], *inside(proj, ctx, marks), spare[1], *inside(w_out, dproj, ups))


LAYERS = 8
FINE = (("zlo", 2), ("y", 4), ("x", 4), ("zhi", 4), ("core", 2))
NAMES = tuple(name for name, size in FINE)
SIZES = tuple(size for name, size in FINE)
STAGE = ("y", "core")


def regroup(back):
    pairs = []
    for zlo, y, x, zhi, core in np.ndindex(*SIZES):
        source = np.ravel_multi_index((zlo, y, x, zhi, core), SIZES)
        target = np.ravel_multi_index((core, zlo * 2 + y // 2, x, zhi, y % 2), SIZES)
        pairs.append((int(target), int(source)) if back else (int(source), int(target)))
    return pairs


def z_index(z):
    return (z % 2) * 4 + z // 2


def send_x(value, step):
    return lax.ppermute(value, "x", [(i, (i + step) % 4) for i in range(4)])


def send_z(value, step):
    return lax.ppermute(value, ("zlo", "zhi"), [(z_index(i), z_index((i + step) % 8)) for i in range(8)])


def gather_ring(own, count, send):
    below, above = [own], [own]
    for step in range(count // 2 - 1):
        below.append(send(below[-1], 1))
        above.append(send(above[-1], -1))
    half = own.shape[0] // 2
    far = [send(below[-1][:half], 1), send(above[-1][half:], -1)]
    return above + far + below[:0:-1]


def add(own, came):
    return (own.astype(jnp.float32) + came.astype(jnp.float32)).astype(jnp.bfloat16)


def scatter_direct(take, send, steps):
    total = take(0).astype(jnp.float32)
    for came in [send(take(step), step) for step in steps]:
        total = total + came.astype(jnp.float32)
    return total.astype(jnp.bfloat16)


def gather_direct(own, send):
    far, above, below = send(own, 2), send(own, -1), send(own, 1)
    return [own, above, far, below]


def taker(value, spots, axis, split):
    def take(d, half=None):
        spot = spots[d % len(spots)]
        start, size = [0] * value.ndim, list(value.shape)
        start[axis], size[axis] = spot, 1
        if half is not None:
            size[split] //= 2
            start[split] = half * size[split]
        block = lax.dynamic_slice(value, start, size, allow_negative_indices=False)
        return block.reshape([n for dim, n in enumerate(size) if dim != axis])

    return take


ARRIVAL = (0, 1, 7, 2, 6, 3, 5, 4)


def assemble_kernel(qkv_plan, out_plan, place, *refs):
    count = len(qkv_plan) + len(out_plan)
    parts, (full_qkv, full_out, sems) = refs[:count], refs[-3:]
    x, z = place[0], place[1]
    copies = []
    for ref, (dx, first, pieces) in zip(parts, qkv_plan):
        for i in range(pieces):
            row = (lax.rem(x + dx, 4) * 8 + lax.rem(z + ARRIVAL[first + i], 8)) * 64
            target = full_qkv.at[pl.ds(pl.multiple_of(row, 64), 64), :]
            copies.append(pltpu.make_async_copy(ref.at[pl.ds(i * 64, 64), :], target, sems.at[len(copies)]))
    for ref, (dz, first, pieces) in zip(parts[len(qkv_plan) :], out_plan):
        for i in range(pieces):
            row = (lax.rem(x + first + i, 4) * 8 + lax.rem(z + dz, 8)) * 32
            target = full_out.at[pl.ds(pl.multiple_of(row, 32), 32), :]
            copies.append(pltpu.make_async_copy(ref.at[pl.ds(i * 32, 32), :], target, sems.at[len(copies)]))
    for copy in copies:
        copy.start()
    for copy in copies:
        copy.wait()


def assemble(place, qkv, out, before):
    qkv_plan, out_plan = [plan for plan, part in qkv], [plan for plan, part in out]
    count = len(qkv) + len(out)
    return pl.pallas_call(
        functools.partial(assemble_kernel, qkv_plan, out_plan),
        out_shape=(v16(D, WCOLS), v16(HQ, D)),
        in_specs=[SMEM] + [ANY] * count + [INSIDE] * len(before),
        out_specs=(INSIDE, INSIDE),
        input_output_aliases={count + 1: 0, count + 2: 1} if before else {},
        scratch_shapes=[pltpu.SemaphoreType.DMA((64,))],
        compiler_params=pltpu.CompilerParams(vmem_limit_bytes=4 * 1024 * 1024),
        cost_estimate=pl.CostEstimate(flops=0, bytes_accessed=6_000_000 if before else 18_000_000, transcendentals=0),
        name="assemble_rest" if before else "assemble",
    )(place, *[part for plan, part in qkv], *[part for plan, part in out], *inside(*before))


def gather_weights(near, far, x, z):
    ring = gather_ring(near, 8, send_z)
    column = jnp.concatenate([ring[i] for i in (0, 1, 8, 2, 7, 3, 6, 4, 5)])
    row = jnp.concatenate(gather_direct(far, send_x))
    qkv_parts = gather_ring(column, 4, send_x)
    out_parts = gather_ring(row, 8, send_z)
    qkv = list(zip([(0, 0, 8), (1, 0, 8), (2, 0, 4), (2, 4, 4), (3, 0, 8)], qkv_parts))
    spots = [(0, 0, 4), (1, 0, 4), (2, 0, 4), (3, 0, 4), (4, 0, 2), (4, 2, 2), (5, 0, 4), (6, 0, 4), (7, 0, 4)]
    out = list(zip(spots, out_parts))
    place = jnp.stack([x, z])
    early = assemble(place, [qkv[0], qkv[1], qkv[4]], out[:3] + out[7:], ())
    return assemble(place, qkv[2:4], out[3:7], early)


def sum_of(*terms):
    return sum(term.astype(jnp.float32) for term in terms).astype(jnp.bfloat16)


def scatter_start(part_out, spins):
    take = taker(part_out.reshape(4, 8, 32, D), spins, 1, 0)
    return take, send_z(take(4, 0), 1), send_z(take(4, 1), -1)


def scatter_both(part_qkv, started, turns, spins):
    take_z, up_z, down_z = started
    take_x = taker(part_qkv.reshape(4, 512, WCOLS), turns, 0, 1)
    up_x, down_x = send_x(take_x(2, 0), 1), send_x(take_x(2, 1), -1)
    out_up = jnp.concatenate([add(take_z(3, 0), up_z), take_z(3, 1)])
    out_down = jnp.concatenate([take_z(-3, 0), add(take_z(-3, 1), down_z)])
    up_z, down_z = send_z(out_up, 1), send_z(out_down, -1)
    qkv_up = jnp.concatenate([add(take_x(1, 0), up_x), take_x(1, 1)])
    qkv_down = jnp.concatenate([take_x(-1, 0), add(take_x(-1, 1), down_x)])
    out_up, out_down = add(take_z(2), up_z), add(take_z(-2), down_z)
    qkv_up, qkv_down, out_up, out_down = lax.optimization_barrier((qkv_up, qkv_down, out_up, out_down))
    up_x, down_x = send_x(qkv_up, 1), send_x(qkv_down, -1)
    up_z, down_z = send_z(out_up, 1), send_z(out_down, -1)
    up_z, down_z = send_z(add(take_z(1), up_z), 1), send_z(add(take_z(-1), down_z), -1)
    mine_out = sum_of(take_z(0), up_z, down_z)
    mine_qkv = sum_of(take_x(0), up_x, down_x)
    grad_out = scatter_direct(taker(mine_out, turns, 0, 1), send_x, (2, 1, -1))
    grad_qkv = scatter_direct(
        taker(mine_qkv.reshape(8, 64, WCOLS), spins, 0, 1), send_z, (4, 3, -3, 2, -2, 1, -1)
    )
    return grad_qkv, grad_out


def on_device(inputs, cotangent, joined, w_qkv, w_out):
    micro = lax.axis_index("zlo")
    stage = 2 * lax.axis_index("y") + lax.axis_index("core")
    x_index = lax.axis_index("x")
    z_place = 2 * lax.axis_index("zhi") + micro
    bin_index = 4 * x_index + lax.axis_index("zhi")
    flag = joined[micro, bin_index]
    near = lax.ppermute(w_qkv[0], NAMES, regroup(False))
    far = lax.ppermute(w_out[0], NAMES, regroup(False))
    full_qkv, full_out = gather_weights(near, far, x_index, z_place)
    block = lax.dynamic_index_in_dim(inputs, micro, 0, keepdims=False)
    hidden = jnp.concatenate([block, lax.ppermute(block, "core", [(1, 0)])])
    block = lax.dynamic_index_in_dim(cotangent, micro, 0, keepdims=False)
    upstream = jnp.concatenate([lax.ppermute(block, "core", [(0, 1)]), block])

    places = [jnp.stack([stage - layer, flag]) for layer in range(LAYERS)]
    turns = [((x_index + d) % 4) for d in range(4)]
    spins = [((z_place + d) % 8) for d in range(8)]
    places, turns, spins = lax.optimization_barrier((places, turns, spins))
    normed = jnp.zeros((ROWS, D), jnp.bfloat16)
    kept = jnp.zeros((ROWS, D), jnp.bfloat16)
    proj = jnp.zeros((ROWS, WCOLS), jnp.bfloat16)
    ctx = jnp.zeros((ROWS, HQ), jnp.bfloat16)
    marks = jnp.zeros((ROWS, HQ), jnp.bfloat16)
    for layer in range(LAYERS):
        result, normed, proj, ctx, kept, marks = forward_layer(
            layer, places[layer], hidden, full_qkv, full_out, normed, proj, ctx, kept, marks
        )
        if layer < LAYERS - 1:
            hidden = lax.ppermute(result, STAGE, [(layer, layer + 1)])
    dproj = jnp.zeros((ROWS, WCOLS), jnp.bfloat16)
    ups = jnp.zeros((ROWS, D), jnp.bfloat16)
    contract = (((0,), (0,)), ((), ()))
    for layer in reversed(range(LAYERS)):
        if layer == 0:
            arrived = jnp.where(stage == 0, upstream, ups)
            part_out = lax.dot_general(ctx, arrived, contract, preferred_element_type=jnp.float32).astype(jnp.bfloat16)
            part_out, upstream = lax.optimization_barrier((part_out, upstream))
            started = scatter_start(part_out, spins)
        result, dproj, ups = backward_layer(
            layer, places[layer], upstream, kept, proj, ctx, marks, full_qkv, full_out, dproj, ups
        )
        if layer:
            upstream = lax.ppermute(result, STAGE, [(layer, layer - 1)])
    part_qkv = lax.dot_general(normed, dproj, contract, preferred_element_type=jnp.float32).astype(jnp.bfloat16)
    grad_qkv, grad_out = scatter_both(part_qkv, started, turns, spins)
    grad_out = lax.ppermute(grad_out, NAMES, regroup(True)).astype(jnp.float32)
    grad_qkv = lax.ppermute(grad_qkv, NAMES, regroup(True)).astype(jnp.float32)
    return (grad_qkv[None], grad_out[None])


def solution(mesh):
    fine = jax.sharding.Mesh(mesh.devices.reshape(SIZES), NAMES)
    token = P(None, ("x", "zhi", "core"), None)
    weight = P(("zlo", "y"), ("x", "zhi", "core"), None)
    return jax.shard_map(
        on_device,
        mesh=fine,
        in_specs=(token, token, P(), weight, weight),
        out_specs=(weight, weight),
        check_vma=False,
    )
```
